128 devices in a mesh: gx: 32 (over x, z, core), gy: 4 (over y).
Axes of the slice: x: 4, y: 4, z: 4, core: 2. Of those that a mesh axis runs over, the one named last changes fastest.
Arguments:
- forcing: float32 [8, 4096, 1024], P(None, 'gx', 'gy'), may hold values from -120 to 120
- patches: bfloat16 [4096, 512, 128], P('gx', 'gy'), may hold values from -6 to 6
- owners: int32 [4096, 4], P('gx', 'gy'), may hold values from 0 to 127, as said below
- slots: int32 [4096, 4], P('gx', 'gy'), may hold values from 0 to 1
- cond_x: float32 [8, 4096, 1024], P(None, 'gx', 'gy'), may hold values from 0.2 to 5
- cond_y: float32 [8, 4096, 1024], P(None, 'gx', 'gy'), may hold values from 0.2 to 5
- cond_z: float32 [8, 4096, 1024], P(None, 'gx', 'gy'), may hold values from 0.02 to 0.5
- storage: float32 [8, 4096, 1024], P(None, 'gx', 'gy'), may hold values from 0.1 to 1
- fixed: int32 [8, 4096, 1024], P(None, 'gx', 'gy'), may hold values 0 or 1
- closed: int32 [8, 4096, 1024], P(None, 'gx', 'gy'), may hold values 0 or 1
Outputs:
- solution: float32 [8, 4096, 1024], P(None, 'gx', 'gy')
- residual: float32 [8, 4096, 1024], P(None, 'gx', 'gy')
The draws below stay inside these ranges and needn't reach their ends.
Inputs may be any that keep to these rules, and one draw needn't show every extreme that they name: `owners`: among the 128 patches of one device (entries q of one block of 128 along the first dimension, one column c) no owner appears more than 2 times, and in every device's patches one common owner appears exactly 2 times.
All inputs are finite; a program needn't handle non-finite values. No bound on the sum of `fixed` or of `closed` on one device may be relied on, other than what follows from the above.
Results may differ from the reference program's by a relative error of at most 0.0003.
Values may be sent and summed in bfloat16 or wider, within the bound.
A program may use at most 128 MiB of HBM per device.

```python
import math
import jax
import jax.numpy as jnp
from jax import lax

LAYERS = 8
PATCH = 128
SLOTS = 2
ITERS = 3
TILES_X = 32
TILES_Y = 4
PATCH_DEV = 128
NX = 4096
NY = 1024
PATCH_ROWS = 4096


def draw_forcing(key, part):
    key_base, key_rows, key_cols = jax.random.split(key, 3)
    positions = jnp.arange(NX, dtype=jnp.float32) / NX
    rise_factor = jnp.exp(jnp.log(3.0) * positions)
    row_scale = jnp.exp(jax.random.uniform(key_rows, (NX,), jnp.float32, 0.0, jnp.log(3.3)))
    col_scale = jnp.exp(jax.random.uniform(key_cols, (NY,), jnp.float32, 0.0, jnp.log(10.0)))
    scaling = 0.3 * (rise_factor * row_scale)[:, None] * col_scale[None, :]
    base_draw = jax.random.truncated_normal(key_base, -4.0, 4.0, (LAYERS, NX, NY), jnp.float32)
    return base_draw * scaling[None]


def draw_owners(key, part):
    key_star, key_order, key_shuffle = jax.random.split(key, 3)
    sources = TILES_X * TILES_Y
    devices_all = TILES_X * TILES_Y
    star_owner = jax.random.randint(key_star, (), 0, devices_all, dtype=jnp.int32)
    scores = jax.random.randint(key_order, (sources, devices_all - 1), 0, 2 ** 20, dtype=jnp.int32) * devices_all
    scores = scores + jnp.arange(devices_all - 1, dtype=jnp.int32)[None, :]
    ordering = jnp.argsort(scores, axis=1).astype(jnp.int32)
    others = (star_owner + 1 + ordering[:, :PATCH_DEV - 2]) % devices_all
    doubled = jnp.zeros((sources, 2), jnp.int32) + star_owner
    listing = jnp.concatenate([doubled, others.astype(jnp.int32)], axis=1)
    shuffle_scores = jax.random.randint(key_shuffle, (sources, PATCH_DEV), 0, 2 ** 20, dtype=jnp.int32) * PATCH_DEV
    shuffle_scores = shuffle_scores + jnp.arange(PATCH_DEV, dtype=jnp.int32)[None, :]
    shuffled = jnp.argsort(shuffle_scores, axis=1).astype(jnp.int32)
    listing = jnp.take_along_axis(listing, shuffled, axis=1)
    return listing.reshape(TILES_X, TILES_Y, PATCH_DEV).transpose(0, 2, 1).reshape(TILES_X * PATCH_DEV, TILES_Y)


def place_ends(result, rng, least, top_value):
    extent = result.shape
    index_at = [jax.random.randint(jax.random.fold_in(rng, axis), (), 0, extent[axis]) for axis in range(len(extent))]
    result = result.at[tuple(index_at)].set(least)
    longest = extent.index(max(extent))
    index_at[longest] = (index_at[longest] + 1) % extent[longest]
    return result.at[tuple(index_at)].set(top_value)


def block_levels(rng, dims, cuts, low, largest):
    factor_of = 1.0
    for axis_at, parts in cuts:
        steps = jax.random.uniform(jax.random.fold_in(jax.random.fold_in(rng, 6), axis_at), (parts,), jnp.float32, low / len(cuts), largest / len(cuts))
        factor_of = factor_of * jnp.repeat(jnp.exp(steps), dims[axis_at] // parts).reshape((-1,) + (1,) * (len(dims) - 1 - axis_at))
    return factor_of


def normal_values(own_key, extent, deviation, most, cuts=(), kind=jnp.bfloat16):
    drawn = jax.random.normal(own_key, extent, jnp.float32) * deviation
    if len(cuts) > 0:
        drawn = block_levels(own_key, extent, cuts, -0.22, 0.18) * drawn
    return jnp.clip(drawn, min=-most, max=most).astype(kind)


def setup_inputs(seed: int = 0) -> dict:
    seeds = jax.random.split(jax.random.key(seed), 11)
    return {
        "forcing": draw_forcing(jax.random.fold_in(seeds[10], 71), 0),
        "patches": normal_values(seeds[1], (PATCH_ROWS, TILES_Y * PATCH, PATCH), 1.0, 6.0, ((0, 32), (1, 4))),
        "owners": draw_owners(jax.random.fold_in(seeds[10], 71), 0),
        "slots": place_ends(jax.random.randint(seeds[3], (PATCH_ROWS, TILES_Y), 0, SLOTS), jax.random.fold_in(seeds[3], 1), 0, SLOTS - 1).astype(jnp.int32),
        "cond_x": jnp.clip(jnp.exp(math.log(5.0) - 3.218876 * jax.random.uniform(seeds[4], (LAYERS, NX, NY), jnp.float32) ** block_levels(seeds[4], (LAYERS, NX, NY), ((1, 32), (2, 4)), -0.2, 0.2)), 0.2, 5.0),
        "cond_y": jnp.clip(jnp.exp(math.log(5.0) - 3.218876 * jax.random.uniform(seeds[5], (LAYERS, NX, NY), jnp.float32) ** block_levels(seeds[5], (LAYERS, NX, NY), ((1, 32), (2, 4)), -0.2, 0.2)), 0.2, 5.0),
        "cond_z": jnp.clip(jnp.exp(math.log(0.5) - 3.218876 * jax.random.uniform(seeds[6], (LAYERS, NX, NY), jnp.float32) ** block_levels(seeds[6], (LAYERS, NX, NY), ((1, 32), (2, 4)), -0.2, 0.2)), 0.02, 0.5),
        "storage": jnp.clip(jnp.exp(math.log(1.0) - 2.3025851 * jax.random.uniform(seeds[7], (LAYERS, NX, NY), jnp.float32) ** block_levels(seeds[7], (LAYERS, NX, NY), ((1, 32), (2, 4)), -0.2, 0.2)), 0.1, 1.0),
        "fixed": place_ends((jax.random.randint(seeds[8], (LAYERS, NX, NY), 0, 16) < 1).astype(jnp.int32), jax.random.fold_in(seeds[8], 1), 0, 1),
        "closed": place_ends((jax.random.randint(seeds[9], (LAYERS, NX, NY), 0, 8) < 1).astype(jnp.int32), jax.random.fold_in(seeds[9], 1), 0, 1),
    }


def operate(field, keep_mask, diagonal, cond_east, cond_west, cond_north, cond_south, cond_above, cond_below):
    masked = keep_mask * field
    pad_x = jnp.pad(masked, ((0, 0), (1, 1), (0, 0)))
    pad_y = jnp.pad(masked, ((0, 0), (0, 0), (1, 1)))
    pad_z = jnp.pad(masked, ((1, 1), (0, 0), (0, 0)))
    flux = diagonal * masked - cond_east * pad_x[:, 2:, :] - cond_west * pad_x[:, :-2, :]
    flux = flux - cond_north * pad_y[:, :, 2:] - cond_south * pad_y[:, :, :-2]
    flux = flux - cond_above * pad_z[2:] - cond_below * pad_z[:-2]
    return keep_mask * flux + (1.0 - keep_mask) * field


def reference(forcing, patches, owners, slots, cond_x, cond_y, cond_z, storage, fixed, closed):
    layers, rows_all, cols_all = forcing.shape
    targets = (owners * SLOTS + slots).astype(jnp.int32)
    blocks = patches.reshape(TILES_X, PATCH_DEV, TILES_Y, PATCH, PATCH)
    block_ids = targets.reshape(TILES_X, PATCH_DEV, TILES_Y)

    def add_block(total, item):
        values, ids = item
        flat = values.astype(jnp.float32).reshape(PATCH_DEV * TILES_Y, PATCH * PATCH)
        return total + jax.ops.segment_sum(flat, ids.reshape(-1), num_segments=TILES_X * TILES_Y * SLOTS), None

    start = jnp.zeros((TILES_X * TILES_Y * SLOTS, PATCH * PATCH), jnp.float32)
    totals, unused = lax.scan(add_block, start, (blocks, block_ids))
    surface = totals.reshape(TILES_X, TILES_Y, SLOTS, PATCH, PATCH).transpose(0, 3, 1, 2, 4).reshape(rows_all, cols_all)
    keep_mask = (1 - fixed).astype(jnp.float32)
    top_layer = forcing[0] + surface
    rhs = keep_mask * jnp.concatenate([top_layer[None], forcing[1:]], axis=0)
    open_faces = (1 - closed).astype(jnp.float32)
    row_keep = (jnp.arange(rows_all) < rows_all - 1).astype(jnp.float32)
    col_keep = (jnp.arange(cols_all) < cols_all - 1).astype(jnp.float32)
    layer_keep = (jnp.arange(layers) < layers - 1).astype(jnp.float32)
    cond_east = cond_x * open_faces * row_keep[None, :, None]
    cond_north = cond_y * open_faces * col_keep[None, None, :]
    cond_above = cond_z * layer_keep[:, None, None]
    cond_west = jnp.pad(cond_east, ((0, 0), (1, 0), (0, 0)))[:, :-1, :]
    cond_south = jnp.pad(cond_north, ((0, 0), (0, 0), (1, 0)))[:, :, :-1]
    cond_below = jnp.pad(cond_above, ((1, 0), (0, 0), (0, 0)))[:-1]
    diagonal = storage + cond_east + cond_west + cond_north + cond_south + cond_above + cond_below
    inverse = 1.0 / (keep_mask * diagonal + 1.0 - keep_mask)
    solution = jnp.zeros_like(rhs)
    residual = rhs
    precond = inverse * residual
    direction = precond
    inner = jnp.sum(residual * precond)
    for iteration in range(ITERS):
        image = operate(direction, keep_mask, diagonal, cond_east, cond_west, cond_north, cond_south, cond_above, cond_below)
        step_size = inner / jnp.sum(direction * image)
        solution = solution + step_size * direction
        residual = residual - step_size * image
        precond = inverse * residual
        inner_next = jnp.sum(residual * precond)
        direction = precond + (inner_next / inner) * direction
        inner = inner_next
    return solution, residual
```

```python
import functools

import jax
import jax.numpy as jnp
from jax import lax
from jax.experimental import pallas as pl
from jax.experimental.pallas import tpu as pltpu
from jax.sharding import PartitionSpec as P

CAP = 2
MESH = pl.DeviceIdType.MESH
PAD = 8
MIB = 1 << 20


class Layout:
    def __init__(self, count_x, count_y):
        self.cores = 2 if count_x % 2 == 0 else 1
        chips = count_x // self.cores
        self.nz = 4 if chips % 4 == 0 else chips
        self.nx = chips // self.nz
        self.ny = count_y

    def me(self):
        gx, gy = lax.axis_index("gx"), lax.axis_index("gy")
        core = gx % self.cores
        chip = gx // self.cores
        return chip // self.nz, chip % self.nz, core, gy

    def device(self, x, z, core, y):
        return ((x * self.nz + z) * self.cores + core, y)

    def moved(self, dx=0, dz=0, dc=0, dy=0):
        x, z, core, y = self.me()
        return self.device(
            (x + dx) % self.nx, (z + dz) % self.nz, (core + dc) % self.cores, (y + dy) % self.ny
        )

    def stages(self):
        first = [
            dict(dc=c, dy=y) for c in range(self.cores) for y in range(self.ny) if (c, y) != (0, 0)
        ]
        return [s for s in (first, [dict(dz=d) for d in range(1, self.nz)],
                            [dict(dx=d) for d in range(1, self.nx)]) if s]


def remote(src, dst, send, recv, device):
    return pltpu.make_async_remote_copy(
        src_ref=src, dst_ref=dst, send_sem=send, recv_sem=recv, device_id=device, device_id_type=MESH
    )


def cg_body(
    lay, count_x, count_y, surface, forcing, cond_x, cond_y, cond_z, storage, fixed, closed,
    solution, residual, tees, east, north, south, above, inverse, enns, col_out, col_in,
    partial, gathered, halo_send, halo_recv, sum_send, sum_recv,
):
    layers, rows, cols = forcing.shape
    step = 32
    blocks = rows // step
    gx, gy = lax.axis_index("gx"), lax.axis_index("gy")
    right = ((gx + 1) % count_x, gy)
    left = ((gx + count_x - 1) % count_x, gy)
    up = (gx, (gy + 1) % count_y)
    down = (gx, (gy + count_y - 1) % count_y)
    lanes = lax.broadcasted_iota(jnp.int32, (step, cols), 1)
    first_lane, last_lane = lanes == 0, lanes == cols - 1
    row_ids = lax.broadcasted_iota(jnp.int32, (rows, rows), 0)
    eye = row_ids == lax.broadcasted_iota(jnp.int32, (rows, rows), 1)

    def east_scale(block):
        last = jnp.where(gx == count_x - 1, 0.0, 1.0).astype(jnp.float32)
        ids = lax.broadcasted_iota(jnp.int32, (step, cols), 0) + block * step
        return jnp.where(ids == rows - 1, last, 1.0)

    north_last = jnp.where(gy == count_y - 1, 0.0, 1.0).astype(jnp.float32)
    north_scale = jnp.where(last_lane, north_last, 1.0)

    def column(block):
        wide = jnp.broadcast_to(block, (rows, rows))
        return jnp.sum(jnp.where(eye, wide, 0.0), axis=0, keepdims=True)

    def uncolumn(row, block):
        wide = jnp.broadcast_to(row, (step, rows))
        mask = eye[block * step : (block + 1) * step]
        return jnp.sum(jnp.where(mask, wide, 0.0), axis=1, keepdims=True)

    def faces(layer, carry):
        for b in range(blocks):
            at = pl.ds(b * step, step)
            open_faces = (1 - closed[layer, at, :]).astype(jnp.float32)
            east[layer, pl.ds(PAD + b * step, step), :] = (
                cond_x[layer, at, :] * open_faces * east_scale(b)
            )
            north[layer, at, :] = cond_y[layer, at, :] * open_faces * north_scale
        above[layer + 1] = cond_z[layer] * jnp.where(layer == layers - 1, 0.0, 1.0)
        col_out[0, 0, pl.ds(layer, 1), :] = column(north[layer, :, cols - 1 : cols])
        return carry

    above[0] = jnp.zeros((rows, cols), jnp.float32)
    lax.fori_loop(0, layers, faces, 0)
    rim_x = remote(
        east.at[:, pl.ds(PAD + rows - 1, 1), :], east.at[:, pl.ds(PAD - 1, 1), :],
        halo_send.at[0, 0], halo_recv.at[0, 0], right,
    )
    rim_y = remote(
        col_out.at[0, 0], col_in.at[0, 0], halo_send.at[0, 1], halo_recv.at[0, 1], up
    )
    rim_x.start()
    rim_y.start()
    rim_x.wait()
    rim_y.wait()

    def prepare(layer, total):
        south_row = col_in[0, 0, pl.ds(layer, 1), :]
        for b in range(blocks):
            at = pl.ds(b * step, step)
            north_here = north[layer, at, :]
            south_here = jnp.where(
                first_lane, uncolumn(south_row, b), pltpu.roll(north_here, 1, 1)
            )
            south[layer, at, :] = south_here
            keep = (1 - fixed[layer, at, :]).astype(jnp.float32)
            diagonal = (
                storage[layer, at, :]
                + east[layer, pl.ds(PAD + b * step, step), :]
                + east[layer, pl.ds(PAD - 1 + b * step, step), :]
                + north_here + south_here + above[layer + 1, at, :] + above[layer, at, :]
            )
            inv = keep / diagonal
            inverse[layer, at, :] = inv
            extra = surface[at, :] * jnp.where(layer == 0, 1.0, 0.0)
            start = keep * (forcing[layer, at, :] + extra)
            enns[0, layer, at, :] = start
            tee = inv * start
            tees[0, layer, pl.ds(PAD + b * step, step), :] = tee
            total = total + fold(tee * start)
        return total

    def fold(x):
        parts = [x[i * 8 : (i + 1) * 8] for i in range(step // 8)]
        while len(parts) > 1:
            parts = [a + b for a, b in zip(parts[::2], parts[1::2])]
        return parts[0]

    zero = jnp.zeros((8, cols), jnp.float32)
    moments = [lax.fori_loop(0, layers, prepare, zero)]

    for j in range(3):
        def borders(layer, carry, j=j):
            here = tees.at[j, layer, pl.ds(PAD, rows), :]
            col_out[j + 1, 0, pl.ds(layer, 1), :] = column(here[:, cols - 1 : cols])
            col_out[j + 1, 1, pl.ds(layer, 1), :] = column(here[:, 0:1])
            return carry

        lax.fori_loop(0, layers, borders, 0)
        copies = [
            remote(tees.at[j, :, pl.ds(PAD + rows - 1, 1), :], tees.at[j, :, pl.ds(PAD - 1, 1), :],
                   halo_send.at[j + 1, 0], halo_recv.at[j + 1, 0], right),
            remote(tees.at[j, :, pl.ds(PAD, 1), :], tees.at[j, :, pl.ds(PAD + rows, 1), :],
                   halo_send.at[j + 1, 1], halo_recv.at[j + 1, 1], left),
            remote(col_out.at[j + 1, 0], col_in.at[j + 1, 0],
                   halo_send.at[j + 1, 2], halo_recv.at[j + 1, 2], up),
            remote(col_out.at[j + 1, 1], col_in.at[j + 1, 1],
                   halo_send.at[j + 1, 3], halo_recv.at[j + 1, 3], down),
        ]
        for copy in copies:
            copy.start()
        for copy in copies:
            copy.wait()

        def apply(layer, carry, j=j):
            odd, even = carry
            south_row = col_in[j + 1, 0, pl.ds(layer, 1), :]
            north_row = col_in[j + 1, 1, pl.ds(layer, 1), :]
            higher = jnp.minimum(layer + 1, layers - 1)
            lower = jnp.maximum(layer - 1, 0)
            for b in range(blocks):
                at = pl.ds(b * step, step)
                mid = pl.ds(PAD + b * step, step)
                here = tees[j, layer, mid, :]
                north_val = jnp.where(
                    last_lane, uncolumn(north_row, b), pltpu.roll(here, cols - 1, 1)
                )
                south_val = jnp.where(first_lane, uncolumn(south_row, b), pltpu.roll(here, 1, 1))
                flux = east[layer, mid, :] * tees[j, layer, pl.ds(PAD + 1 + b * step, step), :]
                flux += (east[layer, pl.ds(PAD - 1 + b * step, step), :]
                         * tees[j, layer, pl.ds(PAD - 1 + b * step, step), :])
                flux += north[layer, at, :] * north_val + south[layer, at, :] * south_val
                flux += above[layer + 1, at, :] * tees[j, higher, mid, :]
                flux += above[layer, at, :] * tees[j, lower, mid, :]
                enns[j + 1, layer, at, :] = flux
                odd = odd + fold(here * flux)
                if j < 2:
                    tee = inverse[layer, at, :] * flux
                    tees[j + 1, layer, mid, :] = tee
                    even = even + fold(tee * flux)
            return odd, even

        odd, even = lax.fori_loop(0, layers, apply, (zero, zero))
        moments.append(odd)
        if j < 2:
            moments.append(even)

    partial[0] = jnp.zeros((8, 128), jnp.float32)
    for k, value in enumerate(moments):
        both = sum(value[:, i * 128 : (i + 1) * 128] for i in range(cols // 128))
        partial[0, k : k + 1, :] = jnp.sum(both, axis=0, keepdims=True)
    base = 0
    for s, peers in enumerate(lay.stages()):
        copies = [
            remote(partial.at[s], gathered.at[base + i], sum_send.at[base + i],
                   sum_recv.at[base + i], lay.moved(**offset))
            for i, offset in enumerate(peers)
        ]
        for copy in copies:
            copy.start()
        for copy in copies:
            copy.wait()
        total = partial[s]
        for i in range(len(peers)):
            total = total + gathered[base + i]
        base += len(peers)
        partial[s + 1] = total
    total = partial[len(lay.stages())]
    sol_w, res_w = scalars(total)

    def finish(layer, carry):
        for b in range(blocks):
            at = pl.ds(b * step, step)
            mid = pl.ds(PAD + b * step, step)
            keep = (1 - fixed[layer, at, :]).astype(jnp.float32)
            out = sol_w[0] * tees[0, layer, mid, :]
            for j in range(1, 3):
                out += sol_w[j] * tees[j, layer, mid, :]
            solution[layer, at, :] = out
            out = res_w[0] * enns[0, layer, at, :]
            for j in range(1, 4):
                out += res_w[j] * enns[j, layer, at, :]
            residual[layer, at, :] = keep * out
        return carry

    lax.fori_loop(0, layers, finish, 0)


def scalars(total):
    def reduce(row):
        return jnp.sum(row, axis=1, keepdims=True)

    rows = [total[k : k + 1, :] for k in range(6)]
    m0, m1 = reduce(rows[0]), reduce(rows[1])
    shift = jnp.where(m1 > 0.5 * m0, 1.0, 0.0)
    scale = 1.0 - shift
    c, current = [m0], rows
    for _ in range(5):
        current = [current[q + 1] - shift * current[q] for q in range(len(current) - 1)]
        c.append(reduce(current[0]))
    d = [scale * c[k] - c[k + 1] for k in range(5)]
    zero = jnp.zeros_like(m0)
    rho, pi, sol = [zero + 1.0], [zero + 1.0], [zero, zero, zero]
    inner = m0
    for i in range(3):
        curve = zero
        for a in range(len(pi)):
            for b in range(len(pi)):
                curve = curve + pi[a] * pi[b] * d[a + b]
        alpha = inner / curve
        for a in range(len(pi)):
            sol[a] = sol[a] + alpha * pi[a]
        rho = rho + [zero]
        for a in range(len(pi)):
            rho[a] = rho[a] - alpha * scale * pi[a]
            rho[a + 1] = rho[a + 1] + alpha * pi[a]
        if i < 2:
            inner_next = zero
            for a in range(len(rho)):
                for b in range(len(rho)):
                    inner_next = inner_next + rho[a] * rho[b] * c[a + b]
            beta = inner_next / inner
            pi = [rho[a] + beta * pi[a] if a < len(pi) else rho[a] for a in range(len(rho))]
            inner = inner_next

    def unshift(w):
        out = [zero] * len(w)
        for k in reversed(range(len(w))):
            moved = [zero] + out[:-1]
            out = [moved[i] - shift * out[i] for i in range(len(w))]
            out[0] = out[0] + w[k]
        return out

    return unshift(sol), unshift(rho)


def cg_kernel(lay, count_x, count_y, *refs):
    barrier = pltpu.get_barrier_semaphore()
    gx, gy = lax.axis_index("gx"), lax.axis_index("gy")
    friends = [((gx + 1) % count_x, gy), ((gx + count_x - 1) % count_x, gy),
               (gx, (gy + 1) % count_y), (gx, (gy + count_y - 1) % count_y)]
    for peers in lay.stages():
        friends += [lay.moved(**offset) for offset in peers]
    for friend in friends:
        pl.semaphore_signal(barrier, inc=1, device_id=friend, device_id_type=MESH)
    pl.semaphore_wait(barrier, len(friends))
    cg_body(lay, count_x, count_y, *refs)


def cg(lay, count_x, count_y, *args):
    layers, rows, cols = args[1].shape
    stages = lay.stages()
    peers = sum(len(s) for s in stages)
    full = lambda *lead: pltpu.VMEM((*lead, layers, rows, cols), jnp.float32)
    padded = lambda *lead: pltpu.VMEM((*lead, layers, rows + 2 * PAD, cols), jnp.float32)
    return pl.pallas_call(
        functools.partial(cg_kernel, lay, count_x, count_y),
        out_shape=[jax.ShapeDtypeStruct((layers, rows, cols), jnp.float32)] * 2,
        in_specs=[pl.BlockSpec(memory_space=pltpu.VMEM)] * len(args),
        out_specs=[pl.BlockSpec(memory_space=pltpu.VMEM)] * 2,
        scratch_shapes=[
            padded(3), padded(), full(), full(),
            pltpu.VMEM((layers + 1, rows, cols), jnp.float32), full(), full(4),
            pltpu.VMEM((4, 2, layers, rows), jnp.float32),
            pltpu.VMEM((4, 2, layers, rows), jnp.float32),
            pltpu.VMEM((len(stages) + 1, 8, 128), jnp.float32),
            pltpu.VMEM((peers, 8, 128), jnp.float32),
            pltpu.SemaphoreType.DMA((4, 4)), pltpu.SemaphoreType.DMA((4, 4)),
            pltpu.SemaphoreType.DMA((peers,)), pltpu.SemaphoreType.DMA((peers,)),
        ],
        compiler_params=pltpu.CompilerParams(
            collective_id=1, has_side_effects=True, vmem_limit_bytes=48 * MIB
        ),
    )(*args)


def exchange(patches, owners, slots, tile_cols):
    count_x = lax.axis_size("gx")
    count_y = lax.axis_size("gy")
    devices_all = count_x * count_y
    per_device = patches.shape[0]
    side = patches.shape[1]
    slot_count = tile_cols // side
    owner_list = owners[:, 0]
    slot_list = slots[:, 0]
    targets = jnp.arange(devices_all, dtype=jnp.int32)
    owner_hits = (owner_list[:, None] == targets[None, :]).astype(jnp.float32)
    earlier = (jnp.arange(per_device)[:, None] > jnp.arange(per_device)[None, :]).astype(
        jnp.float32
    )
    before = jnp.dot(earlier, owner_hits, precision=lax.Precision.HIGHEST)
    ranking = jnp.sum(before * owner_hits, axis=1).astype(jnp.int32)
    destination = owner_list * CAP + ranking
    mailbox = jnp.arange(devices_all * CAP, dtype=jnp.int32)
    chosen = mailbox[:, None] == destination[None, :]
    outgoing = jnp.einsum(
        "sp,pab->sab", chosen.astype(jnp.bfloat16), patches, preferred_element_type=jnp.float32
    ).astype(jnp.bfloat16)
    labels = jnp.sum(
        chosen.astype(jnp.float32) * (slot_list + 1).astype(jnp.float32)[None, :], axis=1
    ).astype(jnp.bfloat16)
    arrived, arrived_labels = (
        lax.all_to_all(outgoing, ("gx", "gy"), split_axis=0, concat_axis=0, tiled=True),
        lax.all_to_all(labels, ("gx", "gy"), split_axis=0, concat_axis=0, tiled=True),
    )
    slot_ids = jnp.arange(1, slot_count + 1).astype(jnp.float32)
    placing = (arrived_labels.astype(jnp.float32)[None, :] == slot_ids[:, None]).astype(
        jnp.bfloat16
    )
    placed = jnp.einsum("sm,mab->sab", placing, arrived, preferred_element_type=jnp.float32)
    return placed.transpose(1, 0, 2).reshape(side, slot_count * side)


def on_device(forcing, patches, owners, slots, cond_x, cond_y, cond_z, storage, fixed, closed):
    count_x, count_y = lax.axis_size("gx"), lax.axis_size("gy")
    lay = Layout(count_x, count_y)
    surface = exchange(patches, owners, slots, forcing.shape[2])
    return tuple(
        cg(lay, count_x, count_y, surface, forcing, cond_x, cond_y, cond_z, storage, fixed, closed)
    )


def solution(mesh):
    grid = P(None, "gx", "gy")
    return jax.shard_map(
        on_device,
        mesh=mesh,
        in_specs=(grid, P("gx", "gy", None), P("gx", "gy"), P("gx", "gy")) + (grid,) * 6,
        out_specs=(grid, grid),
        check_vma=False,
    )
```

```python
import functools

import jax
import jax.numpy as jnp
from jax import lax
from jax.experimental import pallas as pl
from jax.experimental.pallas import tpu as pltpu
from jax.sharding import PartitionSpec as P

CAP = 2
MESH = pl.DeviceIdType.MESH
PAD = 8
MIB = 1 << 20


class Layout:
    def __init__(self, count_x, count_y):
        self.cores = 2 if count_x % 2 == 0 else 1
        chips = count_x // self.cores
        self.nz = 4 if chips % 4 == 0 else chips
        self.nx = chips // self.nz
        self.ny = count_y

    def me(self):
        gx, gy = lax.axis_index("gx"), lax.axis_index("gy")
        core = gx % self.cores
        chip = gx // self.cores
        return chip // self.nz, chip % self.nz, core, gy

    def device(self, x, z, core, y):
        return ((x * self.nz + z) * self.cores + core, y)

    def moved(self, dx=0, dz=0, dc=0, dy=0):
        x, z, core, y = self.me()
        return self.device(
            (x + dx) % self.nx, (z + dz) % self.nz, (core + dc) % self.cores, (y + dy) % self.ny
        )

    def stages(self):
        first = [
            dict(dc=c, dy=y) for c in range(self.cores) for y in range(self.ny) if (c, y) != (0, 0)
        ]
        return [s for s in (first, [dict(dz=d) for d in range(1, self.nz)],
                            [dict(dx=d) for d in range(1, self.nx)]) if s]


def remote(src, dst, send, recv, device):
    return pltpu.make_async_remote_copy(
        src_ref=src, dst_ref=dst, send_sem=send, recv_sem=recv, device_id=device, device_id_type=MESH
    )


def cg_body(
    lay, count_x, count_y, surface, forcing, cond_x, cond_y, cond_z, storage, fixed, closed,
    solution, residual, tees, east, north, south, above, inverse, enns, col_out, col_in,
    partial, gathered, halo_send, halo_recv, sum_send, sum_recv,
):
    layers, rows, cols = forcing.shape
    step = 32
    blocks = rows // step
    gx, gy = lax.axis_index("gx"), lax.axis_index("gy")
    right = ((gx + 1) % count_x, gy)
    left = ((gx + count_x - 1) % count_x, gy)
    up = (gx, (gy + 1) % count_y)
    down = (gx, (gy + count_y - 1) % count_y)
    lanes = lax.broadcasted_iota(jnp.int32, (step, cols), 1)
    first_lane, last_lane = lanes == 0, lanes == cols - 1
    row_ids = lax.broadcasted_iota(jnp.int32, (rows, rows), 0)
    eye = row_ids == lax.broadcasted_iota(jnp.int32, (rows, rows), 1)

    def east_scale(block):
        last = jnp.where(gx == count_x - 1, 0.0, 1.0).astype(jnp.float32)
        ids = lax.broadcasted_iota(jnp.int32, (step, cols), 0) + block * step
        return jnp.where(ids == rows - 1, last, 1.0)

    north_last = jnp.where(gy == count_y - 1, 0.0, 1.0).astype(jnp.float32)
    north_scale = jnp.where(last_lane, north_last, 1.0)

    def column(block):
        wide = jnp.broadcast_to(block, (rows, rows))
        return jnp.sum(jnp.where(eye, wide, 0.0), axis=0, keepdims=True)

    def uncolumn(row, block):
        wide = jnp.broadcast_to(row, (step, rows))
        mask = eye[block * step : (block + 1) * step]
        return jnp.sum(jnp.where(mask, wide, 0.0), axis=1, keepdims=True)

    def faces(layer, carry):
        for b in range(blocks):
            at = pl.ds(b * step, step)
            open_faces = (1 - closed[layer, at, :]).astype(jnp.float32)
            east[layer, pl.ds(PAD + b * step, step), :] = (
                cond_x[layer, at, :] * open_faces * east_scale(b)
            )
            north[layer, at, :] = cond_y[layer, at, :] * open_faces * north_scale
        above[layer + 1] = cond_z[layer] * jnp.where(layer == layers - 1, 0.0, 1.0)
        col_out[0, 0, pl.ds(layer, 1), :] = column(north[layer, :, cols - 1 : cols])
        return carry

    above[0] = jnp.zeros((rows, cols), jnp.float32)
    lax.fori_loop(0, layers, faces, 0)
    rim_x = remote(
        east.at[:, pl.ds(PAD + rows - 1, 1), :], east.at[:, pl.ds(PAD - 1, 1), :],
        halo_send.at[0, 0], halo_recv.at[0, 0], right,
    )
    rim_y = remote(
        col_out.at[0, 0], col_in.at[0, 0], halo_send.at[0, 1], halo_recv.at[0, 1], up
    )
    rim_x.start()
    rim_y.start()
    rim_x.wait()
    rim_y.wait()

    def prepare(layer, total):
        south_row = col_in[0, 0, pl.ds(layer, 1), :]
        for b in range(blocks):
            at = pl.ds(b * step, step)
            north_here = north[layer, at, :]
            south_here = jnp.where(
                first_lane, uncolumn(south_row, b), pltpu.roll(north_here, 1, 1)
            )
            south[layer, at, :] = south_here
            keep = (1 - fixed[layer, at, :]).astype(jnp.float32)
            diagonal = (
                storage[layer, at, :]
                + east[layer, pl.ds(PAD + b * step, step), :]
                + east[layer, pl.ds(PAD - 1 + b * step, step), :]
                + north_here + south_here + above[layer + 1, at, :] + above[layer, at, :]
            )
            inv = keep / diagonal
            inverse[layer, at, :] = inv
            extra = surface[at, :] * jnp.where(layer == 0, 1.0, 0.0)
            start = keep * (forcing[layer, at, :] + extra)
            enns[0, layer, at, :] = start
            tee = inv * start
            tees[0, layer, pl.ds(PAD + b * step, step), :] = tee
            total = total + fold(tee * start)
        return total

    def fold(x):
        parts = [x[i * 8 : (i + 1) * 8] for i in range(step // 8)]
        while len(parts) > 1:
            parts = [a + b for a, b in zip(parts[::2], parts[1::2])]
        return parts[0]

    zero = jnp.zeros((8, cols), jnp.float32)
    moments = [lax.fori_loop(0, layers, prepare, zero)]

    for j in range(3):
        def borders(layer, carry, j=j):
            here = tees.at[j, layer, pl.ds(PAD, rows), :]
            col_out[j + 1, 0, pl.ds(layer, 1), :] = column(here[:, cols - 1 : cols])
            col_out[j + 1, 1, pl.ds(layer, 1), :] = column(here[:, 0:1])
            return carry

        lax.fori_loop(0, layers, borders, 0)
        copies = [
            remote(tees.at[j, :, pl.ds(PAD + rows - 1, 1), :], tees.at[j, :, pl.ds(PAD - 1, 1), :],
                   halo_send.at[j + 1, 0], halo_recv.at[j + 1, 0], right),
            remote(tees.at[j, :, pl.ds(PAD, 1), :], tees.at[j, :, pl.ds(PAD + rows, 1), :],
                   halo_send.at[j + 1, 1], halo_recv.at[j + 1, 1], left),
            remote(col_out.at[j + 1, 0], col_in.at[j + 1, 0],
                   halo_send.at[j + 1, 2], halo_recv.at[j + 1, 2], up),
            remote(col_out.at[j + 1, 1], col_in.at[j + 1, 1],
                   halo_send.at[j + 1, 3], halo_recv.at[j + 1, 3], down),
        ]
        for copy in copies:
            copy.start()
        for copy in copies:
            copy.wait()

        def apply(layer, carry, j=j):
            odd, even = carry
            south_row = col_in[j + 1, 0, pl.ds(layer, 1), :]
            north_row = col_in[j + 1, 1, pl.ds(layer, 1), :]
            higher = jnp.minimum(layer + 1, layers - 1)
            lower = jnp.maximum(layer - 1, 0)
            for b in range(blocks):
                at = pl.ds(b * step, step)
                mid = pl.ds(PAD + b * step, step)
                here = tees[j, layer, mid, :]
                north_val = jnp.where(
                    last_lane, uncolumn(north_row, b), pltpu.roll(here, cols - 1, 1)
                )
                south_val = jnp.where(first_lane, uncolumn(south_row, b), pltpu.roll(here, 1, 1))
                flux = east[layer, mid, :] * tees[j, layer, pl.ds(PAD + 1 + b * step, step), :]
                flux += (east[layer, pl.ds(PAD - 1 + b * step, step), :]
                         * tees[j, layer, pl.ds(PAD - 1 + b * step, step), :])
                flux += north[layer, at, :] * north_val + south[layer, at, :] * south_val
                flux += above[layer + 1, at, :] * tees[j, higher, mid, :]
                flux += above[layer, at, :] * tees[j, lower, mid, :]
                enns[j + 1, layer, at, :] = flux
                odd = odd + fold(here * flux)
                if j < 2:
                    tee = inverse[layer, at, :] * flux
                    tees[j + 1, layer, mid, :] = tee
                    even = even + fold(tee * flux)
            return odd, even

        odd, even = lax.fori_loop(0, layers, apply, (zero, zero))
        moments.append(odd)
        if j < 2:
            moments.append(even)

    partial[0] = jnp.zeros((8, 128), jnp.float32)
    for k, value in enumerate(moments):
        both = sum(value[:, i * 128 : (i + 1) * 128] for i in range(cols // 128))
        partial[0, k : k + 1, :] = jnp.sum(both, axis=0, keepdims=True)
    base = 0
    for s, peers in enumerate(lay.stages()):
        copies = [
            remote(partial.at[s], gathered.at[base + i], sum_send.at[base + i],
                   sum_recv.at[base + i], lay.moved(**offset))
            for i, offset in enumerate(peers)
        ]
        for copy in copies:
            copy.start()
        for copy in copies:
            copy.wait()
        total = partial[s]
        for i in range(len(peers)):
            total = total + gathered[base + i]
        base += len(peers)
        partial[s + 1] = total
    total = partial[len(lay.stages())]
    sol_w, res_w = scalars(total)

    def finish(layer, carry):
        for b in range(blocks):
            at = pl.ds(b * step, step)
            mid = pl.ds(PAD + b * step, step)
            keep = (1 - fixed[layer, at, :]).astype(jnp.float32)
            out = sol_w[0] * tees[0, layer, mid, :]
            for j in range(1, 3):
                out += sol_w[j] * tees[j, layer, mid, :]
            solution[layer, at, :] = out
            out = res_w[0] * enns[0, layer, at, :]
            for j in range(1, 4):
                out += res_w[j] * enns[j, layer, at, :]
            residual[layer, at, :] = keep * out
        return carry

    lax.fori_loop(0, layers, finish, 0)


def scalars(total):
    def reduce(row):
        return jnp.sum(row, axis=1, keepdims=True)

    rows = [total[k : k + 1, :] for k in range(6)]
    m0, m1 = reduce(rows[0]), reduce(rows[1])
    shift = jnp.where(m1 > 0.5 * m0, 1.0, 0.0)
    scale = 1.0 - shift
    c, current = [m0], rows
    for _ in range(5):
        current = [current[q + 1] - shift * current[q] for q in range(len(current) - 1)]
        c.append(reduce(current[0]))
    d = [scale * c[k] - c[k + 1] for k in range(5)]
    zero = jnp.zeros_like(m0)
    rho, pi, sol = [zero + 1.0], [zero + 1.0], [zero, zero, zero]
    inner = m0
    for i in range(3):
        curve = zero
        for a in range(len(pi)):
            for b in range(len(pi)):
                curve = curve + pi[a] * pi[b] * d[a + b]
        alpha = inner / curve
        for a in range(len(pi)):
            sol[a] = sol[a] + alpha * pi[a]
        rho = rho + [zero]
        for a in range(len(pi)):
            rho[a] = rho[a] - alpha * scale * pi[a]
            rho[a + 1] = rho[a + 1] + alpha * pi[a]
        if i < 2:
            inner_next = zero
            for a in range(len(rho)):
                for b in range(len(rho)):
                    inner_next = inner_next + rho[a] * rho[b] * c[a + b]
            beta = inner_next / inner
            pi = [rho[a] + beta * pi[a] if a < len(pi) else rho[a] for a in range(len(rho))]
            inner = inner_next

    def unshift(w):
        out = [zero] * len(w)
        for k in reversed(range(len(w))):
            moved = [zero] + out[:-1]
            out = [moved[i] - shift * out[i] for i in range(len(w))]
            out[0] = out[0] + w[k]
        return out

    return unshift(sol), unshift(rho)


def cg_kernel(lay, count_x, count_y, *refs):
    barrier = pltpu.get_barrier_semaphore()
    gx, gy = lax.axis_index("gx"), lax.axis_index("gy")
    friends = [((gx + 1) % count_x, gy), ((gx + count_x - 1) % count_x, gy),
               (gx, (gy + 1) % count_y), (gx, (gy + count_y - 1) % count_y)]
    for peers in lay.stages():
        friends += [lay.moved(**offset) for offset in peers]
    for friend in friends:
        pl.semaphore_signal(barrier, inc=1, device_id=friend, device_id_type=MESH)
    pl.semaphore_wait(barrier, len(friends))
    cg_body(lay, count_x, count_y, *refs)


def cg(lay, count_x, count_y, *args):
    layers, rows, cols = args[1].shape
    stages = lay.stages()
    peers = sum(len(s) for s in stages)
    full = lambda *lead: pltpu.VMEM((*lead, layers, rows, cols), jnp.float32)
    padded = lambda *lead: pltpu.VMEM((*lead, layers, rows + 2 * PAD, cols), jnp.float32)
    return pl.pallas_call(
        functools.partial(cg_kernel, lay, count_x, count_y),
        out_shape=[jax.ShapeDtypeStruct((layers, rows, cols), jnp.float32)] * 2,
        in_specs=[pl.BlockSpec(memory_space=pltpu.VMEM)] * len(args),
        out_specs=[pl.BlockSpec(memory_space=pltpu.VMEM)] * 2,
        scratch_shapes=[
            padded(3), padded(), full(), full(),
            pltpu.VMEM((layers + 1, rows, cols), jnp.float32), full(), full(4),
            pltpu.VMEM((4, 2, layers, rows), jnp.float32),
            pltpu.VMEM((4, 2, layers, rows), jnp.float32),
            pltpu.VMEM((len(stages) + 1, 8, 128), jnp.float32),
            pltpu.VMEM((peers, 8, 128), jnp.float32),
            pltpu.SemaphoreType.DMA((4, 4)), pltpu.SemaphoreType.DMA((4, 4)),
            pltpu.SemaphoreType.DMA((peers,)), pltpu.SemaphoreType.DMA((peers,)),
        ],
        compiler_params=pltpu.CompilerParams(
            collective_id=1, has_side_effects=True, vmem_limit_bytes=48 * MIB
        ),
    )(*args)


ORDERS = (("x", "y", "z"), ("y", "z", "x"), ("z", "x", "y"))
DIMS = {"x": "zy", "y": "xz", "z": "xy"}


def portions(side):
    tiles = side // 16
    cut = [0, -(-tiles // 3), -(-2 * tiles // 3), tiles]
    return [(16 * cut[i], 16 * (cut[i + 1] - cut[i])) for i in range(3)]


def exchange_body(
    lay, cap, owners, slots, patches, surface, held, packed, arrived, summed, landed, second,
    third, index_v, weight_v, weight_in, index_s, weight_s, load_sem, move_sem,
    send1, recv1, send1w, recv1w, send2, recv2, send3, recv3,
):
    per_device, side, _ = patches.shape
    me = dict(zip("xzcy", lay.me()))
    count = dict(x=lay.nx, y=lay.ny, z=lay.nz)
    parts = portions(side)
    load = pltpu.make_async_copy(patches, held, load_sem.at[0])
    load.start()

    shape = (per_device, 128)
    patch_ids = lax.broadcasted_iota(jnp.int32, shape, 0)
    hit = jnp.broadcast_to(owners[...], shape) == lax.broadcasted_iota(jnp.int32, shape, 1)
    slot = jnp.broadcast_to(slots[...], shape)
    first = jnp.min(jnp.where(hit, patch_ids, per_device), axis=0, keepdims=True)
    last = jnp.max(jnp.where(hit, patch_ids, -1), axis=0, keepdims=True)
    index_v[0:1, :] = jnp.minimum(first, per_device - 1)
    index_v[1:2, :] = jnp.maximum(last, 0)
    for j in range(cap):
        chosen = patch_ids == (first if j == 0 else last)
        if j > 0:
            chosen = jnp.logical_and(chosen, last > first)
        chosen = jnp.logical_and(hit, chosen)
        for s in range(2):
            weight_v[2 * j + s : 2 * j + s + 1, :] = jnp.sum(
                jnp.where(jnp.logical_and(chosen, slot == s), 1.0, 0.0), axis=0, keepdims=True
            )
    to_scalar = pltpu.make_async_copy(index_v, index_s, move_sem.at[0])
    to_scalar.start()
    own_weight = pltpu.make_async_copy(weight_v, weight_s.at[0, 0], move_sem.at[1])
    own_weight.start()

    offsets = [(d, c) for d in range(4) for c in range(lay.cores) if (d, c) != (0, 0)]

    def moved(axis, d, c):
        return lay.moved(**{"d" + axis: d, "dc": c})

    weight_copies = []
    for q, order in enumerate(ORDERS):
        weight_copies.append([
            remote(weight_v, weight_in.at[q, i], send1w.at[q, i], recv1w.at[q, i],
                   moved(order[0], d, c))
            for i, (d, c) in enumerate(offsets)
        ])
        for copy in weight_copies[-1]:
            copy.start()

    load.wait()
    to_scalar.wait()
    own_weight.wait()

    def pack(o, carry):
        for j in range(cap):
            packed[o // 32, o // 8 % 4, o // 4 % 2, o % 4, j] = held[index_s[j, o]]
        return carry

    lax.fori_loop(0, 128, pack, 0)

    def outgoing(q, a, c):
        at = pl.ds(*parts[q])
        axis = ORDERS[q][0]
        if axis == "x":
            return packed.at[a, :, c, :, :, at, :]
        if axis == "y":
            return packed.at[:, :, c, a, :, at, :]
        return packed.at[:, a, c, :, :, at, :]

    copies1 = []
    for i, (d, c) in enumerate(offsets):
        for q, order in enumerate(ORDERS):
            axis = order[0]
            copy = remote(
                outgoing(q, (me[axis] + d) % 4, (me["c"] + c) % lay.cores),
                arrived[q].at[i], send1.at[q, i], recv1.at[q, i], moved(axis, d, c),
            )
            copy.start()
            copies1.append((q, copy))

    copies2, copies3 = [], []
    for q, order in enumerate(ORDERS):
        for copy in weight_copies[q]:
            copy.wait()
        gather = pltpu.make_async_copy(weight_in.at[q], weight_s.at[q, pl.ds(1, 7)], move_sem.at[2 + q])
        gather.start()
        gather.wait()
        for p, copy in copies1:
            if p == q:
                copy.wait()
        at = pl.ds(*parts[q])
        rows = parts[q][1]
        dims = DIMS[order[0]]

        def reduce(k, carry, q=q, order=order, at=at, rows=rows, dims=dims):
            spot = {dims[0]: k // 4, dims[1]: k % 4, order[0]: me[order[0]]}
            owner = spot["x"] * 32 + spot["z"] * 8 + me["c"] * 4 + spot["y"]
            sums = [jnp.zeros((rows, side), jnp.float32) for _ in range(2)]
            for source in range(8):
                for j in range(cap):
                    if source == 0:
                        value = packed[spot["x"], spot["z"], me["c"], spot["y"], j, at, :]
                    else:
                        value = arrived[q][source - 1, k // 4, k % 4, j]
                    value = value.astype(jnp.float32)
                    table = (0, 0) if source == 0 else (q, source)
                    for s in range(2):
                        sums[s] = sums[s] + weight_s[(*table, 2 * j + s, owner)] * value
            for s in range(2):
                summed[q][spot[order[1]], spot[order[2]], s] = sums[s]
            return carry

        lax.fori_loop(0, 16, reduce, 0)
        mine = []
        for d in range(1, 4):
            copy = remote(summed[q].at[(me[order[1]] + d) % 4], landed[q].at[d - 1],
                          send2.at[q, d - 1], recv2.at[q, d - 1], moved(order[1], d, 0))
            copy.start()
            mine.append(copy)
        copies2.append(mine)
    for q, order in enumerate(ORDERS):
        for copy in copies2[q]:
            copy.wait()

        def reduce(k, carry, q=q, order=order):
            total = summed[q][me[order[1]], k]
            for d in range(3):
                total = total + landed[q][d, k]
            second[q][k] = total
            return carry

        lax.fori_loop(0, 4, reduce, 0)
        mine = []
        for d in range(1, 4):
            copy = remote(second[q].at[(me[order[2]] + d) % 4], third[q].at[d - 1],
                          send3.at[q, d - 1], recv3.at[q, d - 1], moved(order[2], d, 0))
            copy.start()
            mine.append(copy)
        copies3.append(mine)
    for q, order in enumerate(ORDERS):
        for copy in copies3[q]:
            copy.wait()
        for s in range(2):
            total = second[q][me[order[2]], s]
            for d in range(3):
                total = total + third[q][d, s]
            surface[pl.ds(*parts[q]), s * side : (s + 1) * side] = total


def exchange_scratch(cap, side):
    parts = portions(side)

    def each(*lead, kind=jnp.float32):
        return [pltpu.VMEM((*lead, rows, side), kind) for _, rows in parts]

    bf16 = jnp.bfloat16
    dma = pltpu.SemaphoreType.DMA
    return [
        pltpu.VMEM((128, side, side), bf16),
        pltpu.VMEM((4, 4, 2, 4, cap, side, side), bf16),
        each(7, 4, 4, cap, kind=bf16), each(4, 4, 2), each(3, 4, 2), each(4, 2), each(3, 2),
        pltpu.VMEM((8, 128), jnp.int32), pltpu.VMEM((8, 128), jnp.float32),
        pltpu.VMEM((3, 7, 8, 128), jnp.float32),
        pltpu.SMEM((8, 128), jnp.int32), pltpu.SMEM((3, 8, 8, 128), jnp.float32),
        dma((1,)), dma((5,)),
        dma((3, 7)), dma((3, 7)), dma((3, 7)), dma((3, 7)),
        dma((3, 3)), dma((3, 3)), dma((3, 3)), dma((3, 3)),
    ]


def exchange_friends(lay):
    return [
        lay.moved(**{"d" + axis: d, "dc": c})
        for axis in "xyz" for d in range(4) for c in range(lay.cores) if (d, c) != (0, 0)
    ]


def meet(friends):
    barrier = pltpu.get_barrier_semaphore()
    for friend in friends:
        pl.semaphore_signal(barrier, inc=1, device_id=friend, device_id_type=MESH)
    pl.semaphore_wait(barrier, len(friends))


def exchange_kernel(lay, cap, *refs):
    meet(exchange_friends(lay))
    exchange_body(lay, cap, *refs)


def exchange(lay, cap, patches, owners, slots, tile_cols):
    side = patches.shape[1]
    return pl.pallas_call(
        functools.partial(exchange_kernel, lay, cap),
        out_shape=jax.ShapeDtypeStruct((side, tile_cols), jnp.float32),
        in_specs=[
            pl.BlockSpec(memory_space=pltpu.VMEM), pl.BlockSpec(memory_space=pltpu.VMEM),
            pl.BlockSpec(memory_space=pl.ANY),
        ],
        out_specs=pl.BlockSpec(memory_space=pltpu.VMEM),
        scratch_shapes=exchange_scratch(cap, side),
        compiler_params=pltpu.CompilerParams(
            collective_id=2, has_side_effects=True, vmem_limit_bytes=48 * MIB
        ),
    )(owners, slots, patches)


def on_device(forcing, patches, owners, slots, cond_x, cond_y, cond_z, storage, fixed, closed):
    count_x, count_y = lax.axis_size("gx"), lax.axis_size("gy")
    lay = Layout(count_x, count_y)
    surface = exchange(lay, CAP, patches, owners, slots, forcing.shape[2])
    return tuple(
        cg(lay, count_x, count_y, surface, forcing, cond_x, cond_y, cond_z, storage, fixed, closed)
    )


def solution(mesh):
    grid = P(None, "gx", "gy")
    return jax.shard_map(
        on_device,
        mesh=mesh,
        in_specs=(grid, P("gx", "gy", None), P("gx", "gy"), P("gx", "gy")) + (grid,) * 6,
        out_specs=(grid, grid),
        check_vma=False,
    )
```

```python
import functools

import jax
import jax.numpy as jnp
from jax import lax
from jax.experimental import pallas as pl
from jax.experimental.pallas import tpu as pltpu
from jax.sharding import PartitionSpec as P

MESH = pl.DeviceIdType.MESH
PAD = 8
MIB = 1 << 20


class Layout:
    def __init__(self, count_x, count_y):
        self.cores = 2 if count_x % 2 == 0 else 1
        chips = count_x // self.cores
        self.nz = 4 if chips % 4 == 0 else chips
        self.nx = chips // self.nz
        self.ny = count_y

    def me(self):
        gx, gy = lax.axis_index("gx"), lax.axis_index("gy")
        core = gx % self.cores
        chip = gx // self.cores
        return chip // self.nz, chip % self.nz, core, gy

    def device(self, x, z, core, y):
        return ((x * self.nz + z) * self.cores + core, y)

    def moved(self, dx=0, dz=0, dc=0, dy=0):
        x, z, core, y = self.me()
        return self.device(
            (x + dx) % self.nx, (z + dz) % self.nz, (core + dc) % self.cores, (y + dy) % self.ny
        )

    def stages(self):
        first = [
            dict(dc=c, dy=y) for c in range(self.cores) for y in range(self.ny) if (c, y) != (0, 0)
        ]
        second = [
            dict(dx=x, dz=z) for x in range(self.nx) for z in range(self.nz) if (x, z) != (0, 0)
        ]
        return [first, second]


def remote(src, dst, send, recv, device):
    return pltpu.make_async_remote_copy(
        src_ref=src, dst_ref=dst, send_sem=send, recv_sem=recv, device_id=device, device_id_type=MESH
    )


class Solve:
    names = (
        "forcing", "cond_x", "cond_y", "cond_z", "storage", "fixed", "closed", "tees", "east",
        "north", "south", "above", "inverse", "enns", "col_out", "col_in", "partial", "gathered",
        "halo_send", "halo_recv", "sum_send", "sum_recv",
    )

    def __init__(self, lay, count_x, count_y, refs):
        self.lay, self.count_x, self.count_y = lay, count_x, count_y
        for name, ref in zip(self.names, refs, strict=True):
            setattr(self, name, ref)
        self.layers, self.rows, self.cols = self.forcing.shape
        self.step = 32
        self.blocks = self.rows // self.step
        gx, gy = lax.axis_index("gx"), lax.axis_index("gy")
        self.gx, self.gy = gx, gy
        self.right = ((gx + 1) % count_x, gy)
        self.left = ((gx + count_x - 1) % count_x, gy)
        self.up = (gx, (gy + 1) % count_y)
        self.down = (gx, (gy + count_y - 1) % count_y)
        lanes = lax.broadcasted_iota(jnp.int32, (self.step, self.cols), 1)
        self.first_lane, self.last_lane = lanes == 0, lanes == self.cols - 1
        square = (self.rows, self.rows)
        self.eye = lax.broadcasted_iota(jnp.int32, square, 0) == lax.broadcasted_iota(
            jnp.int32, square, 1
        )
        self.zero = jnp.zeros((8, self.cols), jnp.float32)
        self.moments = [self.zero] * 6

    def load_faces(self):
        for i in (1, 6, 2, 3):
            self.loads[i].wait()

    def load_rest(self):
        for i in (4, 5, 0):
            self.loads[i].wait()

    def column(self, block):
        wide = jnp.broadcast_to(block, (self.rows, self.rows))
        return jnp.sum(jnp.where(self.eye, wide, 0.0), axis=0, keepdims=True)

    def uncolumn(self, row, block):
        wide = jnp.broadcast_to(row, (self.step, self.rows))
        mask = self.eye[block * self.step : (block + 1) * self.step]
        return jnp.sum(jnp.where(mask, wide, 0.0), axis=1, keepdims=True)

    def fold(self, x):
        parts = [x[i * 8 : (i + 1) * 8] for i in range(self.step // 8)]
        while len(parts) > 1:
            parts = [a + b for a, b in zip(parts[::2], parts[1::2])]
        return parts[0]

    def faces(self):
        layers, rows, cols, step = self.layers, self.rows, self.cols, self.step
        east_last = jnp.where(self.gx == self.count_x - 1, 0.0, 1.0).astype(jnp.float32)
        north_last = jnp.where(self.gy == self.count_y - 1, 0.0, 1.0).astype(jnp.float32)
        north_scale = jnp.where(self.last_lane, north_last, 1.0)
        row_ids = lax.broadcasted_iota(jnp.int32, (step, cols), 0)

        def body(layer, carry):
            for b in range(self.blocks):
                at = pl.ds(b * step, step)
                open_faces = (1 - self.closed[layer, at, :]).astype(jnp.float32)
                scale = jnp.where(row_ids == rows - 1 - b * step, east_last, 1.0)
                self.east[layer, pl.ds(PAD + b * step, step), :] = (
                    self.cond_x[layer, at, :] * open_faces * scale
                )
                self.north[layer, at, :] = self.cond_y[layer, at, :] * open_faces * north_scale
            self.above[layer + 1] = self.cond_z[layer] * jnp.where(layer == layers - 1, 0.0, 1.0)
            self.col_out[0, 0, pl.ds(layer, 1), :] = self.column(
                self.north[layer, :, cols - 1 : cols]
            )
            return carry

        self.above[0] = jnp.zeros((rows, cols), jnp.float32)
        lax.fori_loop(0, layers, body, 0)
        self.rims = [
            remote(self.east.at[:, pl.ds(PAD + rows - 1, 1), :],
                   self.east.at[:, pl.ds(PAD - 1, 1), :],
                   self.halo_send.at[0, 0], self.halo_recv.at[0, 0], self.right),
            remote(self.col_out.at[0, 0], self.col_in.at[0, 0],
                   self.halo_send.at[0, 1], self.halo_recv.at[0, 1], self.up),
        ]

    def send_rims(self):
        for copy in self.rims:
            copy.start()

    def prepare(self):
        step = self.step
        for copy in self.rims:
            copy.wait()

        def body(layer, carry):
            south_row = self.col_in[0, 0, pl.ds(layer, 1), :]
            for b in range(self.blocks):
                at = pl.ds(b * step, step)
                north = self.north[layer, at, :]
                south = jnp.where(
                    self.first_lane, self.uncolumn(south_row, b), pltpu.roll(north, 1, 1)
                )
                self.south[layer, at, :] = south
                keep = (1 - self.fixed[layer, at, :]).astype(jnp.float32)
                diagonal = (
                    self.storage[layer, at, :]
                    + self.east[layer, pl.ds(PAD + b * step, step), :]
                    + self.east[layer, pl.ds(PAD - 1 + b * step, step), :]
                    + north + south + self.above[layer + 1, at, :] + self.above[layer, at, :]
                )
                self.inverse[layer, at, :] = keep / diagonal
            return carry

        lax.fori_loop(0, self.layers, body, 0)

    def start(self, low, high, surface=None):
        step = self.step

        def body(layer, total):
            for b in range(self.blocks):
                at = pl.ds(b * step, step)
                keep = (1 - self.fixed[layer, at, :]).astype(jnp.float32)
                value = self.forcing[layer, at, :]
                if surface is not None:
                    value = value + surface[at, :]
                value = keep * value
                self.enns[0, layer, at, :] = value
                tee = self.inverse[layer, at, :] * value
                self.tees[0, layer, pl.ds(PAD + b * step, step), :] = tee
                total = total + self.fold(tee * value)
            return total

        self.moments[0] = lax.fori_loop(low, high, body, self.moments[0])

    def send(self, j, low, high, early):
        rows, cols = self.rows, self.cols

        def body(layer, carry):
            here = self.tees.at[j, layer, pl.ds(PAD, rows), :]
            self.col_out[j + 1, 0, pl.ds(layer, 1), :] = self.column(here[:, cols - 1 : cols])
            self.col_out[j + 1, 1, pl.ds(layer, 1), :] = self.column(here[:, 0:1])
            return carry

        lax.fori_loop(low, high, body, 0)
        some = pl.ds(low, high - low)
        tee = self.tees.at[j, some]
        k = 2 * j + 1 + early
        copies = [
            remote(tee.at[:, pl.ds(PAD + rows - 1, 1), :], tee.at[:, pl.ds(PAD - 1, 1), :],
                   self.halo_send.at[k, 0], self.halo_recv.at[k, 0], self.right),
            remote(tee.at[:, pl.ds(PAD, 1), :], tee.at[:, pl.ds(PAD + rows, 1), :],
                   self.halo_send.at[k, 1], self.halo_recv.at[k, 1], self.left),
            remote(self.col_out.at[j + 1, 0, some], self.col_in.at[j + 1, 0, some],
                   self.halo_send.at[k, 2], self.halo_recv.at[k, 2], self.up),
            remote(self.col_out.at[j + 1, 1, some], self.col_in.at[j + 1, 1, some],
                   self.halo_send.at[k, 3], self.halo_recv.at[k, 3], self.down),
        ]
        for copy in copies:
            copy.start()
        return copies

    def apply(self, j, low, high):
        layers, cols, step, tees = self.layers, self.cols, self.step, self.tees

        def body(layer, carry):
            odd, even = carry
            south_row = self.col_in[j + 1, 0, pl.ds(layer, 1), :]
            north_row = self.col_in[j + 1, 1, pl.ds(layer, 1), :]
            higher = jnp.minimum(layer + 1, layers - 1)
            lower = jnp.maximum(layer - 1, 0)
            for b in range(self.blocks):
                at = pl.ds(b * step, step)
                mid = pl.ds(PAD + b * step, step)
                before = pl.ds(PAD - 1 + b * step, step)
                after = pl.ds(PAD + 1 + b * step, step)
                here = tees[j, layer, mid, :]
                north = jnp.where(
                    self.last_lane, self.uncolumn(north_row, b), pltpu.roll(here, cols - 1, 1)
                )
                south = jnp.where(
                    self.first_lane, self.uncolumn(south_row, b), pltpu.roll(here, 1, 1)
                )
                flux = self.east[layer, mid, :] * tees[j, layer, after, :]
                flux += self.east[layer, before, :] * tees[j, layer, before, :]
                flux += self.north[layer, at, :] * north + self.south[layer, at, :] * south
                flux += self.above[layer + 1, at, :] * tees[j, higher, mid, :]
                flux += self.above[layer, at, :] * tees[j, lower, mid, :]
                self.enns[j + 1, layer, at, :] = flux
                odd = odd + self.fold(here * flux)
                if j < 2:
                    tee = self.inverse[layer, at, :] * flux
                    tees[j + 1, layer, mid, :] = tee
                    even = even + self.fold(tee * flux)
            return odd, even

        last = self.moments[2 * j + 2] if j < 2 else self.zero
        odd, even = lax.fori_loop(low, high, body, (self.moments[2 * j + 1], last))
        self.moments[2 * j + 1] = odd
        if j < 2:
            self.moments[2 * j + 2] = even

    def total(self, extra):
        partial, gathered = self.partial, self.gathered
        partial[0] = jnp.zeros((8, 128), jnp.float32)
        for k, value in enumerate(self.moments):
            both = sum(value[:, i * 128 : (i + 1) * 128] for i in range(self.cols // 128))
            partial[0, k : k + 1, :] = jnp.sum(both, axis=0, keepdims=True)
        partial[0, 6:7, :] = extra
        base = 0
        for s, peers in enumerate(self.lay.stages()):
            copies = [
                remote(partial.at[s], gathered.at[base + i], self.sum_send.at[base + i],
                       self.sum_recv.at[base + i], self.lay.moved(**offset))
                for i, offset in enumerate(peers)
            ]
            for copy in copies:
                copy.start()
            for copy in copies:
                copy.wait()
            total = partial[s]
            for i in range(len(peers)):
                total = total + gathered[base + i]
            base += len(peers)
            partial[s + 1] = total
        return partial[len(self.lay.stages())]

    def finish(self, total, solution, residual):
        sol_w, res_w = scalars(total)
        step = self.step

        def body(layer, carry):
            for b in range(self.blocks):
                at = pl.ds(b * step, step)
                mid = pl.ds(PAD + b * step, step)
                keep = (1 - self.fixed[layer, at, :]).astype(jnp.float32)
                out = sol_w[0] * self.tees[0, layer, mid, :]
                for j in range(1, 3):
                    out += sol_w[j] * self.tees[j, layer, mid, :]
                solution[layer, at, :] = out
                out = res_w[0] * self.enns[0, layer, at, :]
                for j in range(1, 4):
                    out += res_w[j] * self.enns[j, layer, at, :]
                residual[layer, at, :] = keep * out
            return carry

        lax.fori_loop(0, self.layers, body, 0)


def solve_scratch(lay, layers, rows, cols):
    peers = sum(len(s) for s in lay.stages())
    f32, dma = jnp.float32, pltpu.SemaphoreType.DMA

    def full(*lead, kind=f32):
        return pltpu.VMEM((*lead, layers, rows, cols), kind)

    def padded(*lead):
        return pltpu.VMEM((*lead, layers, rows + 2 * PAD, cols), f32)

    return [
        full(), full(), full(), full(), full(), full(kind=jnp.int32), full(kind=jnp.int32),
        padded(3), padded(), full(), full(),
        pltpu.VMEM((layers + 1, rows, cols), f32), full(), full(4),
        pltpu.VMEM((4, 2, layers, rows), f32), pltpu.VMEM((4, 2, layers, rows), f32),
        pltpu.VMEM((len(lay.stages()) + 1, 8, 128), f32), pltpu.VMEM((peers, 8, 128), f32),
        dma((7, 4)), dma((7, 4)), dma((peers,)), dma((peers,)),
    ]


def solve_friends(lay, count_x, count_y):
    gx, gy = lax.axis_index("gx"), lax.axis_index("gy")
    friends = [((gx + 1) % count_x, gy), ((gx + count_x - 1) % count_x, gy),
               (gx, (gy + 1) % count_y), (gx, (gy + count_y - 1) % count_y)]
    for peers in lay.stages():
        friends += [lay.moved(**offset) for offset in peers]
    return friends


def scalars(total):
    def reduce(row):
        return jnp.sum(row, axis=1, keepdims=True)

    rows = [total[k : k + 1, :] for k in range(6)]
    m0, m1 = reduce(rows[0]), reduce(rows[1])
    shift = jnp.where(m1 > 0.5 * m0, 1.0, 0.0)
    scale = 1.0 - shift
    c, current = [m0], rows
    for _ in range(5):
        current = [current[q + 1] - shift * current[q] for q in range(len(current) - 1)]
        c.append(reduce(current[0]))
    d = [scale * c[k] - c[k + 1] for k in range(5)]
    zero = jnp.zeros_like(m0)
    rho, pi, sol = [zero + 1.0], [zero + 1.0], [zero, zero, zero]
    inner = m0
    for i in range(3):
        curve = zero
        for a in range(len(pi)):
            for b in range(len(pi)):
                curve = curve + pi[a] * pi[b] * d[a + b]
        alpha = inner / curve
        for a in range(len(pi)):
            sol[a] = sol[a] + alpha * pi[a]
        rho = rho + [zero]
        for a in range(len(pi)):
            rho[a] = rho[a] - alpha * scale * pi[a]
            rho[a + 1] = rho[a + 1] + alpha * pi[a]
        if i < 2:
            inner_next = zero
            for a in range(len(rho)):
                for b in range(len(rho)):
                    inner_next = inner_next + rho[a] * rho[b] * c[a + b]
            beta = inner_next / inner
            pi = [rho[a] + beta * pi[a] if a < len(pi) else rho[a] for a in range(len(rho))]
            inner = inner_next

    def unshift(w):
        out = [zero] * len(w)
        for k in reversed(range(len(w))):
            moved = [zero] + out[:-1]
            out = [moved[i] - shift * out[i] for i in range(len(w))]
            out[0] = out[0] + w[k]
        return out

    return unshift(sol), unshift(rho)


ORDERS = (("x", "y", "z"), ("y", "z", "x"), ("z", "x", "y"))
DIMS = {"x": "zy", "y": "xz", "z": "xy"}


def portions(side):
    tiles = side // 16
    cut = [0, -(-tiles // 3), -(-2 * tiles // 3), tiles]
    return [(16 * cut[i], 16 * (cut[i + 1] - cut[i])) for i in range(3)]


def exchange_body(
    lay, cap, solve, enter, load, places, surface, held, packed, arrived, summed, landed, second,
    third, index_v, weight_v, weight_in, index_s, weight_s, move_sem,
    send1, recv1, send1w, recv1w, send2, recv2, send3, recv3, *star,
):
    per_device, side, _ = held.shape
    me = dict(zip("xzcy", lay.me()))
    count = dict(x=lay.nx, y=lay.ny, z=lay.nz)
    parts = portions(side)

    shape = (per_device, 128)
    patch_ids = lax.broadcasted_iota(jnp.int32, shape, 0)
    place = jnp.broadcast_to(places[...], shape) - 2 * lax.broadcasted_iota(jnp.int32, shape, 1)
    hit = jnp.logical_or(place == 0, place == 1)
    first = jnp.min(jnp.where(hit, patch_ids, per_device), axis=0, keepdims=True)
    last = jnp.max(jnp.where(hit, patch_ids, -1), axis=0, keepdims=True)
    index_v[0:1, :] = jnp.minimum(first, per_device - 1)
    index_v[1:2, :] = jnp.maximum(last, 0)
    again = last > first
    for j in range(2):
        chosen = patch_ids == (first if j == 0 else last)
        if j > 0:
            chosen = jnp.logical_and(chosen, again)
        chosen = jnp.logical_and(hit, chosen)
        for s in range(2):
            weight_v[2 * j + s : 2 * j + s + 1, :] = jnp.sum(
                jnp.where(jnp.logical_and(chosen, place == s), 1.0, 0.0), axis=0, keepdims=True
            )
    doubled = jnp.where(again, 1.0, 0.0)
    for s in range(2):
        weight_v[4 + s : 5 + s, :] = jnp.broadcast_to(
            jnp.sum(weight_v[2 + s : 3 + s, :], axis=1, keepdims=True), (1, 128)
        )
    extra = jnp.maximum(jnp.sum(doubled, axis=1, keepdims=True) - 1.0, 0.0)
    weight_v[6:7, :] = jnp.broadcast_to(extra, (1, 128))
    weight_v[7:8, :] = doubled
    spare_index = jnp.max(jnp.where(again, last, 0), axis=1, keepdims=True)
    index_v[2:3, :] = jnp.broadcast_to(spare_index, (1, 128))
    to_scalar = pltpu.make_async_copy(index_v, index_s, move_sem.at[0])
    to_scalar.start()
    own_weight = pltpu.make_async_copy(weight_v, weight_s.at[0, 0], move_sem.at[1])
    own_weight.start()

    offsets = [(d, c) for d in range(4) for c in range(lay.cores) if (d, c) != (0, 0)]

    def moved(axis, d, c):
        return lay.moved(**{"d" + axis: d, "dc": c})

    solve.load_faces()
    solve.faces()
    load.wait()
    to_scalar.wait()
    own_weight.wait()

    def pack(o, carry):
        for j in range(cap):
            packed[o // 32, o // 8 % 4, o // 4 % 2, o % 4, j] = held[index_s[j, o]]
        return carry

    lax.fori_loop(0, 128, pack, 0)
    common = Common(lay, me, held, weight_v, weight_in, *star) if cap == 1 else None
    if common:
        common.pack(index_s[2, 0])
    enter()
    solve.send_rims()
    if common:
        common.scatter()
    weight_copies = []
    for q, order in enumerate(ORDERS):
        weight_copies.append([
            remote(weight_v, weight_in.at[q, i], send1w.at[q, i], recv1w.at[q, i],
                   moved(order[0], d, c))
            for i, (d, c) in enumerate(offsets)
        ])
        for copy in weight_copies[-1]:
            copy.start()


    def outgoing(q, a, c):
        at = pl.ds(*parts[q])
        axis = ORDERS[q][0]
        if axis == "x":
            return packed.at[a, :, c, :, :, at, :]
        if axis == "y":
            return packed.at[:, :, c, a, :, at, :]
        return packed.at[:, a, c, :, :, at, :]

    copies1 = []
    for i, (d, c) in enumerate(offsets):
        for q, order in enumerate(ORDERS):
            axis = order[0]
            copy = remote(
                outgoing(q, (me[axis] + d) % 4, (me["c"] + c) % lay.cores),
                arrived[q].at[i], send1.at[q, i], recv1.at[q, i], moved(axis, d, c),
            )
            copy.start()
            copies1.append((q, copy))

    solve.load_rest()
    solve.prepare()
    solve.start(1, solve.layers)
    early = solve.send(0, 1, solve.layers, True)
    for copy in weight_copies[1]:
        copy.wait()
    if common:
        common.reduce()
    copies2, copies3 = [], []
    for q, order in enumerate(ORDERS):
        for copy in weight_copies[q]:
            if q != 1:
                copy.wait()
        gather = pltpu.make_async_copy(weight_in.at[q], weight_s.at[q, pl.ds(1, 7)], move_sem.at[2 + q])
        gather.start()
        gather.wait()
        for p, copy in copies1:
            if p == q:
                copy.wait()
        at = pl.ds(*parts[q])
        rows = parts[q][1]
        dims = DIMS[order[0]]

        def reduce(k, carry, q=q, order=order, at=at, rows=rows, dims=dims):
            spot = {dims[0]: k // 4, dims[1]: k % 4, order[0]: me[order[0]]}
            owner = spot["x"] * 32 + spot["z"] * 8 + me["c"] * 4 + spot["y"]
            sums = [jnp.zeros((rows, side), jnp.float32) for _ in range(2)]
            for source in range(8):
                for j in range(cap):
                    if source == 0:
                        value = packed[spot["x"], spot["z"], me["c"], spot["y"], j, at, :]
                    else:
                        value = arrived[q][source - 1, k // 4, k % 4, j]
                    value = value.astype(jnp.float32)
                    table = (0, 0) if source == 0 else (q, source)
                    for s in range(2):
                        sums[s] = sums[s] + weight_s[(*table, 2 * j + s, owner)] * value
            for s in range(2):
                summed[q][spot[order[1]], spot[order[2]], s] = sums[s]
            return carry

        lax.fori_loop(0, 16, reduce, 0)
        mine = []
        for d in range(1, 4):
            copy = remote(summed[q].at[(me[order[1]] + d) % 4], landed[q].at[d - 1],
                          send2.at[q, d - 1], recv2.at[q, d - 1], moved(order[1], d, 0))
            copy.start()
            mine.append(copy)
        copies2.append(mine)
    for copy in early:
        copy.wait()
    solve.apply(0, 2, solve.layers)
    early = solve.send(1, 2, solve.layers, True)
    if common:
        common.gather()
    for q, order in enumerate(ORDERS):
        for copy in copies2[q]:
            copy.wait()

        def reduce(k, carry, q=q, order=order):
            total = summed[q][me[order[1]], k]
            for d in range(3):
                total = total + landed[q][d, k]
            second[q][k] = total
            return carry

        lax.fori_loop(0, 4, reduce, 0)
        mine = []
        for d in range(1, 4):
            copy = remote(second[q].at[(me[order[2]] + d) % 4], third[q].at[d - 1],
                          send3.at[q, d - 1], recv3.at[q, d - 1], moved(order[2], d, 0))
            copy.start()
            mine.append(copy)
        copies3.append(mine)
    for copy in early:
        copy.wait()
    solve.apply(1, 3, solve.layers)
    early = solve.send(2, 3, solve.layers, True)
    for q, order in enumerate(ORDERS):
        for copy in copies3[q]:
            copy.wait()
        for s in range(2):
            total = second[q][me[order[2]], s]
            for d in range(3):
                total = total + third[q][d, s]
            surface[pl.ds(*parts[q]), s * side : (s + 1) * side] = total
    if common:
        common.add(surface)
    return early


class Common:
    def __init__(self, lay, me, held, weight_v, weight_in, spare, pieces, sums, others, whole,
                 send_a, recv_a, send_b, recv_b, send_c, recv_c):
        self.__dict__.update(locals())
        self.offsets = [(d, c) for d in range(4) for c in range(2) if (d, c) != (0, 0)]
        self.wide = lay.stages()[1]

    def piece(self, d, c):
        return (self.me["y"] + d) % 4 * 2 + (self.me["c"] + c) % 2

    def pack(self, index):
        for k in range(8):
            self.spare[k] = self.held[index, 16 * k : 16 * (k + 1), :]

    def scatter(self):
        self.copies = [
            remote(self.spare.at[self.piece(d, c)], self.pieces.at[i], self.send_a.at[i],
                   self.recv_a.at[i], self.lay.moved(dy=d, dc=c))
            for i, (d, c) in enumerate(self.offsets)
        ]
        for copy in self.copies:
            copy.start()

    def reduce(self):
        for copy in self.copies:
            copy.wait()
        for s in range(2):
            mine = self.spare[self.piece(0, 0)].astype(jnp.float32)
            total = self.weight_v[4 + s : 5 + s, :] * mine
            for i in range(7):
                weight = self.weight_in[1, i, 4 + s : 5 + s, :]
                total = total + weight * self.pieces[i].astype(jnp.float32)
            self.sums[0, s] = total
        self.copies = [
            remote(self.sums.at[0], self.others.at[i], self.send_b.at[i], self.recv_b.at[i],
                   self.lay.moved(**offset))
            for i, offset in enumerate(self.wide)
        ]
        for copy in self.copies:
            copy.start()

    def gather(self):
        for copy in self.copies:
            copy.wait()
        for s in range(2):
            total = self.sums[0, s]
            for i in range(len(self.wide)):
                total = total + self.others[i, s]
            self.sums[1, s] = total
        k = self.piece(0, 0)
        self.whole[k] = self.sums[1]
        self.copies = [
            remote(self.sums.at[1], self.whole.at[k], self.send_c.at[i], self.recv_c.at[i],
                   self.lay.moved(dy=d, dc=c))
            for i, (d, c) in enumerate(self.offsets)
        ]
        for copy in self.copies:
            copy.start()

    def add(self, surface):
        for copy in self.copies:
            copy.wait()
        me = self.me
        owner = me["x"] * 32 + me["z"] * 8 + me["c"] * 4 + me["y"]
        here = lax.broadcasted_iota(jnp.int32, (1, 128), 1) == owner
        mine = jnp.sum(jnp.where(here, self.weight_v[7:8, :], 0.0), axis=1, keepdims=True)
        for k in range(8):
            for s in range(2):
                at = (slice(16 * k, 16 * (k + 1)), slice(128 * s, 128 * (s + 1)))
                surface[at] = surface[at] + mine * self.whole[k, s]


def exchange_scratch(cap, side):
    parts = portions(side)

    def each(*lead, kind=jnp.float32):
        return [pltpu.VMEM((*lead, rows, side), kind) for _, rows in parts]

    bf16 = jnp.bfloat16
    dma = pltpu.SemaphoreType.DMA
    return [
        pltpu.VMEM((128, side, side), bf16),
        pltpu.VMEM((4, 4, 2, 4, cap, side, side), bf16),
        each(7, 4, 4, cap, kind=bf16), each(4, 4, 2), each(3, 4, 2), each(4, 2), each(3, 2),
        pltpu.VMEM((8, 128), jnp.int32), pltpu.VMEM((8, 128), jnp.float32),
        pltpu.VMEM((3, 7, 8, 128), jnp.float32),
        pltpu.SMEM((8, 128), jnp.int32), pltpu.SMEM((3, 8, 8, 128), jnp.float32),
        dma((5,)),
        dma((3, 7)), dma((3, 7)), dma((3, 7)), dma((3, 7)),
        dma((3, 3)), dma((3, 3)), dma((3, 3)), dma((3, 3)),
    ] + ([
        pltpu.VMEM((8, 16, side), bf16), pltpu.VMEM((7, 16, side), bf16),
        pltpu.VMEM((2, 2, 16, side), jnp.float32), pltpu.VMEM((15, 2, 16, side), jnp.float32),
        pltpu.VMEM((8, 2, 16, side), jnp.float32),
        dma((7,)), dma((7,)), dma((15,)), dma((15,)), dma((7,)), dma((7,)),
    ] if cap == 1 else [])


def exchange_friends(lay):
    return [
        lay.moved(**{"d" + axis: d, "dc": c})
        for axis in "xyz" for d in range(4) for c in range(lay.cores) if (d, c) != (0, 0)
    ]


def kernel(lay, count_x, count_y, cap, sizes, *refs):
    places, patches, *inputs = refs[:9]
    solution, residual, sums = refs[9:12]
    solve_refs = refs[12 : 12 + sizes[0]]
    exchange_refs = refs[12 + sizes[0] : 12 + sizes[0] + sizes[1]]
    surface, load_sem = refs[12 + sizes[0] + sizes[1] :]
    solve = Solve(lay, count_x, count_y, solve_refs)
    held = exchange_refs[0]
    load = pltpu.make_async_copy(patches, held, load_sem.at[0])
    load.start()
    loads = [
        pltpu.make_async_copy(source, target, load_sem.at[i + 1])
        for i, (source, target) in enumerate(zip(inputs, solve_refs[:7]))
    ]
    for i in (1, 6, 2, 3, 4, 5, 0):
        loads[i].start()
    solve.loads = loads
    friends = exchange_friends(lay) + solve_friends(lay, count_x, count_y)
    barrier = pltpu.get_barrier_semaphore()
    for friend in friends:
        pl.semaphore_signal(barrier, inc=1, device_id=friend, device_id_type=MESH)
    early = exchange_body(
        lay, cap, solve, lambda: pl.semaphore_wait(barrier, len(friends)), load, places, surface,
        *exchange_refs,
    )
    solve.start(0, 1, surface)
    late = solve.send(0, 0, 1, False)
    for copy in early:
        copy.wait()
    solve.apply(2, 4, solve.layers)
    for j in range(3):
        for copy in late:
            copy.wait()
        solve.apply(j, 0, j + 2)
        if j < 2:
            late = solve.send(j + 1, 0, j + 2, False)
    weight_v = exchange_refs[8]
    total = solve.total(weight_v[6:7, :])
    sums[...] = total
    solve.finish(total, solution, residual)


def run(lay, count_x, count_y, cap, places, patches, *grids):
    layers, rows, cols = grids[0].shape
    solve = solve_scratch(lay, layers, rows, cols)
    moving = exchange_scratch(cap, patches.shape[1])
    return pl.pallas_call(
        functools.partial(kernel, lay, count_x, count_y, cap, (len(solve), len(moving))),
        out_shape=[jax.ShapeDtypeStruct((layers, rows, cols), jnp.float32)] * 2
        + [jax.ShapeDtypeStruct((8, 128), jnp.float32)],
        in_specs=[pl.BlockSpec(memory_space=pltpu.VMEM)]
        + [pl.BlockSpec(memory_space=pl.ANY)] * (1 + len(grids)),
        out_specs=[pl.BlockSpec(memory_space=pltpu.VMEM)] * 3,
        scratch_shapes=solve + moving + [
            pltpu.VMEM((rows, cols), jnp.float32), pltpu.SemaphoreType.DMA((8,))
        ],
        compiler_params=pltpu.CompilerParams(
            collective_id=cap, has_side_effects=True,
            vmem_limit_bytes=(42 if cap == 1 else 60) * MIB,
        ),
    )(places, patches, *grids)


def on_device(forcing, patches, owners, slots, cond_x, cond_y, cond_z, storage, fixed, closed):
    count_x, count_y = lax.axis_size("gx"), lax.axis_size("gy")
    lay = Layout(count_x, count_y)
    places = owners * 2 + slots
    args = (places, patches, forcing, cond_x, cond_y, cond_z, storage, fixed, closed)
    *quick, sums = run(lay, count_x, count_y, 1, *args)

    def general(args, quick):
        return tuple(run(lay, count_x, count_y, 2, *args)[:2])

    return lax.cond(sums[6, 0] > 0.0, general, lambda args, quick: quick, args, tuple(quick))


def solution(mesh):
    grid = P(None, "gx", "gy")
    return jax.shard_map(
        on_device,
        mesh=mesh,
        in_specs=(grid, P("gx", "gy", None), P("gx", "gy"), P("gx", "gy")) + (grid,) * 6,
        out_specs=(grid, grid),
        check_vma=False,
    )
```

```python
import functools

import jax
import jax.numpy as jnp
from jax import lax
from jax.experimental import pallas as pl
from jax.experimental.pallas import tpu as pltpu
from jax.sharding import PartitionSpec as P

MESH = pl.DeviceIdType.MESH
PAD = 8
MIB = 1 << 20


class Layout:
    def __init__(self, count_x, count_y):
        self.cores = 2 if count_x % 2 == 0 else 1
        chips = count_x // self.cores
        self.nz = 4 if chips % 4 == 0 else chips
        self.nx = chips // self.nz
        self.ny = count_y

    def me(self):
        gx, gy = lax.axis_index("gx"), lax.axis_index("gy")
        core = gx % self.cores
        chip = gx // self.cores
        return chip // self.nz, chip % self.nz, core, gy

    def device(self, x, z, core, y):
        return ((x * self.nz + z) * self.cores + core, y)

    def moved(self, dx=0, dz=0, dc=0, dy=0):
        x, z, core, y = self.me()
        return self.device(
            (x + dx) % self.nx, (z + dz) % self.nz, (core + dc) % self.cores, (y + dy) % self.ny
        )

    def stages(self):
        first = [
            dict(dc=c, dy=y) for c in range(self.cores) for y in range(self.ny) if (c, y) != (0, 0)
        ]
        second = [
            dict(dx=x, dz=z) for x in range(self.nx) for z in range(self.nz) if (x, z) != (0, 0)
        ]
        return [first, second]


def remote(src, dst, send, recv, device):
    return pltpu.make_async_remote_copy(
        src_ref=src, dst_ref=dst, send_sem=send, recv_sem=recv, device_id=device, device_id_type=MESH
    )


class Solve:
    names = (
        "forcing", "cond_x", "cond_y", "cond_z", "storage", "fixed", "closed", "tees", "east",
        "north", "south", "above", "inverse", "enns", "col_out", "col_in", "partial", "gathered",
        "halo_send", "halo_recv", "sum_send", "sum_recv",
    )

    def __init__(self, lay, count_x, count_y, refs):
        self.lay, self.count_x, self.count_y = lay, count_x, count_y
        for name, ref in zip(self.names, refs, strict=True):
            setattr(self, name, ref)
        self.layers, self.rows, self.cols = self.forcing.shape
        self.step = 32
        self.blocks = self.rows // self.step
        gx, gy = lax.axis_index("gx"), lax.axis_index("gy")
        self.gx, self.gy = gx, gy
        self.right = ((gx + 1) % count_x, gy)
        self.left = ((gx + count_x - 1) % count_x, gy)
        self.up = (gx, (gy + 1) % count_y)
        self.down = (gx, (gy + count_y - 1) % count_y)
        lanes = lax.broadcasted_iota(jnp.int32, (self.step, self.cols), 1)
        self.first_lane, self.last_lane = lanes == 0, lanes == self.cols - 1
        square = (self.rows, self.rows)
        self.eye = lax.broadcasted_iota(jnp.int32, square, 0) == lax.broadcasted_iota(
            jnp.int32, square, 1
        )
        self.zero = jnp.zeros((8, self.cols), jnp.float32)
        self.moments = [self.zero] * 6

    def start_loads(self):
        for i in (1, 6, 2, 3, 4, 5, 0):
            self.loads[i].start()

    def load_faces(self):
        for i in (1, 6, 2, 3):
            self.loads[i].wait()

    def load_rest(self):
        for i in (4, 5, 0):
            self.loads[i].wait()

    def column(self, block):
        wide = jnp.broadcast_to(block, (self.rows, self.rows))
        return jnp.sum(jnp.where(self.eye, wide, 0.0), axis=0, keepdims=True)

    def uncolumn(self, row, block):
        wide = jnp.broadcast_to(row, (self.step, self.rows))
        mask = self.eye[block * self.step : (block + 1) * self.step]
        return jnp.sum(jnp.where(mask, wide, 0.0), axis=1, keepdims=True)

    def fold(self, x):
        parts = [x[i * 8 : (i + 1) * 8] for i in range(self.step // 8)]
        while len(parts) > 1:
            parts = [a + b for a, b in zip(parts[::2], parts[1::2])]
        return parts[0]

    def faces(self):
        layers, rows, cols, step = self.layers, self.rows, self.cols, self.step
        east_last = jnp.where(self.gx == self.count_x - 1, 0.0, 1.0).astype(jnp.float32)
        north_last = jnp.where(self.gy == self.count_y - 1, 0.0, 1.0).astype(jnp.float32)
        north_scale = jnp.where(self.last_lane, north_last, 1.0)
        row_ids = lax.broadcasted_iota(jnp.int32, (step, cols), 0)

        def body(layer, carry):
            for b in range(self.blocks):
                at = pl.ds(b * step, step)
                open_faces = (1 - self.closed[layer, at, :]).astype(jnp.float32)
                scale = jnp.where(row_ids == rows - 1 - b * step, east_last, 1.0)
                self.east[layer, pl.ds(PAD + b * step, step), :] = (
                    self.cond_x[layer, at, :] * open_faces * scale
                )
                self.north[layer, at, :] = self.cond_y[layer, at, :] * open_faces * north_scale
            self.above[layer + 1] = self.cond_z[layer] * jnp.where(layer == layers - 1, 0.0, 1.0)
            self.col_out[0, 0, pl.ds(layer, 1), :] = self.column(
                self.north[layer, :, cols - 1 : cols]
            )
            return carry

        self.above[0] = jnp.zeros((rows, cols), jnp.float32)
        lax.fori_loop(0, layers, body, 0)
        self.rims = [
            remote(self.east.at[:, pl.ds(PAD + rows - 1, 1), :],
                   self.east.at[:, pl.ds(PAD - 1, 1), :],
                   self.halo_send.at[0, 0], self.halo_recv.at[0, 0], self.right),
            remote(self.col_out.at[0, 0], self.col_in.at[0, 0],
                   self.halo_send.at[0, 1], self.halo_recv.at[0, 1], self.up),
        ]

    def send_rims(self):
        for copy in self.rims:
            copy.start()

    def prepare(self):
        step = self.step
        for copy in self.rims:
            copy.wait()

        def body(layer, carry):
            south_row = self.col_in[0, 0, pl.ds(layer, 1), :]
            for b in range(self.blocks):
                at = pl.ds(b * step, step)
                north = self.north[layer, at, :]
                south = jnp.where(
                    self.first_lane, self.uncolumn(south_row, b), pltpu.roll(north, 1, 1)
                )
                self.south[layer, at, :] = south
                keep = (1 - self.fixed[layer, at, :]).astype(jnp.float32)
                diagonal = (
                    self.storage[layer, at, :]
                    + self.east[layer, pl.ds(PAD + b * step, step), :]
                    + self.east[layer, pl.ds(PAD - 1 + b * step, step), :]
                    + north + south + self.above[layer + 1, at, :] + self.above[layer, at, :]
                )
                self.inverse[layer, at, :] = keep / diagonal
            return carry

        lax.fori_loop(0, self.layers, body, 0)

    def start(self, low, high, surface=None):
        step = self.step

        def body(layer, total):
            for b in range(self.blocks):
                at = pl.ds(b * step, step)
                keep = (1 - self.fixed[layer, at, :]).astype(jnp.float32)
                value = self.forcing[layer, at, :]
                if surface is not None:
                    value = value + surface[at, :]
                value = keep * value
                self.enns[0, layer, at, :] = value
                tee = self.inverse[layer, at, :] * value
                self.tees[0, layer, pl.ds(PAD + b * step, step), :] = tee
                total = total + self.fold(tee * value)
            return total

        self.moments[0] = lax.fori_loop(low, high, body, self.moments[0])

    def send(self, j, low, high, early):
        rows, cols = self.rows, self.cols

        def body(layer, carry):
            here = self.tees.at[j, layer, pl.ds(PAD, rows), :]
            self.col_out[j + 1, 0, pl.ds(layer, 1), :] = self.column(here[:, cols - 1 : cols])
            self.col_out[j + 1, 1, pl.ds(layer, 1), :] = self.column(here[:, 0:1])
            return carry

        lax.fori_loop(low, high, body, 0)
        some = pl.ds(low, high - low)
        tee = self.tees.at[j, some]
        k = 2 * j + 1 + early
        copies = [
            remote(tee.at[:, pl.ds(PAD + rows - 1, 1), :], tee.at[:, pl.ds(PAD - 1, 1), :],
                   self.halo_send.at[k, 0], self.halo_recv.at[k, 0], self.right),
            remote(tee.at[:, pl.ds(PAD, 1), :], tee.at[:, pl.ds(PAD + rows, 1), :],
                   self.halo_send.at[k, 1], self.halo_recv.at[k, 1], self.left),
            remote(self.col_out.at[j + 1, 0, some], self.col_in.at[j + 1, 0, some],
                   self.halo_send.at[k, 2], self.halo_recv.at[k, 2], self.up),
            remote(self.col_out.at[j + 1, 1, some], self.col_in.at[j + 1, 1, some],
                   self.halo_send.at[k, 3], self.halo_recv.at[k, 3], self.down),
        ]
        for copy in copies:
            copy.start()
        return copies

    def apply(self, j, low, high):
        layers, cols, step, tees = self.layers, self.cols, self.step, self.tees

        def body(layer, carry):
            odd, even = carry
            south_row = self.col_in[j + 1, 0, pl.ds(layer, 1), :]
            north_row = self.col_in[j + 1, 1, pl.ds(layer, 1), :]
            higher = jnp.minimum(layer + 1, layers - 1)
            lower = jnp.maximum(layer - 1, 0)
            for b in range(self.blocks):
                at = pl.ds(b * step, step)
                mid = pl.ds(PAD + b * step, step)
                before = pl.ds(PAD - 1 + b * step, step)
                after = pl.ds(PAD + 1 + b * step, step)
                here = tees[j, layer, mid, :]
                north = jnp.where(
                    self.last_lane, self.uncolumn(north_row, b), pltpu.roll(here, cols - 1, 1)
                )
                south = jnp.where(
                    self.first_lane, self.uncolumn(south_row, b), pltpu.roll(here, 1, 1)
                )
                flux = self.east[layer, mid, :] * tees[j, layer, after, :]
                flux += self.east[layer, before, :] * tees[j, layer, before, :]
                flux += self.north[layer, at, :] * north + self.south[layer, at, :] * south
                flux += self.above[layer + 1, at, :] * tees[j, higher, mid, :]
                flux += self.above[layer, at, :] * tees[j, lower, mid, :]
                self.enns[j + 1, layer, at, :] = flux
                odd = odd + self.fold(here * flux)
                if j < 2:
                    tee = self.inverse[layer, at, :] * flux
                    tees[j + 1, layer, mid, :] = tee
                    even = even + self.fold(tee * flux)
            return odd, even

        last = self.moments[2 * j + 2] if j < 2 else self.zero
        odd, even = lax.fori_loop(low, high, body, (self.moments[2 * j + 1], last))
        self.moments[2 * j + 1] = odd
        if j < 2:
            self.moments[2 * j + 2] = even

    def total(self, extra):
        partial, gathered = self.partial, self.gathered
        partial[0] = jnp.zeros((8, 128), jnp.float32)
        for k, value in enumerate(self.moments):
            both = sum(value[:, i * 128 : (i + 1) * 128] for i in range(self.cols // 128))
            partial[0, k : k + 1, :] = jnp.sum(both, axis=0, keepdims=True)
        partial[0, 6:7, :] = extra
        base = 0
        for s, peers in enumerate(self.lay.stages()):
            copies = [
                remote(partial.at[s], gathered.at[base + i], self.sum_send.at[base + i],
                       self.sum_recv.at[base + i], self.lay.moved(**offset))
                for i, offset in enumerate(peers)
            ]
            for copy in copies:
                copy.start()
            for copy in copies:
                copy.wait()
            total = partial[s]
            for i in range(len(peers)):
                total = total + gathered[base + i]
            base += len(peers)
            partial[s + 1] = total
        return partial[len(self.lay.stages())]

    def finish(self, total, solution, residual):
        sol_w, res_w = scalars(total)
        step = self.step

        def body(layer, carry):
            for b in range(self.blocks):
                at = pl.ds(b * step, step)
                mid = pl.ds(PAD + b * step, step)
                keep = (1 - self.fixed[layer, at, :]).astype(jnp.float32)
                out = sol_w[0] * self.tees[0, layer, mid, :]
                for j in range(1, 3):
                    out += sol_w[j] * self.tees[j, layer, mid, :]
                solution[layer, at, :] = out
                out = res_w[0] * self.enns[0, layer, at, :]
                for j in range(1, 4):
                    out += res_w[j] * self.enns[j, layer, at, :]
                residual[layer, at, :] = keep * out
            return carry

        lax.fori_loop(0, self.layers, body, 0)


def solve_scratch(lay, layers, rows, cols):
    peers = sum(len(s) for s in lay.stages())
    f32, dma = jnp.float32, pltpu.SemaphoreType.DMA

    def full(*lead, kind=f32):
        return pltpu.VMEM((*lead, layers, rows, cols), kind)

    def padded(*lead):
        return pltpu.VMEM((*lead, layers, rows + 2 * PAD, cols), f32)

    return [
        full(), full(), full(), full(), full(), full(kind=jnp.int32), full(kind=jnp.int32),
        padded(3), padded(), full(), full(),
        pltpu.VMEM((layers + 1, rows, cols), f32), full(), full(4),
        pltpu.VMEM((4, 2, layers, rows), f32), pltpu.VMEM((4, 2, layers, rows), f32),
        pltpu.VMEM((len(lay.stages()) + 1, 8, 128), f32), pltpu.VMEM((peers, 8, 128), f32),
        dma((7, 4)), dma((7, 4)), dma((peers,)), dma((peers,)),
    ]


def every_friend(lay, count_x):
    gx, gy = lax.axis_index("gx"), lax.axis_index("gy")
    friends = [((gx + 1) % count_x, gy), ((gx + count_x - 1) % count_x, gy), lay.moved(dc=1)]
    for axis in "xyz":
        friends += [
            lay.moved(**{"d" + axis: d, "dc": c}) for d in range(1, 4) for c in range(lay.cores)
        ]
    return friends + [lay.moved(dx=x, dz=z) for x in range(1, 4) for z in range(1, 4)]


def scalars(total):
    def reduce(row):
        return jnp.sum(row, axis=1, keepdims=True)

    rows = [total[k : k + 1, :] for k in range(6)]
    m0, m1 = reduce(rows[0]), reduce(rows[1])
    shift = jnp.where(m1 > 0.5 * m0, 1.0, 0.0)
    scale = 1.0 - shift
    c, current = [m0], rows
    for _ in range(5):
        current = [current[q + 1] - shift * current[q] for q in range(len(current) - 1)]
        c.append(reduce(current[0]))
    d = [scale * c[k] - c[k + 1] for k in range(5)]
    zero = jnp.zeros_like(m0)
    rho, pi, sol = [zero + 1.0], [zero + 1.0], [zero, zero, zero]
    inner = m0
    for i in range(3):
        curve = zero
        for a in range(len(pi)):
            for b in range(len(pi)):
                curve = curve + pi[a] * pi[b] * d[a + b]
        alpha = inner / curve
        for a in range(len(pi)):
            sol[a] = sol[a] + alpha * pi[a]
        rho = rho + [zero]
        for a in range(len(pi)):
            rho[a] = rho[a] - alpha * scale * pi[a]
            rho[a + 1] = rho[a + 1] + alpha * pi[a]
        if i < 2:
            inner_next = zero
            for a in range(len(rho)):
                for b in range(len(rho)):
                    inner_next = inner_next + rho[a] * rho[b] * c[a + b]
            beta = inner_next / inner
            pi = [rho[a] + beta * pi[a] if a < len(pi) else rho[a] for a in range(len(rho))]
            inner = inner_next

    def unshift(w):
        out = [zero] * len(w)
        for k in reversed(range(len(w))):
            moved = [zero] + out[:-1]
            out = [moved[i] - shift * out[i] for i in range(len(w))]
            out[0] = out[0] + w[k]
        return out

    return unshift(sol), unshift(rho)


ORDERS = (("x", "y", "z"), ("y", "z", "x"), ("z", "x", "y"))
DIMS = {"x": "zy", "y": "xz", "z": "xy"}


def portions(side):
    tiles = side // 16
    cut = [0, -(-tiles // 3), -(-2 * tiles // 3), tiles]
    return [(16 * cut[i], 16 * (cut[i + 1] - cut[i])) for i in range(3)]


def exchange_body(
    lay, cap, solve, enter, load, owners, slots, surface, held, packed, arrived, summed, landed, second,
    third, index_v, weight_v, weight_in, index_s, weight_s, move_sem,
    send1, recv1, send1w, recv1w, send2, recv2, send3, recv3, *star,
):
    per_device, side, _ = held.shape
    me = dict(zip("xzcy", lay.me()))
    count = dict(x=lay.nx, y=lay.ny, z=lay.nz)
    parts = portions(side)

    shape = (per_device, 128)
    patch_ids = lax.broadcasted_iota(jnp.int32, shape, 0)
    row = (owners[...] * 2 + slots[...]).astype(jnp.float32)
    column = jnp.sum(
        jnp.where(solve.eye, jnp.broadcast_to(row, shape), 0.0), axis=1, keepdims=True
    )
    place = jnp.broadcast_to(column, shape) - (
        2 * lax.broadcasted_iota(jnp.int32, shape, 1)
    ).astype(jnp.float32)
    hit = jnp.logical_or(place == 0.0, place == 1.0)
    first = jnp.min(jnp.where(hit, patch_ids, per_device), axis=0, keepdims=True)
    last = jnp.max(jnp.where(hit, patch_ids, -1), axis=0, keepdims=True)
    index_v[0:1, :] = jnp.minimum(first, per_device - 1)
    index_v[1:2, :] = jnp.maximum(last, 0)
    again = last > first
    for j in range(2):
        chosen = patch_ids == (first if j == 0 else last)
        if j > 0:
            chosen = jnp.logical_and(chosen, again)
        chosen = jnp.logical_and(hit, chosen)
        for s in range(2):
            weight_v[2 * j + s : 2 * j + s + 1, :] = jnp.sum(
                jnp.where(jnp.logical_and(chosen, place == float(s)), 1.0, 0.0), axis=0, keepdims=True
            )
    doubled = jnp.where(again, 1.0, 0.0)
    for s in range(2):
        weight_v[4 + s : 5 + s, :] = jnp.broadcast_to(
            jnp.sum(weight_v[2 + s : 3 + s, :], axis=1, keepdims=True), (1, 128)
        )
    extra = jnp.maximum(jnp.sum(doubled, axis=1, keepdims=True) - 1.0, 0.0)
    weight_v[6:7, :] = jnp.broadcast_to(extra, (1, 128))
    weight_v[7:8, :] = doubled
    spare_index = jnp.max(jnp.where(again, last, 0), axis=1, keepdims=True)
    index_v[2:3, :] = jnp.broadcast_to(spare_index, (1, 128))
    to_scalar = pltpu.make_async_copy(index_v, index_s, move_sem.at[0])
    to_scalar.start()
    own_weight = pltpu.make_async_copy(weight_v, weight_s.at[0, 0], move_sem.at[1])
    own_weight.start()

    offsets = [(d, c) for d in range(4) for c in range(lay.cores) if (d, c) != (0, 0)]

    def moved(axis, d, c):
        return lay.moved(**{"d" + axis: d, "dc": c})

    weight_copies = [
        [
            remote(weight_v, weight_in.at[q, i], send1w.at[q, i], recv1w.at[q, i],
                   moved(order[0], d, c))
            for i, (d, c) in enumerate(offsets)
        ]
        for q, order in enumerate(ORDERS)
    ]
    for copy in load:
        copy.wait()
    solve.start_loads()
    to_scalar.wait()
    own_weight.wait()

    def pack(o, carry):
        for j in range(cap):
            packed[o // 32, o // 8 % 4, o // 4 % 2, o % 4, j] = held[index_s[j, o]]
        return carry

    lax.fori_loop(0, 128, pack, 0)
    common = Common(lay, me, held, weight_v, weight_in, *star) if cap == 1 else None
    if common:
        common.pack(index_s[2, 0])
    enter()
    for group in weight_copies:
        for copy in group:
            copy.start()
    if common:
        common.scatter()

    def first_stage(half):
        some = pl.ds(2 * half, 2)
        copies = [[], [], []]
        for i, (d, c) in enumerate(offsets):
            for q, order in enumerate(ORDERS):
                axis = order[0]
                at = pl.ds(*parts[q])
                a, core = (me[axis] + d) % 4, (me["c"] + c) % lay.cores
                if axis == "x":
                    source = packed.at[a, some, core, :, :, at, :]
                elif axis == "y":
                    source = packed.at[some, :, core, a, :, at, :]
                else:
                    source = packed.at[:, a, core, some, :, at, :]
                target = arrived[q].at[i, :, some] if axis == "z" else arrived[q].at[i, some]
                copy = remote(source, target, send1.at[half, q, i], recv1.at[half, q, i],
                              moved(axis, d, c))
                copy.start()
                copies[q].append(copy)
        return copies

    def second_stage(half, q, copies):
        order = ORDERS[q]
        for copy in copies[q]:
            copy.wait()
        at = pl.ds(*parts[q])
        rows = parts[q][1]
        dims = DIMS[order[0]]

        def reduce(k, carry):
            b, c = k // 2, 2 * half + k % 2
            spot = {order[0]: me[order[0]], order[1]: b, order[2]: c}
            owner = spot["x"] * 32 + spot["z"] * 8 + me["c"] * 4 + spot["y"]
            sums = [jnp.zeros((rows, side), jnp.float32) for _ in range(2)]
            for source in range(8):
                for j in range(cap):
                    if source == 0:
                        value = packed[spot["x"], spot["z"], me["c"], spot["y"], j, at, :]
                    else:
                        value = arrived[q][source - 1, spot[dims[0]], spot[dims[1]], j]
                    value = value.astype(jnp.float32)
                    table = (0, 0) if source == 0 else (q, source)
                    for s in range(2):
                        sums[s] = sums[s] + weight_s[(*table, 2 * j + s, owner)] * value
            for s in range(2):
                summed[q][b, c, s] = sums[s]
            return carry

        lax.fori_loop(0, 8, reduce, 0)
        some = pl.ds(2 * half, 2)
        mine = []
        for d in range(1, 4):
            copy = remote(summed[q].at[(me[order[1]] + d) % 4, some], landed[q].at[d - 1, some],
                          send2.at[half, q, d - 1], recv2.at[half, q, d - 1],
                          moved(order[1], d, 0))
            copy.start()
            mine.append(copy)
        return mine

    copies1 = [first_stage(0)]
    solve.load_faces()
    solve.faces()
    solve.send_rims()
    copies1.append(first_stage(1))
    gathers = []
    for q in range(3):
        for copy in weight_copies[q]:
            copy.wait()
        gathers.append(pltpu.make_async_copy(
            weight_in.at[q], weight_s.at[q, pl.ds(1, 7)], move_sem.at[2 + q]
        ))
        gathers[q].start()
    for gather in gathers:
        gather.wait()
    copies2 = [[second_stage(0, q, copies1[0]) for q in range(3)]]
    solve.load_rest()
    solve.prepare()
    solve.start(1, solve.layers)
    early = solve.send(0, 1, solve.layers, True)
    if common:
        common.reduce()
    copies2.append([second_stage(1, q, copies1[1]) for q in range(3)])
    for copy in early:
        copy.wait()
    solve.apply(0, 2, solve.layers)
    early = solve.send(1, 2, solve.layers, True)
    if common:
        common.gather()
    copies3 = []
    for q, order in enumerate(ORDERS):
        for half in range(2):
            for copy in copies2[half][q]:
                copy.wait()

        def reduce(k, carry, q=q, order=order):
            total = summed[q][me[order[1]], k]
            for d in range(3):
                total = total + landed[q][d, k]
            second[q][k] = total
            return carry

        lax.fori_loop(0, 4, reduce, 0)
        mine = []
        for d in range(1, 4):
            copy = remote(second[q].at[(me[order[2]] + d) % 4], third[q].at[d - 1],
                          send3.at[q, d - 1], recv3.at[q, d - 1], moved(order[2], d, 0))
            copy.start()
            mine.append(copy)
        copies3.append(mine)
    for copy in early:
        copy.wait()
    solve.apply(1, 3, solve.layers)
    early = solve.send(2, 3, solve.layers, True)
    for q, order in enumerate(ORDERS):
        for copy in copies3[q]:
            copy.wait()
        for s in range(2):
            total = second[q][me[order[2]], s]
            for d in range(3):
                total = total + third[q][d, s]
            surface[pl.ds(*parts[q]), s * side : (s + 1) * side] = total
    if common:
        common.add(surface)
    return early


class Common:
    def __init__(self, lay, me, held, weight_v, weight_in, spare, pieces, sums, others, whole,
                 send_a, recv_a, send_b, recv_b, send_c, recv_c):
        self.__dict__.update(locals())
        self.offsets = [(d, c) for d in range(4) for c in range(2) if (d, c) != (0, 0)]
        self.wide = lay.stages()[1]

    def piece(self, d, c):
        return (self.me["y"] + d) % 4 * 2 + (self.me["c"] + c) % 2

    def pack(self, index):
        for k in range(8):
            self.spare[k] = self.held[index, 16 * k : 16 * (k + 1), :]

    def scatter(self):
        self.copies = [
            remote(self.spare.at[self.piece(d, c)], self.pieces.at[i], self.send_a.at[i],
                   self.recv_a.at[i], self.lay.moved(dy=d, dc=c))
            for i, (d, c) in enumerate(self.offsets)
        ]
        for copy in self.copies:
            copy.start()

    def reduce(self):
        for copy in self.copies:
            copy.wait()
        for s in range(2):
            mine = self.spare[self.piece(0, 0)].astype(jnp.float32)
            total = self.weight_v[4 + s : 5 + s, :] * mine
            for i in range(7):
                weight = self.weight_in[1, i, 4 + s : 5 + s, :]
                total = total + weight * self.pieces[i].astype(jnp.float32)
            self.sums[0, s] = total
        self.copies = [
            remote(self.sums.at[0], self.others.at[i], self.send_b.at[i], self.recv_b.at[i],
                   self.lay.moved(**offset))
            for i, offset in enumerate(self.wide)
        ]
        for copy in self.copies:
            copy.start()

    def gather(self):
        for copy in self.copies:
            copy.wait()
        for s in range(2):
            total = self.sums[0, s]
            for i in range(len(self.wide)):
                total = total + self.others[i, s]
            self.sums[1, s] = total
        k = self.piece(0, 0)
        self.whole[k] = self.sums[1]
        self.copies = [
            remote(self.sums.at[1], self.whole.at[k], self.send_c.at[i], self.recv_c.at[i],
                   self.lay.moved(dy=d, dc=c))
            for i, (d, c) in enumerate(self.offsets)
        ]
        for copy in self.copies:
            copy.start()

    def add(self, surface):
        for copy in self.copies:
            copy.wait()
        me = self.me
        owner = me["x"] * 32 + me["z"] * 8 + me["c"] * 4 + me["y"]
        here = lax.broadcasted_iota(jnp.int32, (1, 128), 1) == owner
        mine = jnp.sum(jnp.where(here, self.weight_v[7:8, :], 0.0), axis=1, keepdims=True)
        for k in range(8):
            for s in range(2):
                at = (slice(16 * k, 16 * (k + 1)), slice(128 * s, 128 * (s + 1)))
                surface[at] = surface[at] + mine * self.whole[k, s]


def exchange_scratch(cap, side):
    parts = portions(side)

    def each(*lead, kind=jnp.float32):
        return [pltpu.VMEM((*lead, rows, side), kind) for _, rows in parts]

    bf16 = jnp.bfloat16
    dma = pltpu.SemaphoreType.DMA
    return [
        pltpu.VMEM((128, side, side), bf16),
        pltpu.VMEM((4, 4, 2, 4, cap, side, side), bf16),
        each(7, 4, 4, cap, kind=bf16), each(4, 4, 2), each(3, 4, 2), each(4, 2), each(3, 2),
        pltpu.VMEM((8, 128), jnp.int32), pltpu.VMEM((8, 128), jnp.float32),
        pltpu.VMEM((3, 7, 8, 128), jnp.float32),
        pltpu.SMEM((8, 128), jnp.int32), pltpu.SMEM((3, 8, 8, 128), jnp.float32),
        dma((5,)),
        dma((2, 3, 7)), dma((2, 3, 7)), dma((3, 7)), dma((3, 7)),
        dma((2, 3, 3)), dma((2, 3, 3)), dma((3, 3)), dma((3, 3)),
    ] + ([
        pltpu.VMEM((8, 16, side), bf16), pltpu.VMEM((7, 16, side), bf16),
        pltpu.VMEM((2, 2, 16, side), jnp.float32), pltpu.VMEM((15, 2, 16, side), jnp.float32),
        pltpu.VMEM((8, 2, 16, side), jnp.float32),
        dma((7,)), dma((7,)), dma((15,)), dma((15,)), dma((7,)), dma((7,)),
    ] if cap == 1 else [])


def kernel(lay, count_x, count_y, cap, sizes, *refs):
    owners, slots, patches, *inputs = refs[:10]
    solution, residual, sums = refs[10:13]
    solve_refs = refs[13 : 13 + sizes[0]]
    exchange_refs = refs[13 + sizes[0] : 13 + sizes[0] + sizes[1]]
    surface, load_sem = refs[13 + sizes[0] + sizes[1] :]
    solve = Solve(lay, count_x, count_y, solve_refs)
    held = exchange_refs[0]
    some = held.shape[0] // 4
    load = [
        pltpu.make_async_copy(
            patches.at[pl.ds(i * some, some)], held.at[pl.ds(i * some, some)], load_sem.at[7 + i]
        )
        for i in range(4)
    ]
    for copy in load:
        copy.start()
    loads = [
        pltpu.make_async_copy(source, target, load_sem.at[i])
        for i, (source, target) in enumerate(zip(inputs, solve_refs[:7]))
    ]
    solve.loads = loads
    friends = every_friend(lay, count_x)
    barrier = pltpu.get_barrier_semaphore()
    for friend in friends:
        pl.semaphore_signal(barrier, inc=1, device_id=friend, device_id_type=MESH)
    early = exchange_body(
        lay, cap, solve, lambda: pl.semaphore_wait(barrier, len(friends)), load, owners, slots, surface,
        *exchange_refs,
    )
    solve.start(0, 1, surface)
    late = solve.send(0, 0, 1, False)
    for copy in early:
        copy.wait()
    solve.apply(2, 4, solve.layers)
    for j in range(3):
        for copy in late:
            copy.wait()
        solve.apply(j, 0, j + 2)
        if j < 2:
            late = solve.send(j + 1, 0, j + 2, False)
    weight_v = exchange_refs[8]
    total = solve.total(weight_v[6:7, :])
    sums[...] = total
    solve.finish(total, solution, residual)


def move_kernel(a, b, c, d):
    c[...] = a[...]
    d[...] = b[...]


def move(*arrays):
    layers, rows, cols = arrays[0].shape
    block = pl.BlockSpec((layers // 4, rows, cols), lambda i: (i, 0, 0))
    return tuple(pl.pallas_call(
        move_kernel,
        grid=(4,),
        out_shape=[jax.ShapeDtypeStruct(x.shape, x.dtype) for x in arrays],
        in_specs=[block] * 2,
        out_specs=[block] * 2,
    )(*arrays))


def run(lay, count_x, count_y, cap, owners, slots, patches, *grids):
    layers, rows, cols = grids[0].shape
    solve = solve_scratch(lay, layers, rows, cols)
    moving = exchange_scratch(cap, patches.shape[1])
    return pl.pallas_call(
        functools.partial(kernel, lay, count_x, count_y, cap, (len(solve), len(moving))),
        out_shape=[jax.ShapeDtypeStruct((layers, rows, cols), jnp.float32)] * 2
        + [jax.ShapeDtypeStruct((8, 128), jnp.float32)],
        in_specs=[pl.BlockSpec(memory_space=pltpu.VMEM)] * 2
        + [pl.BlockSpec(memory_space=pl.ANY)] * (1 + len(grids)),
        out_specs=[pl.BlockSpec(memory_space=pltpu.VMEM)] * 3,
        scratch_shapes=solve + moving + [
            pltpu.VMEM((rows, cols), jnp.float32), pltpu.SemaphoreType.DMA((11,))
        ],
        compiler_params=pltpu.CompilerParams(
            collective_id=cap, has_side_effects=True,
            vmem_limit_bytes=(42 if cap == 1 else 60) * MIB,
        ),
    )(owners, slots, patches, *grids)


def on_device(forcing, patches, owners, slots, cond_x, cond_y, cond_z, storage, fixed, closed):
    count_x, count_y = lax.axis_size("gx"), lax.axis_size("gy")
    lay = Layout(count_x, count_y)
    args = (owners.T, slots.T, patches, forcing, cond_x, cond_y, cond_z, storage, fixed, closed)
    *quick, sums = run(lay, count_x, count_y, 1, *args)

    def general(args, quick):
        return tuple(run(lay, count_x, count_y, 2, *args)[:2])

    return move(*lax.cond(sums[6, 0] > 0.0, general, lambda args, quick: quick, args, tuple(quick)))


def solution(mesh):
    grid = P(None, "gx", "gy")
    return jax.shard_map(
        on_device,
        mesh=mesh,
        in_specs=(grid, P("gx", "gy", None), P("gx", "gy"), P("gx", "gy")) + (grid,) * 6,
        out_specs=(grid, grid),
        check_vma=False,
    )
```

```python
import functools

import jax
import jax.numpy as jnp
from jax import lax
from jax.experimental import pallas as pl
from jax.experimental.pallas import tpu as pltpu
from jax.sharding import PartitionSpec as P

MESH = pl.DeviceIdType.MESH
PAD = 8
MIB = 1 << 20


class Layout:
    def __init__(self, count_x, count_y):
        self.cores = 2 if count_x % 2 == 0 else 1
        chips = count_x // self.cores
        self.nz = 4 if chips % 4 == 0 else chips
        self.nx = chips // self.nz
        self.ny = count_y

    def me(self):
        gx, gy = lax.axis_index("gx"), lax.axis_index("gy")
        core = gx % self.cores
        chip = gx // self.cores
        return chip // self.nz, chip % self.nz, core, gy

    def device(self, x, z, core, y):
        return ((x * self.nz + z) * self.cores + core, y)

    def moved(self, dx=0, dz=0, dc=0, dy=0):
        x, z, core, y = self.me()
        return self.device(
            (x + dx) % self.nx, (z + dz) % self.nz, (core + dc) % self.cores, (y + dy) % self.ny
        )

    def stages(self):
        first = [
            dict(dc=c, dy=y) for c in range(self.cores) for y in range(self.ny) if (c, y) != (0, 0)
        ]
        second = [
            dict(dx=x, dz=z) for x in range(self.nx) for z in range(self.nz) if (x, z) != (0, 0)
        ]
        return [first, second]


def remote(src, dst, send, recv, device):
    return pltpu.make_async_remote_copy(
        src_ref=src, dst_ref=dst, send_sem=send, recv_sem=recv, device_id=device, device_id_type=MESH
    )


class Solve:
    names = (
        "forcing", "cond_x", "cond_y", "cond_z", "storage", "fixed", "closed", "tees", "east",
        "north", "south", "above", "inverse", "enns", "col_out", "col_in", "partial", "gathered",
        "halo_send", "halo_recv", "sum_send", "sum_recv",
    )

    def __init__(self, lay, count_x, count_y, refs):
        self.lay, self.count_x, self.count_y = lay, count_x, count_y
        for name, ref in zip(self.names, refs, strict=True):
            setattr(self, name, ref)
        self.layers, self.rows, self.cols = self.forcing.shape
        self.step = 32
        self.blocks = self.rows // self.step
        gx, gy = lax.axis_index("gx"), lax.axis_index("gy")
        self.gx, self.gy = gx, gy
        self.right = ((gx + 1) % count_x, gy)
        self.left = ((gx + count_x - 1) % count_x, gy)
        self.up = (gx, (gy + 1) % count_y)
        self.down = (gx, (gy + count_y - 1) % count_y)
        lanes = lax.broadcasted_iota(jnp.int32, (self.step, self.cols), 1)
        self.first_lane, self.last_lane = lanes == 0, lanes == self.cols - 1
        square = (self.rows, self.rows)
        self.eye = lax.broadcasted_iota(jnp.int32, square, 0) == lax.broadcasted_iota(
            jnp.int32, square, 1
        )
        self.zero = jnp.zeros((8, self.cols), jnp.float32)
        self.moments = [self.zero] * 6

    def start_loads(self):
        for i in (1, 6, 2, 3, 4, 5, 0):
            self.loads[i].start()

    def load_faces(self):
        for i in (1, 6, 2, 3):
            self.loads[i].wait()

    def load_rest(self):
        for i in (4, 5, 0):
            self.loads[i].wait()

    def column(self, block):
        wide = jnp.broadcast_to(block, (self.rows, self.rows))
        return jnp.sum(jnp.where(self.eye, wide, 0.0), axis=0, keepdims=True)

    def uncolumn(self, row, block):
        wide = jnp.broadcast_to(row, (self.step, self.rows))
        mask = self.eye[block * self.step : (block + 1) * self.step]
        return jnp.sum(jnp.where(mask, wide, 0.0), axis=1, keepdims=True)

    def fold(self, x):
        parts = [x[i * 8 : (i + 1) * 8] for i in range(self.step // 8)]
        while len(parts) > 1:
            parts = [a + b for a, b in zip(parts[::2], parts[1::2])]
        return parts[0]

    def faces(self):
        layers, rows, cols, step = self.layers, self.rows, self.cols, self.step
        east_last = jnp.where(self.gx == self.count_x - 1, 0.0, 1.0).astype(jnp.float32)
        north_last = jnp.where(self.gy == self.count_y - 1, 0.0, 1.0).astype(jnp.float32)
        north_scale = jnp.where(self.last_lane, north_last, 1.0)
        row_ids = lax.broadcasted_iota(jnp.int32, (step, cols), 0)

        def body(layer, carry):
            for b in range(self.blocks):
                at = pl.ds(b * step, step)
                open_faces = (1 - self.closed[layer, at, :]).astype(jnp.float32)
                scale = jnp.where(row_ids == rows - 1 - b * step, east_last, 1.0)
                self.east[layer, pl.ds(PAD + b * step, step), :] = (
                    self.cond_x[layer, at, :] * open_faces * scale
                )
                self.north[layer, at, :] = self.cond_y[layer, at, :] * open_faces * north_scale
            self.above[layer + 1] = self.cond_z[layer] * jnp.where(layer == layers - 1, 0.0, 1.0)
            self.col_out[0, 0, pl.ds(layer, 1), :] = self.column(
                self.north[layer, :, cols - 1 : cols]
            )
            return carry

        self.above[0] = jnp.zeros((rows, cols), jnp.float32)
        lax.fori_loop(0, layers, body, 0)
        self.rims = [
            remote(self.east.at[:, pl.ds(PAD + rows - 1, 1), :],
                   self.east.at[:, pl.ds(PAD - 1, 1), :],
                   self.halo_send.at[0, 0], self.halo_recv.at[0, 0], self.right),
            remote(self.col_out.at[0, 0], self.col_in.at[0, 0],
                   self.halo_send.at[0, 1], self.halo_recv.at[0, 1], self.up),
        ]

    def send_rims(self):
        for copy in self.rims:
            copy.start()

    def prepare(self):
        step = self.step
        for copy in self.rims:
            copy.wait()

        def body(layer, carry):
            south_row = self.col_in[0, 0, pl.ds(layer, 1), :]
            for b in range(self.blocks):
                at = pl.ds(b * step, step)
                north = self.north[layer, at, :]
                south = jnp.where(
                    self.first_lane, self.uncolumn(south_row, b), pltpu.roll(north, 1, 1)
                )
                self.south[layer, at, :] = south
                keep = (1 - self.fixed[layer, at, :]).astype(jnp.float32)
                diagonal = (
                    self.storage[layer, at, :]
                    + self.east[layer, pl.ds(PAD + b * step, step), :]
                    + self.east[layer, pl.ds(PAD - 1 + b * step, step), :]
                    + north + south + self.above[layer + 1, at, :] + self.above[layer, at, :]
                )
                self.inverse[layer, at, :] = keep / diagonal
            return carry

        lax.fori_loop(0, self.layers, body, 0)

    def start(self, low, high, surface=None):
        step = self.step

        def body(layer, total):
            for b in range(self.blocks):
                at = pl.ds(b * step, step)
                keep = (1 - self.fixed[layer, at, :]).astype(jnp.float32)
                value = self.forcing[layer, at, :]
                if surface is not None:
                    value = value + surface[at, :]
                value = keep * value
                self.enns[0, layer, at, :] = value
                tee = self.inverse[layer, at, :] * value
                self.tees[0, layer, pl.ds(PAD + b * step, step), :] = tee
                total = total + self.fold(tee * value)
            return total

        self.moments[0] = lax.fori_loop(low, high, body, self.moments[0])

    def send(self, j, low, high, early):
        rows, cols = self.rows, self.cols

        some = pl.ds(low, high - low)
        tee = self.tees.at[j, some]
        k = 2 * j + 1 + early
        copies = [
            remote(tee.at[:, pl.ds(PAD + rows - 1, 1), :], tee.at[:, pl.ds(PAD - 1, 1), :],
                   self.halo_send.at[k, 0], self.halo_recv.at[k, 0], self.right),
            remote(tee.at[:, pl.ds(PAD, 1), :], tee.at[:, pl.ds(PAD + rows, 1), :],
                   self.halo_send.at[k, 1], self.halo_recv.at[k, 1], self.left),
            remote(self.col_out.at[j + 1, 0, some], self.col_in.at[j + 1, 0, some],
                   self.halo_send.at[k, 2], self.halo_recv.at[k, 2], self.up),
            remote(self.col_out.at[j + 1, 1, some], self.col_in.at[j + 1, 1, some],
                   self.halo_send.at[k, 3], self.halo_recv.at[k, 3], self.down),
        ]
        for copy in copies[:2]:
            copy.start()

        def body(layer, carry):
            here = self.tees.at[j, layer, pl.ds(PAD, rows), :]
            self.col_out[j + 1, 0, pl.ds(layer, 1), :] = self.column(here[:, cols - 1 : cols])
            self.col_out[j + 1, 1, pl.ds(layer, 1), :] = self.column(here[:, 0:1])
            return carry

        lax.fori_loop(low, high, body, 0)
        for copy in copies[2:]:
            copy.start()
        return copies

    def apply(self, j, low, high):
        layers, cols, step, tees = self.layers, self.cols, self.step, self.tees

        def body(layer, carry):
            odd, even = carry
            south_row = self.col_in[j + 1, 0, pl.ds(layer, 1), :]
            north_row = self.col_in[j + 1, 1, pl.ds(layer, 1), :]
            higher = jnp.minimum(layer + 1, layers - 1)
            lower = jnp.maximum(layer - 1, 0)
            for b in range(self.blocks):
                at = pl.ds(b * step, step)
                mid = pl.ds(PAD + b * step, step)
                before = pl.ds(PAD - 1 + b * step, step)
                after = pl.ds(PAD + 1 + b * step, step)
                here = tees[j, layer, mid, :]
                north = jnp.where(
                    self.last_lane, self.uncolumn(north_row, b), pltpu.roll(here, cols - 1, 1)
                )
                south = jnp.where(
                    self.first_lane, self.uncolumn(south_row, b), pltpu.roll(here, 1, 1)
                )
                flux = self.east[layer, mid, :] * tees[j, layer, after, :]
                flux += self.east[layer, before, :] * tees[j, layer, before, :]
                flux += self.north[layer, at, :] * north + self.south[layer, at, :] * south
                flux += self.above[layer + 1, at, :] * tees[j, higher, mid, :]
                flux += self.above[layer, at, :] * tees[j, lower, mid, :]
                self.enns[j + 1, layer, at, :] = flux
                odd = odd + self.fold(here * flux)
                if j < 2:
                    tee = self.inverse[layer, at, :] * flux
                    tees[j + 1, layer, mid, :] = tee
                    even = even + self.fold(tee * flux)
            return odd, even

        last = self.moments[2 * j + 2] if j < 2 else self.zero
        odd, even = lax.fori_loop(low, high, body, (self.moments[2 * j + 1], last))
        self.moments[2 * j + 1] = odd
        if j < 2:
            self.moments[2 * j + 2] = even

    def total(self, extra):
        partial, gathered = self.partial, self.gathered
        partial[0] = jnp.zeros((8, 128), jnp.float32)
        for k, value in enumerate(self.moments):
            both = sum(value[:, i * 128 : (i + 1) * 128] for i in range(self.cols // 128))
            partial[0, k : k + 1, :] = jnp.sum(both, axis=0, keepdims=True)
        partial[0, 6:7, :] = extra
        base = 0
        for s, peers in enumerate(self.lay.stages()):
            copies = [
                remote(partial.at[s], gathered.at[base + i], self.sum_send.at[base + i],
                       self.sum_recv.at[base + i], self.lay.moved(**offset))
                for i, offset in enumerate(peers)
            ]
            for copy in copies:
                copy.start()
            for copy in copies:
                copy.wait()
            total = partial[s]
            for i in range(len(peers)):
                total = total + gathered[base + i]
            base += len(peers)
            partial[s + 1] = total
        return partial[len(self.lay.stages())]

    def finish(self, total, solution, residual, outs, sem):
        def leave(layer):
            return [
                pltpu.make_async_copy(source.at[layer], target.at[layer], sem.at[k, layer])
                for k, (source, target) in enumerate(zip((solution, residual), outs))
            ]

        sol_w, res_w = scalars(total)
        step = self.step

        def body(layer, carry):
            for b in range(self.blocks):
                at = pl.ds(b * step, step)
                mid = pl.ds(PAD + b * step, step)
                keep = (1 - self.fixed[layer, at, :]).astype(jnp.float32)
                out = sol_w[0] * self.tees[0, layer, mid, :]
                for j in range(1, 3):
                    out += sol_w[j] * self.tees[j, layer, mid, :]
                solution[layer, at, :] = out
                out = res_w[0] * self.enns[0, layer, at, :]
                for j in range(1, 4):
                    out += res_w[j] * self.enns[j, layer, at, :]
                residual[layer, at, :] = keep * out
            for copy in leave(layer):
                copy.start()
            return carry

        lax.fori_loop(0, self.layers, body, 0)
        for layer in range(self.layers):
            for copy in leave(layer):
                copy.wait()


def solve_scratch(lay, layers, rows, cols):
    peers = sum(len(s) for s in lay.stages())
    f32, dma = jnp.float32, pltpu.SemaphoreType.DMA

    def full(*lead, kind=f32):
        return pltpu.VMEM((*lead, layers, rows, cols), kind)

    def padded(*lead):
        return pltpu.VMEM((*lead, layers, rows + 2 * PAD, cols), f32)

    return [
        full(), full(), full(), full(), full(), full(kind=jnp.int32), full(kind=jnp.int32),
        padded(3), padded(), full(), full(),
        pltpu.VMEM((layers + 1, rows, cols), f32), full(), full(4),
        pltpu.VMEM((4, 2, layers, rows), f32), pltpu.VMEM((4, 2, layers, rows), f32),
        pltpu.VMEM((len(lay.stages()) + 1, 8, 128), f32), pltpu.VMEM((peers, 8, 128), f32),
        dma((7, 4)), dma((7, 4)), dma((peers,)), dma((peers,)),
    ]


def every_friend(lay, count_x):
    gx, gy = lax.axis_index("gx"), lax.axis_index("gy")
    friends = [((gx + 1) % count_x, gy), ((gx + count_x - 1) % count_x, gy), lay.moved(dc=1)]
    for axis in "xyz":
        friends += [
            lay.moved(**{"d" + axis: d, "dc": c}) for d in range(1, 4) for c in range(lay.cores)
        ]
    return friends + [lay.moved(dx=x, dz=z) for x in range(1, 4) for z in range(1, 4)]


def scalars(total):
    def reduce(row):
        return jnp.sum(row, axis=1, keepdims=True)

    rows = [total[k : k + 1, :] for k in range(6)]
    m0, m1 = reduce(rows[0]), reduce(rows[1])
    shift = jnp.where(m1 > 0.5 * m0, 1.0, 0.0)
    scale = 1.0 - shift
    c, current = [m0], rows
    for _ in range(5):
        current = [current[q + 1] - shift * current[q] for q in range(len(current) - 1)]
        c.append(reduce(current[0]))
    d = [scale * c[k] - c[k + 1] for k in range(5)]
    zero = jnp.zeros_like(m0)
    rho, pi, sol = [zero + 1.0], [zero + 1.0], [zero, zero, zero]
    inner = m0
    for i in range(3):
        curve = zero
        for a in range(len(pi)):
            for b in range(len(pi)):
                curve = curve + pi[a] * pi[b] * d[a + b]
        alpha = inner / curve
        for a in range(len(pi)):
            sol[a] = sol[a] + alpha * pi[a]
        rho = rho + [zero]
        for a in range(len(pi)):
            rho[a] = rho[a] - alpha * scale * pi[a]
            rho[a + 1] = rho[a + 1] + alpha * pi[a]
        if i < 2:
            inner_next = zero
            for a in range(len(rho)):
                for b in range(len(rho)):
                    inner_next = inner_next + rho[a] * rho[b] * c[a + b]
            beta = inner_next / inner
            pi = [rho[a] + beta * pi[a] if a < len(pi) else rho[a] for a in range(len(rho))]
            inner = inner_next

    def unshift(w):
        out = [zero] * len(w)
        for k in reversed(range(len(w))):
            moved = [zero] + out[:-1]
            out = [moved[i] - shift * out[i] for i in range(len(w))]
            out[0] = out[0] + w[k]
        return out

    return unshift(sol), unshift(rho)


ORDERS = (("x", "y", "z"), ("y", "z", "x"), ("z", "x", "y"))
DIMS = {"x": "zy", "y": "xz", "z": "xy"}


def portions(side):
    tiles = side // 8
    cut = [0, tiles // 3, tiles - tiles // 3, tiles]
    return [(8 * cut[i], 8 * (cut[i + 1] - cut[i])) for i in range(3)]


def exchange_body(
    lay, cap, solve, enter, load, owners, slots, surface, held, packed, arrived, summed, landed, second,
    third, index_v, weight_v, weight_in, index_s, weight_s, move_sem,
    send1, recv1, send1w, recv1w, send2, recv2, send3, recv3, *star,
):
    per_device, side, _ = held.shape
    me = dict(zip("xzcy", lay.me()))
    count = dict(x=lay.nx, y=lay.ny, z=lay.nz)
    parts = portions(side)

    shape = (per_device, 128)
    patch_ids = lax.broadcasted_iota(jnp.int32, shape, 0)
    row = (owners[...] * 2 + slots[...]).astype(jnp.float32)
    column = jnp.sum(
        jnp.where(solve.eye, jnp.broadcast_to(row, shape), 0.0), axis=1, keepdims=True
    )
    place = jnp.broadcast_to(column, shape) - (
        2 * lax.broadcasted_iota(jnp.int32, shape, 1)
    ).astype(jnp.float32)
    hit = jnp.logical_or(place == 0.0, place == 1.0)
    first = jnp.min(jnp.where(hit, patch_ids, per_device), axis=0, keepdims=True)
    last = jnp.max(jnp.where(hit, patch_ids, -1), axis=0, keepdims=True)
    index_v[0:1, :] = jnp.minimum(first, per_device - 1)
    index_v[1:2, :] = jnp.maximum(last, 0)
    again = last > first
    for j in range(2):
        chosen = patch_ids == (first if j == 0 else last)
        if j > 0:
            chosen = jnp.logical_and(chosen, again)
        chosen = jnp.logical_and(hit, chosen)
        for s in range(2):
            weight_v[2 * j + s : 2 * j + s + 1, :] = jnp.sum(
                jnp.where(jnp.logical_and(chosen, place == float(s)), 1.0, 0.0), axis=0, keepdims=True
            )
    doubled = jnp.where(again, 1.0, 0.0)
    for s in range(2):
        weight_v[4 + s : 5 + s, :] = jnp.broadcast_to(
            jnp.sum(weight_v[2 + s : 3 + s, :], axis=1, keepdims=True), (1, 128)
        )
    extra = jnp.maximum(jnp.sum(doubled, axis=1, keepdims=True) - 1.0, 0.0)
    weight_v[6:7, :] = jnp.broadcast_to(extra, (1, 128))
    weight_v[7:8, :] = doubled
    spare_index = jnp.max(jnp.where(again, last, 0), axis=1, keepdims=True)
    index_v[2:3, :] = jnp.broadcast_to(spare_index, (1, 128))
    to_scalar = pltpu.make_async_copy(index_v, index_s, move_sem.at[0])
    to_scalar.start()
    own_weight = pltpu.make_async_copy(weight_v, weight_s.at[0, 0], move_sem.at[1])
    own_weight.start()

    offsets = [(d, c) for d in range(4) for c in range(lay.cores) if (d, c) != (0, 0)]

    def moved(axis, d, c):
        return lay.moved(**{"d" + axis: d, "dc": c})

    weight_copies = [
        [
            remote(weight_v, weight_in.at[q, i], send1w.at[q, i], recv1w.at[q, i],
                   moved(order[0], d, c))
            for i, (d, c) in enumerate(offsets)
        ]
        for q, order in enumerate(ORDERS)
    ]
    for copy in load:
        copy.wait()
    solve.start_loads()
    to_scalar.wait()
    own_weight.wait()

    def pack(o, carry):
        for j in range(cap):
            packed[o // 32, o // 8 % 4, o // 4 % 2, o % 4, j] = held[index_s[j, o]]
        return carry

    lax.fori_loop(0, 128, pack, 0)
    common = Common(lay, me, held, weight_v, weight_in, *star) if cap == 1 else None
    if common:
        common.pack(index_s[2, 0])
    enter()
    for group in weight_copies:
        for copy in group:
            copy.start()
    if common:
        common.scatter()

    def first_stage(half):
        some = pl.ds(2 * half, 2)
        copies = [[], [], []]
        for i, (d, c) in enumerate(offsets):
            for q, order in enumerate(ORDERS):
                axis = order[0]
                at = pl.ds(*parts[q])
                a, core = (me[axis] + d) % 4, (me["c"] + c) % lay.cores
                if axis == "x":
                    source = packed.at[a, some, core, :, :, at, :]
                elif axis == "y":
                    source = packed.at[some, :, core, a, :, at, :]
                else:
                    source = packed.at[:, a, core, some, :, at, :]
                target = arrived[q].at[i, :, some] if axis == "z" else arrived[q].at[i, some]
                copy = remote(source, target, send1.at[half, q, i], recv1.at[half, q, i],
                              moved(axis, d, c))
                copy.start()
                copies[q].append(copy)
        return copies

    def second_stage(half, q, copies):
        order = ORDERS[q]
        for copy in copies[q]:
            copy.wait()
        at = pl.ds(*parts[q])
        rows = parts[q][1]
        dims = DIMS[order[0]]

        def reduce(k, carry):
            b, c = k // 2, 2 * half + k % 2
            spot = {order[0]: me[order[0]], order[1]: b, order[2]: c}
            owner = spot["x"] * 32 + spot["z"] * 8 + me["c"] * 4 + spot["y"]
            sums = [jnp.zeros((rows, side), jnp.float32) for _ in range(2)]
            for source in range(8):
                for j in range(cap):
                    if source == 0:
                        value = packed[spot["x"], spot["z"], me["c"], spot["y"], j, at, :]
                    else:
                        value = arrived[q][source - 1, spot[dims[0]], spot[dims[1]], j]
                    value = value.astype(jnp.float32)
                    table = (0, 0) if source == 0 else (q, source)
                    for s in range(2):
                        sums[s] = sums[s] + weight_s[(*table, 2 * j + s, owner)] * value
            for s in range(2):
                summed[q][b, c, s] = sums[s]
            return carry

        lax.fori_loop(0, 8, reduce, 0)
        some = pl.ds(2 * half, 2)
        mine = []
        for d in range(1, 4):
            copy = remote(summed[q].at[(me[order[1]] + d) % 4, some], landed[q].at[d - 1, some],
                          send2.at[half, q, d - 1], recv2.at[half, q, d - 1],
                          moved(order[1], d, 0))
            copy.start()
            mine.append(copy)
        return mine

    copies1 = [first_stage(0)]
    solve.load_faces()
    solve.faces()
    solve.send_rims()
    copies1.append(first_stage(1))
    gathers = []
    for q in range(3):
        for copy in weight_copies[q]:
            copy.wait()
        gathers.append(pltpu.make_async_copy(
            weight_in.at[q], weight_s.at[q, pl.ds(1, 7)], move_sem.at[2 + q]
        ))
        gathers[q].start()
    for gather in gathers:
        gather.wait()
    copies2 = [[second_stage(0, q, copies1[0]) for q in range(3)]]
    solve.load_rest()
    solve.prepare()
    solve.start(1, solve.layers)
    early = solve.send(0, 1, solve.layers, True)
    if common:
        common.reduce()
    copies2.append([second_stage(1, q, copies1[1]) for q in range(3)])
    for copy in early:
        copy.wait()
    solve.apply(0, 2, solve.layers)
    early = solve.send(1, 2, solve.layers, True)
    if common:
        common.gather()
    copies3 = []
    for q, order in enumerate(ORDERS):
        for half in range(2):
            for copy in copies2[half][q]:
                copy.wait()

        def reduce(k, carry, q=q, order=order):
            total = summed[q][me[order[1]], k]
            for d in range(3):
                total = total + landed[q][d, k]
            second[q][k] = total
            return carry

        lax.fori_loop(0, 4, reduce, 0)
        mine = []
        for d in range(1, 4):
            copy = remote(second[q].at[(me[order[2]] + d) % 4], third[q].at[d - 1],
                          send3.at[q, d - 1], recv3.at[q, d - 1], moved(order[2], d, 0))
            copy.start()
            mine.append(copy)
        copies3.append(mine)
    for copy in early:
        copy.wait()
    solve.apply(1, 3, solve.layers)
    early = solve.send(2, 3, solve.layers, True)
    for q, order in enumerate(ORDERS):
        for copy in copies3[q]:
            copy.wait()
        for s in range(2):
            total = second[q][me[order[2]], s]
            for d in range(3):
                total = total + third[q][d, s]
            surface[pl.ds(*parts[q]), s * side : (s + 1) * side] = total
    if common:
        common.add(surface)
    return early


class Common:
    def __init__(self, lay, me, held, weight_v, weight_in, spare, pieces, sums, others, whole,
                 send_a, recv_a, send_b, recv_b, send_c, recv_c):
        self.__dict__.update(locals())
        self.offsets = [(d, c) for d in range(4) for c in range(2) if (d, c) != (0, 0)]
        self.wide = lay.stages()[1]

    def piece(self, d, c):
        return (self.me["y"] + d) % 4 * 2 + (self.me["c"] + c) % 2

    def pack(self, index):
        for k in range(8):
            self.spare[k] = self.held[index, 16 * k : 16 * (k + 1), :]

    def scatter(self):
        self.copies = [
            remote(self.spare.at[self.piece(d, c)], self.pieces.at[i], self.send_a.at[i],
                   self.recv_a.at[i], self.lay.moved(dy=d, dc=c))
            for i, (d, c) in enumerate(self.offsets)
        ]
        for copy in self.copies:
            copy.start()

    def reduce(self):
        for copy in self.copies:
            copy.wait()
        for s in range(2):
            mine = self.spare[self.piece(0, 0)].astype(jnp.float32)
            total = self.weight_v[4 + s : 5 + s, :] * mine
            for i in range(7):
                weight = self.weight_in[1, i, 4 + s : 5 + s, :]
                total = total + weight * self.pieces[i].astype(jnp.float32)
            self.sums[0, s] = total
        self.copies = [
            remote(self.sums.at[0], self.others.at[i], self.send_b.at[i], self.recv_b.at[i],
                   self.lay.moved(**offset))
            for i, offset in enumerate(self.wide)
        ]
        for copy in self.copies:
            copy.start()

    def gather(self):
        for copy in self.copies:
            copy.wait()
        for s in range(2):
            total = self.sums[0, s]
            for i in range(len(self.wide)):
                total = total + self.others[i, s]
            self.sums[1, s] = total
        k = self.piece(0, 0)
        self.whole[k] = self.sums[1]
        self.copies = [
            remote(self.sums.at[1], self.whole.at[k], self.send_c.at[i], self.recv_c.at[i],
                   self.lay.moved(dy=d, dc=c))
            for i, (d, c) in enumerate(self.offsets)
        ]
        for copy in self.copies:
            copy.start()

    def add(self, surface):
        for copy in self.copies:
            copy.wait()
        me = self.me
        owner = me["x"] * 32 + me["z"] * 8 + me["c"] * 4 + me["y"]
        here = lax.broadcasted_iota(jnp.int32, (1, 128), 1) == owner
        mine = jnp.sum(jnp.where(here, self.weight_v[7:8, :], 0.0), axis=1, keepdims=True)
        for k in range(8):
            for s in range(2):
                at = (slice(16 * k, 16 * (k + 1)), slice(128 * s, 128 * (s + 1)))
                surface[at] = surface[at] + mine * self.whole[k, s]


def exchange_scratch(cap, side):
    parts = portions(side)

    def each(*lead, kind=jnp.float32):
        return [pltpu.VMEM((*lead, rows, side), kind) for _, rows in parts]

    bf16 = jnp.bfloat16
    dma = pltpu.SemaphoreType.DMA
    return [
        pltpu.VMEM((128, side, side), bf16),
        pltpu.VMEM((4, 4, 2, 4, cap, side, side), bf16),
        each(7, 4, 4, cap, kind=bf16), each(4, 4, 2), each(3, 4, 2), each(4, 2), each(3, 2),
        pltpu.VMEM((8, 128), jnp.int32), pltpu.VMEM((8, 128), jnp.float32),
        pltpu.VMEM((3, 7, 8, 128), jnp.float32),
        pltpu.SMEM((8, 128), jnp.int32), pltpu.SMEM((3, 8, 8, 128), jnp.float32),
        dma((5,)),
        dma((2, 3, 7)), dma((2, 3, 7)), dma((3, 7)), dma((3, 7)),
        dma((2, 3, 3)), dma((2, 3, 3)), dma((3, 3)), dma((3, 3)),
    ] + ([
        pltpu.VMEM((8, 16, side), bf16), pltpu.VMEM((7, 16, side), bf16),
        pltpu.VMEM((2, 2, 16, side), jnp.float32), pltpu.VMEM((15, 2, 16, side), jnp.float32),
        pltpu.VMEM((8, 2, 16, side), jnp.float32),
        dma((7,)), dma((7,)), dma((15,)), dma((15,)), dma((7,)), dma((7,)),
    ] if cap == 1 else [])


def kernel(lay, count_x, count_y, cap, sizes, *refs):
    owners, slots, patches, *inputs = refs[:10]
    *outs, sums = refs[10:13]
    solve_refs = refs[13 : 13 + sizes[0]]
    exchange_refs = refs[13 + sizes[0] : 13 + sizes[0] + sizes[1]]
    surface, load_sem, solution, residual, leave_sem = refs[13 + sizes[0] + sizes[1] :]
    solve = Solve(lay, count_x, count_y, solve_refs)
    held = exchange_refs[0]
    some = held.shape[0] // 4
    load = [
        pltpu.make_async_copy(
            patches.at[pl.ds(i * some, some)], held.at[pl.ds(i * some, some)], load_sem.at[7 + i]
        )
        for i in range(4)
    ]
    for copy in load:
        copy.start()
    loads = [
        pltpu.make_async_copy(source, target, load_sem.at[i])
        for i, (source, target) in enumerate(zip(inputs, solve_refs[:7]))
    ]
    solve.loads = loads
    friends = every_friend(lay, count_x)
    barrier = pltpu.get_barrier_semaphore()
    for friend in friends:
        pl.semaphore_signal(barrier, inc=1, device_id=friend, device_id_type=MESH)
    early = exchange_body(
        lay, cap, solve, lambda: pl.semaphore_wait(barrier, len(friends)), load, owners, slots, surface,
        *exchange_refs,
    )
    solve.start(0, 1, surface)
    late = solve.send(0, 0, 1, False)
    for copy in early:
        copy.wait()
    solve.apply(2, 4, solve.layers)
    for j in range(3):
        solve.apply(j, j + 1, j + 2)
        for copy in late:
            copy.wait()
        solve.apply(j, 0, j + 1)
        if j < 2:
            late = solve.send(j + 1, 0, j + 2, False)
    weight_v = exchange_refs[8]
    total = solve.total(weight_v[6:7, :])
    sums[...] = total
    solve.finish(total, solution, residual, outs, leave_sem)


def move_kernel(a, b, c, d, held, sem):
    layers = a.shape[0]
    into = [pltpu.make_async_copy(x.at[i], held.at[k, i], sem.at[0, k, i])
            for i in range(layers) for k, x in enumerate((a, b))]
    away = [pltpu.make_async_copy(held.at[k, i], x.at[i], sem.at[1, k, i])
            for i in range(layers) for k, x in enumerate((c, d))]
    for copy in into:
        copy.start()
    for first, then in zip(into, away):
        first.wait()
        then.start()
    for copy in away:
        copy.wait()


def move(*arrays):
    shape = arrays[0].shape
    return tuple(pl.pallas_call(
        move_kernel,
        out_shape=[jax.ShapeDtypeStruct(x.shape, x.dtype) for x in arrays],
        in_specs=[pl.BlockSpec(memory_space=pl.ANY)] * 2,
        out_specs=[pl.BlockSpec(memory_space=pl.ANY)] * 2,
        scratch_shapes=[
            pltpu.VMEM((2, *shape), jnp.float32), pltpu.SemaphoreType.DMA((2, 2, shape[0]))
        ],
    )(*arrays))


def run(lay, count_x, count_y, cap, owners, slots, patches, *grids):
    layers, rows, cols = grids[0].shape
    solve = solve_scratch(lay, layers, rows, cols)
    moving = exchange_scratch(cap, patches.shape[1])
    return pl.pallas_call(
        functools.partial(kernel, lay, count_x, count_y, cap, (len(solve), len(moving))),
        out_shape=[jax.ShapeDtypeStruct((layers, rows, cols), jnp.float32)] * 2
        + [jax.ShapeDtypeStruct((8, 128), jnp.float32)],
        in_specs=[pl.BlockSpec(memory_space=pltpu.VMEM)] * 2
        + [pl.BlockSpec(memory_space=pl.ANY)] * (1 + len(grids)),
        out_specs=[pl.BlockSpec(memory_space=pl.ANY)] * 2
        + [pl.BlockSpec(memory_space=pltpu.VMEM)],
        scratch_shapes=solve + moving + [
            pltpu.VMEM((rows, cols), jnp.float32), pltpu.SemaphoreType.DMA((11,)),
            pltpu.VMEM((layers, rows, cols), jnp.float32),
            pltpu.VMEM((layers, rows, cols), jnp.float32),
            pltpu.SemaphoreType.DMA((2, layers)),
        ],
        compiler_params=pltpu.CompilerParams(
            collective_id=cap, has_side_effects=True,
            vmem_limit_bytes=(42 if cap == 1 else 60) * MIB,
        ),
    )(owners, slots, patches, *grids)


def on_device(forcing, patches, owners, slots, cond_x, cond_y, cond_z, storage, fixed, closed):
    count_x, count_y = lax.axis_size("gx"), lax.axis_size("gy")
    lay = Layout(count_x, count_y)
    args = (owners.T, slots.T, patches, forcing, cond_x, cond_y, cond_z, storage, fixed, closed)
    *quick, sums = run(lay, count_x, count_y, 1, *args)

    def general(args, quick):
        return tuple(run(lay, count_x, count_y, 2, *args)[:2])

    return move(*lax.cond(sums[6, 0] > 0.0, general, lambda args, quick: quick, args, tuple(quick)))


def solution(mesh):
    grid = P(None, "gx", "gy")
    return jax.shard_map(
        on_device,
        mesh=mesh,
        in_specs=(grid, P("gx", "gy", None), P("gx", "gy"), P("gx", "gy")) + (grid,) * 6,
        out_specs=(grid, grid),
        check_vma=False,
    )
```

```python
import functools

import jax
import jax.numpy as jnp
from jax import lax
from jax.experimental import pallas as pl
from jax.experimental.pallas import tpu as pltpu
from jax.sharding import PartitionSpec as P

MESH = pl.DeviceIdType.MESH
PAD = 8
MIB = 1 << 20


class Layout:
    def __init__(self, count_x, count_y):
        self.cores = 2 if count_x % 2 == 0 else 1
        chips = count_x // self.cores
        self.nz = 4 if chips % 4 == 0 else chips
        self.nx = chips // self.nz
        self.ny = count_y

    def me(self):
        gx, gy = lax.axis_index("gx"), lax.axis_index("gy")
        core = gx % self.cores
        chip = gx // self.cores
        return chip // self.nz, chip % self.nz, core, gy

    def device(self, x, z, core, y):
        return ((x * self.nz + z) * self.cores + core, y)

    def moved(self, dx=0, dz=0, dc=0, dy=0):
        x, z, core, y = self.me()
        return self.device(
            (x + dx) % self.nx, (z + dz) % self.nz, (core + dc) % self.cores, (y + dy) % self.ny
        )

    def stages(self):
        first = [
            dict(dc=c, dy=y) for c in range(self.cores) for y in range(self.ny) if (c, y) != (0, 0)
        ]
        second = [
            dict(dx=x, dz=z) for x in range(self.nx) for z in range(self.nz) if (x, z) != (0, 0)
        ]
        return [first, second]


def remote(src, dst, send, recv, device):
    return pltpu.make_async_remote_copy(
        src_ref=src, dst_ref=dst, send_sem=send, recv_sem=recv, device_id=device, device_id_type=MESH
    )


class Solve:
    names = (
        "forcing", "cond_x", "cond_y", "cond_z", "storage", "fixed", "closed", "tees", "east",
        "north", "south", "above", "inverse", "enns", "col_out", "col_in", "partial", "gathered",
        "halo_send", "halo_recv", "sum_send", "sum_recv",
    )

    def __init__(self, lay, count_x, count_y, refs):
        self.lay, self.count_x, self.count_y = lay, count_x, count_y
        for name, ref in zip(self.names, refs, strict=True):
            setattr(self, name, ref)
        self.layers, self.rows, self.cols = self.forcing.shape
        self.step = 32
        self.blocks = self.rows // self.step
        gx, gy = lax.axis_index("gx"), lax.axis_index("gy")
        self.gx, self.gy = gx, gy
        self.right = ((gx + 1) % count_x, gy)
        self.left = ((gx + count_x - 1) % count_x, gy)
        self.up = (gx, (gy + 1) % count_y)
        self.down = (gx, (gy + count_y - 1) % count_y)
        lanes = lax.broadcasted_iota(jnp.int32, (self.step, self.cols), 1)
        self.first_lane, self.last_lane = lanes == 0, lanes == self.cols - 1
        square = (self.rows, self.rows)
        self.eye = lax.broadcasted_iota(jnp.int32, square, 0) == lax.broadcasted_iota(
            jnp.int32, square, 1
        )
        self.zero = jnp.zeros((8, self.cols), jnp.float32)
        self.moments = [self.zero] * 6

    def start_loads(self):
        for i in (1, 6, 2, 3, 4, 5, 0):
            self.loads[i].start()

    def load_faces(self):
        for i in (1, 6, 2, 3):
            self.loads[i].wait()

    def load_rest(self):
        for i in (4, 5, 0):
            self.loads[i].wait()

    def column(self, block):
        wide = jnp.broadcast_to(block, (self.rows, self.rows))
        return jnp.sum(jnp.where(self.eye, wide, 0.0), axis=0, keepdims=True)

    def spread(self, row):
        return jnp.broadcast_to(row, (self.rows, self.rows)).T

    def uncolumn(self, wide, block):
        part = wide[block * self.step : (block + 1) * self.step]
        return jnp.concatenate([part] * (self.cols // self.rows), axis=1)

    def fold(self, x):
        parts = [x[i * 8 : (i + 1) * 8] for i in range(self.step // 8)]
        while len(parts) > 1:
            parts = [a + b for a, b in zip(parts[::2], parts[1::2])]
        return parts[0]

    def faces(self):
        layers, rows, cols, step = self.layers, self.rows, self.cols, self.step
        east_last = jnp.where(self.gx == self.count_x - 1, 0.0, 1.0).astype(jnp.float32)
        north_last = jnp.where(self.gy == self.count_y - 1, 0.0, 1.0).astype(jnp.float32)
        north_scale = jnp.where(self.last_lane, north_last, 1.0)
        row_ids = lax.broadcasted_iota(jnp.int32, (step, cols), 0)

        def body(layer, carry):
            for b in range(self.blocks):
                at = pl.ds(b * step, step)
                open_faces = (1 - self.closed[layer, at, :]).astype(jnp.float32)
                scale = jnp.where(row_ids == rows - 1 - b * step, east_last, 1.0)
                self.east[layer, pl.ds(PAD + b * step, step), :] = (
                    self.cond_x[layer, at, :] * open_faces * scale
                )
                self.north[layer, at, :] = self.cond_y[layer, at, :] * open_faces * north_scale
            self.above[layer + 1] = self.cond_z[layer] * jnp.where(layer == layers - 1, 0.0, 1.0)
            self.col_out[0, 0, pl.ds(layer, 1), :] = self.column(
                self.north[layer, :, cols - 1 : cols]
            )
            return carry

        self.above[0] = jnp.zeros((rows, cols), jnp.float32)
        lax.fori_loop(0, layers, body, 0)
        self.rims = [
            remote(self.east.at[:, pl.ds(PAD + rows - 1, 1), :],
                   self.east.at[:, pl.ds(PAD - 1, 1), :],
                   self.halo_send.at[0, 0], self.halo_recv.at[0, 0], self.right),
            remote(self.col_out.at[0, 0], self.col_in.at[0, 0],
                   self.halo_send.at[0, 1], self.halo_recv.at[0, 1], self.up),
        ]

    def send_rims(self):
        for copy in self.rims:
            copy.start()

    def prepare(self):
        step = self.step
        for copy in self.rims:
            copy.wait()

        def body(layer, carry):
            south_row = self.spread(self.col_in[0, 0, pl.ds(layer, 1), :])
            for b in range(self.blocks):
                at = pl.ds(b * step, step)
                north = self.north[layer, at, :]
                south = jnp.where(
                    self.first_lane, self.uncolumn(south_row, b), pltpu.roll(north, 1, 1)
                )
                self.south[layer, at, :] = south
                keep = (1 - self.fixed[layer, at, :]).astype(jnp.float32)
                diagonal = (
                    self.storage[layer, at, :]
                    + self.east[layer, pl.ds(PAD + b * step, step), :]
                    + self.east[layer, pl.ds(PAD - 1 + b * step, step), :]
                    + north + south + self.above[layer + 1, at, :] + self.above[layer, at, :]
                )
                self.inverse[layer, at, :] = keep / diagonal
            return carry

        lax.fori_loop(0, self.layers, body, 0)

    def start(self, low, high, surface=None):
        step = self.step

        def body(layer, total):
            for b in range(self.blocks):
                at = pl.ds(b * step, step)
                keep = (1 - self.fixed[layer, at, :]).astype(jnp.float32)
                value = self.forcing[layer, at, :]
                if surface is not None:
                    value = value + surface[at, :]
                value = keep * value
                self.enns[0, layer, at, :] = value
                tee = self.inverse[layer, at, :] * value
                self.tees[0, layer, pl.ds(PAD + b * step, step), :] = tee
                total = total + self.fold(tee * value)
            return total

        self.moments[0] = lax.fori_loop(low, high, body, self.moments[0])

    def send(self, j, low, high, early):
        rows, cols = self.rows, self.cols

        some = pl.ds(low, high - low)
        tee = self.tees.at[j, some]
        k = 2 * j + 1 + early
        copies = [
            remote(tee.at[:, pl.ds(PAD + rows - 1, 1), :], tee.at[:, pl.ds(PAD - 1, 1), :],
                   self.halo_send.at[k, 0], self.halo_recv.at[k, 0], self.right),
            remote(tee.at[:, pl.ds(PAD, 1), :], tee.at[:, pl.ds(PAD + rows, 1), :],
                   self.halo_send.at[k, 1], self.halo_recv.at[k, 1], self.left),
            remote(self.col_out.at[j + 1, 0, some], self.col_in.at[j + 1, 0, some],
                   self.halo_send.at[k, 2], self.halo_recv.at[k, 2], self.up),
            remote(self.col_out.at[j + 1, 1, some], self.col_in.at[j + 1, 1, some],
                   self.halo_send.at[k, 3], self.halo_recv.at[k, 3], self.down),
        ]
        for copy in copies[:2]:
            copy.start()

        def body(layer, carry):
            here = self.tees.at[j, layer, pl.ds(PAD, rows), :]
            self.col_out[j + 1, 0, pl.ds(layer, 1), :] = self.column(here[:, cols - 1 : cols])
            self.col_out[j + 1, 1, pl.ds(layer, 1), :] = self.column(here[:, 0:1])
            return carry

        lax.fori_loop(low, high, body, 0)
        for copy in copies[2:]:
            copy.start()
        return copies

    def apply(self, j, low, high):
        layers, cols, step, tees = self.layers, self.cols, self.step, self.tees

        def body(layer, carry):
            odd, even = carry
            south_row = self.spread(self.col_in[j + 1, 0, pl.ds(layer, 1), :])
            north_row = self.spread(self.col_in[j + 1, 1, pl.ds(layer, 1), :])
            higher = jnp.minimum(layer + 1, layers - 1)
            lower = jnp.maximum(layer - 1, 0)
            for b in range(self.blocks):
                at = pl.ds(b * step, step)
                mid = pl.ds(PAD + b * step, step)
                before = pl.ds(PAD - 1 + b * step, step)
                after = pl.ds(PAD + 1 + b * step, step)
                here = tees[j, layer, mid, :]
                north = jnp.where(
                    self.last_lane, self.uncolumn(north_row, b), pltpu.roll(here, cols - 1, 1)
                )
                south = jnp.where(
                    self.first_lane, self.uncolumn(south_row, b), pltpu.roll(here, 1, 1)
                )
                flux = self.east[layer, mid, :] * tees[j, layer, after, :]
                flux += self.east[layer, before, :] * tees[j, layer, before, :]
                flux += self.north[layer, at, :] * north + self.south[layer, at, :] * south
                flux += self.above[layer + 1, at, :] * tees[j, higher, mid, :]
                flux += self.above[layer, at, :] * tees[j, lower, mid, :]
                self.enns[j + 1, layer, at, :] = flux
                odd = odd + self.fold(here * flux)
                if j < 2:
                    tee = self.inverse[layer, at, :] * flux
                    tees[j + 1, layer, mid, :] = tee
                    even = even + self.fold(tee * flux)
            return odd, even

        last = self.moments[2 * j + 2] if j < 2 else self.zero
        odd, even = lax.fori_loop(low, high, body, (self.moments[2 * j + 1], last))
        self.moments[2 * j + 1] = odd
        if j < 2:
            self.moments[2 * j + 2] = even

    def total(self, extra):
        partial, gathered = self.partial, self.gathered
        partial[0] = jnp.zeros((8, 128), jnp.float32)
        for k, value in enumerate(self.moments):
            both = sum(value[:, i * 128 : (i + 1) * 128] for i in range(self.cols // 128))
            partial[0, k : k + 1, :] = jnp.sum(both, axis=0, keepdims=True)
        partial[0, 6:7, :] = extra
        base = 0
        for s, peers in enumerate(self.lay.stages()):
            copies = [
                remote(partial.at[s], gathered.at[base + i], self.sum_send.at[base + i],
                       self.sum_recv.at[base + i], self.lay.moved(**offset))
                for i, offset in enumerate(peers)
            ]
            for copy in copies:
                copy.start()
            for copy in copies:
                copy.wait()
            total = partial[s]
            for i in range(len(peers)):
                total = total + gathered[base + i]
            base += len(peers)
            partial[s + 1] = total
        return partial[len(self.lay.stages())]

    def finish(self, total, solution, residual, outs, sem):
        def leave(layer):
            return [
                pltpu.make_async_copy(source.at[layer], target.at[layer], sem.at[k, layer])
                for k, (source, target) in enumerate(zip((solution, residual), outs))
            ]

        sol_w, res_w = scalars(total)
        step = self.step

        def body(layer, carry):
            for b in range(self.blocks):
                at = pl.ds(b * step, step)
                mid = pl.ds(PAD + b * step, step)
                keep = (1 - self.fixed[layer, at, :]).astype(jnp.float32)
                out = sol_w[0] * self.tees[0, layer, mid, :]
                for j in range(1, 3):
                    out += sol_w[j] * self.tees[j, layer, mid, :]
                solution[layer, at, :] = out
                out = res_w[0] * self.enns[0, layer, at, :]
                for j in range(1, 4):
                    out += res_w[j] * self.enns[j, layer, at, :]
                residual[layer, at, :] = keep * out
            for copy in leave(layer):
                copy.start()
            return carry

        lax.fori_loop(0, self.layers, body, 0)
        for layer in range(self.layers):
            for copy in leave(layer):
                copy.wait()


def solve_scratch(lay, layers, rows, cols):
    peers = sum(len(s) for s in lay.stages())
    f32, dma = jnp.float32, pltpu.SemaphoreType.DMA

    def full(*lead, kind=f32):
        return pltpu.VMEM((*lead, layers, rows, cols), kind)

    def padded(*lead):
        return pltpu.VMEM((*lead, layers, rows + 2 * PAD, cols), f32)

    return [
        full(), full(), full(), full(), full(), full(kind=jnp.int32), full(kind=jnp.int32),
        padded(3), padded(), full(), full(),
        pltpu.VMEM((layers + 1, rows, cols), f32), full(), full(4),
        pltpu.VMEM((4, 2, layers, rows), f32), pltpu.VMEM((4, 2, layers, rows), f32),
        pltpu.VMEM((len(lay.stages()) + 1, 8, 128), f32), pltpu.VMEM((peers, 8, 128), f32),
        dma((7, 4)), dma((7, 4)), dma((peers,)), dma((peers,)),
    ]


def every_friend(lay, count_x):
    gx, gy = lax.axis_index("gx"), lax.axis_index("gy")
    friends = [((gx + 1) % count_x, gy), ((gx + count_x - 1) % count_x, gy), lay.moved(dc=1)]
    for axis in "xyz":
        friends += [
            lay.moved(**{"d" + axis: d, "dc": c}) for d in range(1, 4) for c in range(lay.cores)
        ]
    return friends + [lay.moved(dx=x, dz=z) for x in range(1, 4) for z in range(1, 4)]


def scalars(total):
    def reduce(row):
        return jnp.sum(row, axis=1, keepdims=True)

    rows = [total[k : k + 1, :] for k in range(6)]
    m0, m1 = reduce(rows[0]), reduce(rows[1])
    shift = jnp.where(m1 > 0.5 * m0, 1.0, 0.0)
    scale = 1.0 - shift
    c, current = [m0], rows
    for _ in range(5):
        current = [current[q + 1] - shift * current[q] for q in range(len(current) - 1)]
        c.append(reduce(current[0]))
    d = [scale * c[k] - c[k + 1] for k in range(5)]
    zero = jnp.zeros_like(m0)
    rho, pi, sol = [zero + 1.0], [zero + 1.0], [zero, zero, zero]
    inner = m0
    for i in range(3):
        curve = zero
        for a in range(len(pi)):
            for b in range(len(pi)):
                curve = curve + pi[a] * pi[b] * d[a + b]
        alpha = inner / curve
        for a in range(len(pi)):
            sol[a] = sol[a] + alpha * pi[a]
        rho = rho + [zero]
        for a in range(len(pi)):
            rho[a] = rho[a] - alpha * scale * pi[a]
            rho[a + 1] = rho[a + 1] + alpha * pi[a]
        if i < 2:
            inner_next = zero
            for a in range(len(rho)):
                for b in range(len(rho)):
                    inner_next = inner_next + rho[a] * rho[b] * c[a + b]
            beta = inner_next / inner
            pi = [rho[a] + beta * pi[a] if a < len(pi) else rho[a] for a in range(len(rho))]
            inner = inner_next

    def unshift(w):
        out = [zero] * len(w)
        for k in reversed(range(len(w))):
            moved = [zero] + out[:-1]
            out = [moved[i] - shift * out[i] for i in range(len(w))]
            out[0] = out[0] + w[k]
        return out

    return unshift(sol), unshift(rho)


ORDERS = (("x", "y", "z"), ("y", "z", "x"), ("z", "x", "y"))
DIMS = {"x": "zy", "y": "xz", "z": "xy"}


def portions(side):
    tiles = side // 8
    cut = [0, tiles // 3, tiles - tiles // 3, tiles]
    return [(8 * cut[i], 8 * (cut[i + 1] - cut[i])) for i in range(3)]


def exchange_body(
    lay, cap, solve, enter, load, owners, slots, surface, held, packed, arrived, summed, landed, second,
    third, index_v, weight_v, weight_in, index_s, weight_s, move_sem,
    send1, recv1, send1w, recv1w, send2, recv2, send3, recv3, *star,
):
    per_device, side, _ = held.shape
    me = dict(zip("xzcy", lay.me()))
    count = dict(x=lay.nx, y=lay.ny, z=lay.nz)
    parts = portions(side)

    shape = (per_device, 128)
    patch_ids = lax.broadcasted_iota(jnp.int32, shape, 0)
    row = (owners[...] * 2 + slots[...]).astype(jnp.float32)
    column = jnp.sum(
        jnp.where(solve.eye, jnp.broadcast_to(row, shape), 0.0), axis=1, keepdims=True
    )
    place = jnp.broadcast_to(column, shape) - (
        2 * lax.broadcasted_iota(jnp.int32, shape, 1)
    ).astype(jnp.float32)
    hit = jnp.logical_or(place == 0.0, place == 1.0)
    first = jnp.min(jnp.where(hit, patch_ids, per_device), axis=0, keepdims=True)
    last = jnp.max(jnp.where(hit, patch_ids, -1), axis=0, keepdims=True)
    index_v[0:1, :] = jnp.minimum(first, per_device - 1)
    index_v[1:2, :] = jnp.maximum(last, 0)
    again = last > first
    for j in range(2):
        chosen = patch_ids == (first if j == 0 else last)
        if j > 0:
            chosen = jnp.logical_and(chosen, again)
        chosen = jnp.logical_and(hit, chosen)
        for s in range(2):
            weight_v[2 * j + s : 2 * j + s + 1, :] = jnp.sum(
                jnp.where(jnp.logical_and(chosen, place == float(s)), 1.0, 0.0), axis=0, keepdims=True
            )
    doubled = jnp.where(again, 1.0, 0.0)
    for s in range(2):
        weight_v[4 + s : 5 + s, :] = jnp.broadcast_to(
            jnp.sum(weight_v[2 + s : 3 + s, :], axis=1, keepdims=True), (1, 128)
        )
    extra = jnp.maximum(jnp.sum(doubled, axis=1, keepdims=True) - 1.0, 0.0)
    weight_v[6:7, :] = jnp.broadcast_to(extra, (1, 128))
    weight_v[7:8, :] = doubled
    spare_index = jnp.max(jnp.where(again, last, 0), axis=1, keepdims=True)
    index_v[2:3, :] = jnp.broadcast_to(spare_index, (1, 128))
    to_scalar = pltpu.make_async_copy(index_v, index_s, move_sem.at[0])
    to_scalar.start()
    own_weight = pltpu.make_async_copy(weight_v, weight_s.at[0, 0], move_sem.at[1])
    own_weight.start()

    offsets = [(1, 0), (3, 1), (2, 0), (2, 1), (1, 1), (3, 0), (0, 1)]

    def moved(axis, d, c):
        return lay.moved(**{"d" + axis: d, "dc": c})

    weight_copies = [
        [
            remote(weight_v, weight_in.at[q, i], send1w.at[q, i], recv1w.at[q, i],
                   moved(order[0], d, c))
            for i, (d, c) in enumerate(offsets)
        ]
        for q, order in enumerate(ORDERS)
    ]
    for copy in load:
        copy.wait()
    solve.start_loads()
    to_scalar.wait()
    own_weight.wait()

    def pack(o, carry):
        for j in range(cap):
            packed[o // 32, o // 8 % 4, o // 4 % 2, o % 4, j] = held[index_s[j, o]]
        return carry

    lax.fori_loop(0, 128, pack, 0)
    common = Common(lay, me, held, weight_v, weight_in, *star) if cap == 1 else None
    if common:
        common.pack(index_s[2, 0])
    enter()
    for group in weight_copies:
        for copy in group:
            copy.start()
    if common:
        common.scatter()

    def first_stage(half):
        some = pl.ds(2 * half, 2)
        copies = [[], [], []]
        for i, (d, c) in enumerate(offsets):
            for q, order in enumerate(ORDERS):
                axis = order[0]
                at = pl.ds(*parts[q])
                a, core = (me[axis] + d) % 4, (me["c"] + c) % lay.cores
                if axis == "x":
                    source = packed.at[a, some, core, :, :, at, :]
                elif axis == "y":
                    source = packed.at[some, :, core, a, :, at, :]
                else:
                    source = packed.at[:, a, core, some, :, at, :]
                target = arrived[q].at[i, :, some] if axis == "z" else arrived[q].at[i, some]
                copy = remote(source, target, send1.at[half, q, i], recv1.at[half, q, i],
                              moved(axis, d, c))
                copy.start()
                copies[q].append(copy)
        return copies

    def second_stage(half, q, copies):
        order = ORDERS[q]
        for copy in copies[q]:
            copy.wait()
        at = pl.ds(*parts[q])
        rows = parts[q][1]
        dims = DIMS[order[0]]

        def reduce(k, carry):
            b, c = k // 2, 2 * half + k % 2
            spot = {order[0]: me[order[0]], order[1]: b, order[2]: c}
            owner = spot["x"] * 32 + spot["z"] * 8 + me["c"] * 4 + spot["y"]
            sums = [jnp.zeros((rows, side), jnp.float32) for _ in range(2)]
            for source in range(8):
                for j in range(cap):
                    if source == 0:
                        value = packed[spot["x"], spot["z"], me["c"], spot["y"], j, at, :]
                    else:
                        value = arrived[q][source - 1, spot[dims[0]], spot[dims[1]], j]
                    value = value.astype(jnp.float32)
                    table = (0, 0) if source == 0 else (q, source)
                    for s in range(2):
                        sums[s] = sums[s] + weight_s[(*table, 2 * j + s, owner)] * value
            for s in range(2):
                summed[q][b, c, s] = sums[s]
            return carry

        lax.fori_loop(0, 8, reduce, 0)
        some = pl.ds(2 * half, 2)
        mine = []
        for d in (1, 3, 2):
            copy = remote(summed[q].at[(me[order[1]] + d) % 4, some], landed[q].at[d - 1, some],
                          send2.at[half, q, d - 1], recv2.at[half, q, d - 1],
                          moved(order[1], d, 0))
            copy.start()
            mine.append(copy)
        return mine

    copies1 = [first_stage(0)]
    solve.load_faces()
    solve.faces()
    solve.send_rims()
    copies1.append(first_stage(1))
    gathers = []
    for q in range(3):
        for copy in weight_copies[q]:
            copy.wait()
        gathers.append(pltpu.make_async_copy(
            weight_in.at[q], weight_s.at[q, pl.ds(1, 7)], move_sem.at[2 + q]
        ))
        gathers[q].start()
    for gather in gathers:
        gather.wait()
    copies2 = [[second_stage(0, q, copies1[0]) for q in range(3)]]
    solve.load_rest()
    solve.prepare()
    solve.start(1, solve.layers)
    early = solve.send(0, 1, solve.layers, True)
    if common:
        common.reduce()
    copies2.append([second_stage(1, q, copies1[1]) for q in range(3)])
    for copy in early:
        copy.wait()
    solve.apply(0, 2, solve.layers)
    early = solve.send(1, 2, solve.layers, True)
    if common:
        common.gather()
    copies3 = []
    for q, order in enumerate(ORDERS):
        for half in range(2):
            for copy in copies2[half][q]:
                copy.wait()

        def reduce(k, carry, q=q, order=order):
            total = summed[q][me[order[1]], k]
            for d in range(3):
                total = total + landed[q][d, k]
            second[q][k] = total
            return carry

        lax.fori_loop(0, 4, reduce, 0)
        mine = []
        for d in (1, 3, 2):
            copy = remote(second[q].at[(me[order[2]] + d) % 4], third[q].at[d - 1],
                          send3.at[q, d - 1], recv3.at[q, d - 1], moved(order[2], d, 0))
            copy.start()
            mine.append(copy)
        copies3.append(mine)
    for copy in early:
        copy.wait()
    solve.apply(1, 3, solve.layers)
    early = solve.send(2, 3, solve.layers, True)
    if common:
        common.place(surface)
    for q, order in enumerate(ORDERS):
        for copy in copies3[q]:
            copy.wait()
        for s in range(2):
            total = second[q][me[order[2]], s]
            for d in range(3):
                total = total + third[q][d, s]
            spot = (pl.ds(*parts[q]), slice(s * side, (s + 1) * side))
            surface[spot] = surface[spot] + total if common else total
    return early


class Common:
    def __init__(self, lay, me, held, weight_v, weight_in, spare, pieces, sums, others, whole,
                 send_a, recv_a, send_b, recv_b, send_c, recv_c):
        self.__dict__.update(locals())
        self.offsets = [(1, 0), (3, 1), (2, 0), (2, 1), (1, 1), (3, 0), (0, 1)]
        self.wide = lay.stages()[1]

    def piece(self, d, c):
        return (self.me["y"] + d) % 4 * 2 + (self.me["c"] + c) % 2

    def pack(self, index):
        for k in range(8):
            self.spare[k] = self.held[index, 16 * k : 16 * (k + 1), :]

    def scatter(self):
        self.copies = [
            remote(self.spare.at[self.piece(d, c)], self.pieces.at[i], self.send_a.at[i],
                   self.recv_a.at[i], self.lay.moved(dy=d, dc=c))
            for i, (d, c) in enumerate(self.offsets)
        ]
        for copy in self.copies:
            copy.start()

    def reduce(self):
        for copy in self.copies:
            copy.wait()
        for s in range(2):
            mine = self.spare[self.piece(0, 0)].astype(jnp.float32)
            total = self.weight_v[4 + s : 5 + s, :] * mine
            for i in range(7):
                weight = self.weight_in[1, i, 4 + s : 5 + s, :]
                total = total + weight * self.pieces[i].astype(jnp.float32)
            self.sums[0, s] = total
        self.copies = [
            remote(self.sums.at[0], self.others.at[i], self.send_b.at[i], self.recv_b.at[i],
                   self.lay.moved(**offset))
            for i, offset in enumerate(self.wide)
        ]
        for copy in self.copies:
            copy.start()

    def gather(self):
        for copy in self.copies:
            copy.wait()
        for s in range(2):
            total = self.sums[0, s]
            for i in range(len(self.wide)):
                total = total + self.others[i, s]
            self.sums[1, s] = total
        k = self.piece(0, 0)
        self.whole[k] = self.sums[1]
        self.copies = [
            remote(self.sums.at[1], self.whole.at[k], self.send_c.at[i], self.recv_c.at[i],
                   self.lay.moved(dy=d, dc=c))
            for i, (d, c) in enumerate(self.offsets)
        ]
        for copy in self.copies:
            copy.start()

    def place(self, surface):
        for copy in self.copies:
            copy.wait()
        me = self.me
        owner = me["x"] * 32 + me["z"] * 8 + me["c"] * 4 + me["y"]
        here = lax.broadcasted_iota(jnp.int32, (1, 128), 1) == owner
        mine = jnp.sum(jnp.where(here, self.weight_v[7:8, :], 0.0), axis=1, keepdims=True)
        for k in range(8):
            for s in range(2):
                at = (slice(16 * k, 16 * (k + 1)), slice(128 * s, 128 * (s + 1)))
                surface[at] = mine * self.whole[k, s]


def exchange_scratch(cap, side):
    parts = portions(side)

    def each(*lead, kind=jnp.float32):
        return [pltpu.VMEM((*lead, rows, side), kind) for _, rows in parts]

    bf16 = jnp.bfloat16
    dma = pltpu.SemaphoreType.DMA
    return [
        pltpu.VMEM((128, side, side), bf16),
        pltpu.VMEM((4, 4, 2, 4, cap, side, side), bf16),
        each(7, 4, 4, cap, kind=bf16), each(4, 4, 2), each(3, 4, 2), each(4, 2), each(3, 2),
        pltpu.VMEM((8, 128), jnp.int32), pltpu.VMEM((8, 128), jnp.float32),
        pltpu.VMEM((3, 7, 8, 128), jnp.float32),
        pltpu.SMEM((8, 128), jnp.int32), pltpu.SMEM((3, 8, 8, 128), jnp.float32),
        dma((5,)),
        dma((2, 3, 7)), dma((2, 3, 7)), dma((3, 7)), dma((3, 7)),
        dma((2, 3, 3)), dma((2, 3, 3)), dma((3, 3)), dma((3, 3)),
    ] + ([
        pltpu.VMEM((8, 16, side), bf16), pltpu.VMEM((7, 16, side), bf16),
        pltpu.VMEM((2, 2, 16, side), jnp.float32), pltpu.VMEM((15, 2, 16, side), jnp.float32),
        pltpu.VMEM((8, 2, 16, side), jnp.float32),
        dma((7,)), dma((7,)), dma((15,)), dma((15,)), dma((7,)), dma((7,)),
    ] if cap == 1 else [])


def kernel(lay, count_x, count_y, cap, sizes, *refs):
    owners, slots, patches, *inputs = refs[:10]
    *outs, sums = refs[10:13]
    solve_refs = refs[13 : 13 + sizes[0]]
    exchange_refs = refs[13 + sizes[0] : 13 + sizes[0] + sizes[1]]
    surface, load_sem, solution, residual, leave_sem = refs[13 + sizes[0] + sizes[1] :]
    solve = Solve(lay, count_x, count_y, solve_refs)
    held = exchange_refs[0]
    some = held.shape[0] // 4
    load = [
        pltpu.make_async_copy(
            patches.at[pl.ds(i * some, some)], held.at[pl.ds(i * some, some)], load_sem.at[7 + i]
        )
        for i in range(4)
    ]
    for copy in load:
        copy.start()
    loads = [
        pltpu.make_async_copy(source, target, load_sem.at[i])
        for i, (source, target) in enumerate(zip(inputs, solve_refs[:7]))
    ]
    solve.loads = loads
    friends = every_friend(lay, count_x)
    barrier = pltpu.get_barrier_semaphore()
    for friend in friends:
        pl.semaphore_signal(barrier, inc=1, device_id=friend, device_id_type=MESH)
    early = exchange_body(
        lay, cap, solve, lambda: pl.semaphore_wait(barrier, len(friends)), load, owners, slots, surface,
        *exchange_refs,
    )
    solve.start(0, 1, surface)
    late = solve.send(0, 0, 1, False)
    for copy in early:
        copy.wait()
    solve.apply(2, 4, solve.layers)
    for j in range(3):
        solve.apply(j, j + 1, j + 2)
        for copy in late:
            copy.wait()
        solve.apply(j, 0, j + 1)
        if j < 2:
            late = solve.send(j + 1, 0, j + 2, False)
    weight_v = exchange_refs[8]
    total = solve.total(weight_v[6:7, :])
    sums[...] = jnp.where(total[6:7, 0:1] > 0.0, 1, 0)
    solve.finish(total, solution, residual, outs, leave_sem)


def move_kernel(a, b, c, d, held, sem):
    layers = a.shape[0]
    into = [pltpu.make_async_copy(x.at[i], held.at[k, i], sem.at[0, k, i])
            for i in range(layers) for k, x in enumerate((a, b))]
    away = [pltpu.make_async_copy(held.at[k, i], x.at[i], sem.at[1, k, i])
            for i in range(layers) for k, x in enumerate((c, d))]
    for copy in into:
        copy.start()
    for first, then in zip(into, away):
        first.wait()
        then.start()
    for copy in away:
        copy.wait()


def move(*arrays):
    shape = arrays[0].shape
    return tuple(pl.pallas_call(
        move_kernel,
        out_shape=[jax.ShapeDtypeStruct(x.shape, x.dtype) for x in arrays],
        in_specs=[pl.BlockSpec(memory_space=pl.ANY)] * 2,
        out_specs=[pl.BlockSpec(memory_space=pl.ANY)] * 2,
        scratch_shapes=[
            pltpu.VMEM((2, *shape), jnp.float32), pltpu.SemaphoreType.DMA((2, 2, shape[0]))
        ],
    )(*arrays))


def run(lay, count_x, count_y, cap, owners, slots, patches, *grids):
    layers, rows, cols = grids[0].shape
    solve = solve_scratch(lay, layers, rows, cols)
    moving = exchange_scratch(cap, patches.shape[1])
    return pl.pallas_call(
        functools.partial(kernel, lay, count_x, count_y, cap, (len(solve), len(moving))),
        out_shape=[jax.ShapeDtypeStruct((layers, rows, cols), jnp.float32)] * 2
        + [jax.ShapeDtypeStruct((1, 1), jnp.int32)],
        in_specs=[pl.BlockSpec(memory_space=pltpu.VMEM)] * 2
        + [pl.BlockSpec(memory_space=pl.ANY)] * (1 + len(grids)),
        out_specs=[pl.BlockSpec(memory_space=pl.ANY)] * 2
        + [pl.BlockSpec(memory_space=pltpu.VMEM)],
        scratch_shapes=solve + moving + [
            pltpu.VMEM((rows, cols), jnp.float32), pltpu.SemaphoreType.DMA((11,)),
            pltpu.VMEM((layers, rows, cols), jnp.float32),
            pltpu.VMEM((layers, rows, cols), jnp.float32),
            pltpu.SemaphoreType.DMA((2, layers)),
        ],
        compiler_params=pltpu.CompilerParams(
            collective_id=cap, has_side_effects=True,
            vmem_limit_bytes=(42 if cap == 1 else 60) * MIB,
        ),
    )(owners, slots, patches, *grids)


def on_device(forcing, patches, owners, slots, cond_x, cond_y, cond_z, storage, fixed, closed):
    count_x, count_y = lax.axis_size("gx"), lax.axis_size("gy")
    lay = Layout(count_x, count_y)
    args = (owners.T, slots.T, patches, forcing, cond_x, cond_y, cond_z, storage, fixed, closed)
    *quick, sums = run(lay, count_x, count_y, 1, *args)

    def general(args, quick):
        return tuple(run(lay, count_x, count_y, 2, *args)[:2])

    return move(*lax.cond(sums[0, 0] > 0, general, lambda args, quick: quick, args, tuple(quick)))


def solution(mesh):
    grid = P(None, "gx", "gy")
    return jax.shard_map(
        on_device,
        mesh=mesh,
        in_specs=(grid, P("gx", "gy", None), P("gx", "gy"), P("gx", "gy")) + (grid,) * 6,
        out_specs=(grid, grid),
        check_vma=False,
    )
```

```python
import functools

import jax
import jax.numpy as jnp
from jax import lax
from jax.experimental import pallas as pl
from jax.experimental.pallas import tpu as pltpu
from jax.sharding import PartitionSpec as P

MESH = pl.DeviceIdType.MESH
PAD = 8
MIB = 1 << 20


class Layout:
    def __init__(self, count_x, count_y):
        self.cores = 2 if count_x % 2 == 0 else 1
        chips = count_x // self.cores
        self.nz = 4 if chips % 4 == 0 else chips
        self.nx = chips // self.nz
        self.ny = count_y

    def me(self):
        gx, gy = lax.axis_index("gx"), lax.axis_index("gy")
        core = gx % self.cores
        chip = gx // self.cores
        return chip // self.nz, chip % self.nz, core, gy

    def device(self, x, z, core, y):
        return ((x * self.nz + z) * self.cores + core, y)

    def moved(self, dx=0, dz=0, dc=0, dy=0):
        x, z, core, y = self.me()
        return self.device(
            (x + dx) % self.nx, (z + dz) % self.nz, (core + dc) % self.cores, (y + dy) % self.ny
        )

    def stages(self):
        first = [
            dict(dc=c, dy=y) for c in range(self.cores) for y in range(self.ny) if (c, y) != (0, 0)
        ]
        second = [
            dict(dx=x, dz=z) for x in range(self.nx) for z in range(self.nz) if (x, z) != (0, 0)
        ]
        return [first, second]


def remote(src, dst, send, recv, device):
    return pltpu.make_async_remote_copy(
        src_ref=src, dst_ref=dst, send_sem=send, recv_sem=recv, device_id=device, device_id_type=MESH
    )


class Solve:
    names = (
        "forcing", "cond_x", "cond_y", "cond_z", "storage", "fixed", "closed", "tees", "east",
        "north", "south", "above", "inverse", "enns", "col_out", "col_in", "partial", "gathered",
        "halo_send", "halo_recv", "sum_send", "sum_recv",
    )

    def __init__(self, lay, count_x, count_y, refs):
        self.lay, self.count_x, self.count_y = lay, count_x, count_y
        for name, ref in zip(self.names, refs, strict=True):
            setattr(self, name, ref)
        self.layers, self.rows, self.cols = self.forcing.shape
        self.step = 32
        self.blocks = self.rows // self.step
        gx, gy = lax.axis_index("gx"), lax.axis_index("gy")
        self.gx, self.gy = gx, gy
        self.right = ((gx + 1) % count_x, gy)
        self.left = ((gx + count_x - 1) % count_x, gy)
        self.up = (gx, (gy + 1) % count_y)
        self.down = (gx, (gy + count_y - 1) % count_y)
        lanes = lax.broadcasted_iota(jnp.int32, (self.step, self.cols), 1)
        self.first_lane, self.last_lane = lanes == 0, lanes == self.cols - 1
        square = (self.rows, self.rows)
        self.eye = lax.broadcasted_iota(jnp.int32, square, 0) == lax.broadcasted_iota(
            jnp.int32, square, 1
        )
        self.zero = jnp.zeros((8, self.cols), jnp.float32)
        self.moments = [self.zero] * 6

    def start_loads(self):
        for i in (1, 6, 2, 3, 4, 5, 0):
            self.loads[i].start()

    def load_faces(self):
        for i in (1, 6, 2, 3):
            self.loads[i].wait()

    def load_rest(self):
        for i in (4, 5, 0):
            self.loads[i].wait()

    def column(self, block):
        wide = jnp.broadcast_to(block, (self.rows, self.rows))
        return jnp.sum(jnp.where(self.eye, wide, 0.0), axis=0, keepdims=True)

    def spread(self, row):
        return jnp.broadcast_to(row, (self.rows, self.rows)).T

    def uncolumn(self, wide, block):
        part = wide[block * self.step : (block + 1) * self.step]
        return jnp.concatenate([part] * (self.cols // self.rows), axis=1)

    def fold(self, x):
        parts = [x[i * 8 : (i + 1) * 8] for i in range(self.step // 8)]
        while len(parts) > 1:
            parts = [a + b for a, b in zip(parts[::2], parts[1::2])]
        return parts[0]

    def faces(self):
        layers, rows, cols, step = self.layers, self.rows, self.cols, self.step
        east_last = jnp.where(self.gx == self.count_x - 1, 0.0, 1.0).astype(jnp.float32)
        north_last = jnp.where(self.gy == self.count_y - 1, 0.0, 1.0).astype(jnp.float32)
        north_scale = jnp.where(self.last_lane, north_last, 1.0)
        row_ids = lax.broadcasted_iota(jnp.int32, (step, cols), 0)

        def body(layer, carry):
            for b in range(self.blocks):
                at = pl.ds(b * step, step)
                open_faces = (1 - self.closed[layer, at, :]).astype(jnp.float32)
                scale = jnp.where(row_ids == rows - 1 - b * step, east_last, 1.0)
                self.east[layer, pl.ds(PAD + b * step, step), :] = (
                    self.cond_x[layer, at, :] * open_faces * scale
                )
                self.north[layer, at, :] = self.cond_y[layer, at, :] * open_faces * north_scale
            self.above[layer + 1] = self.cond_z[layer] * jnp.where(layer == layers - 1, 0.0, 1.0)
            self.col_out[0, 0, pl.ds(layer, 1), :] = self.column(
                self.north[layer, :, cols - 1 : cols]
            )
            return carry

        self.above[0] = jnp.zeros((rows, cols), jnp.float32)
        lax.fori_loop(0, layers, body, 0)
        self.rims = [
            remote(self.east.at[:, pl.ds(PAD + rows - 1, 1), :],
                   self.east.at[:, pl.ds(PAD - 1, 1), :],
                   self.halo_send.at[0, 0], self.halo_recv.at[0, 0], self.right),
            remote(self.col_out.at[0, 0], self.col_in.at[0, 0],
                   self.halo_send.at[0, 1], self.halo_recv.at[0, 1], self.up),
        ]

    def send_rims(self):
        for copy in self.rims:
            copy.start()

    def prepare(self):
        step = self.step
        for copy in self.rims:
            copy.wait()

        def body(layer, carry):
            south_row = self.spread(self.col_in[0, 0, pl.ds(layer, 1), :])
            for b in range(self.blocks):
                at = pl.ds(b * step, step)
                north = self.north[layer, at, :]
                south = jnp.where(
                    self.first_lane, self.uncolumn(south_row, b), pltpu.roll(north, 1, 1)
                )
                self.south[layer, at, :] = south
                keep = (1 - self.fixed[layer, at, :]).astype(jnp.float32)
                diagonal = (
                    self.storage[layer, at, :]
                    + self.east[layer, pl.ds(PAD + b * step, step), :]
                    + self.east[layer, pl.ds(PAD - 1 + b * step, step), :]
                    + north + south + self.above[layer + 1, at, :] + self.above[layer, at, :]
                )
                self.inverse[layer, at, :] = keep / diagonal
            return carry

        lax.fori_loop(0, self.layers, body, 0)

    def start(self, low, high, surface=None):
        step = self.step

        def body(layer, total):
            for b in range(self.blocks):
                at = pl.ds(b * step, step)
                keep = (1 - self.fixed[layer, at, :]).astype(jnp.float32)
                value = self.forcing[layer, at, :]
                if surface is not None:
                    value = value + surface[at, :]
                value = keep * value
                self.enns[0, layer, at, :] = value
                tee = self.inverse[layer, at, :] * value
                self.tees[0, layer, pl.ds(PAD + b * step, step), :] = tee
                total = total + self.fold(tee * value)
            return total

        self.moments[0] = lax.fori_loop(low, high, body, self.moments[0])

    def send(self, j, low, high, early):
        rows, cols = self.rows, self.cols

        some = pl.ds(low, high - low)
        tee = self.tees.at[j, some]
        k = 2 * j + 1 + early
        copies = [
            remote(tee.at[:, pl.ds(PAD + rows - 1, 1), :], tee.at[:, pl.ds(PAD - 1, 1), :],
                   self.halo_send.at[k, 0], self.halo_recv.at[k, 0], self.right),
            remote(tee.at[:, pl.ds(PAD, 1), :], tee.at[:, pl.ds(PAD + rows, 1), :],
                   self.halo_send.at[k, 1], self.halo_recv.at[k, 1], self.left),
            remote(self.col_out.at[j + 1, 0, some], self.col_in.at[j + 1, 0, some],
                   self.halo_send.at[k, 2], self.halo_recv.at[k, 2], self.up),
            remote(self.col_out.at[j + 1, 1, some], self.col_in.at[j + 1, 1, some],
                   self.halo_send.at[k, 3], self.halo_recv.at[k, 3], self.down),
        ]
        for copy in copies[:2]:
            copy.start()

        def body(layer, carry):
            here = self.tees.at[j, layer, pl.ds(PAD, rows), :]
            self.col_out[j + 1, 0, pl.ds(layer, 1), :] = self.column(here[:, cols - 1 : cols])
            self.col_out[j + 1, 1, pl.ds(layer, 1), :] = self.column(here[:, 0:1])
            return carry

        lax.fori_loop(low, high, body, 0)
        for copy in copies[2:]:
            copy.start()
        return copies

    def apply(self, j, low, high):
        layers, cols, step, tees = self.layers, self.cols, self.step, self.tees

        def body(layer, carry):
            odd, even = carry
            south_row = self.spread(self.col_in[j + 1, 0, pl.ds(layer, 1), :])
            north_row = self.spread(self.col_in[j + 1, 1, pl.ds(layer, 1), :])
            higher = jnp.minimum(layer + 1, layers - 1)
            lower = jnp.maximum(layer - 1, 0)
            for b in range(self.blocks):
                at = pl.ds(b * step, step)
                mid = pl.ds(PAD + b * step, step)
                before = pl.ds(PAD - 1 + b * step, step)
                after = pl.ds(PAD + 1 + b * step, step)
                here = tees[j, layer, mid, :]
                north = jnp.where(
                    self.last_lane, self.uncolumn(north_row, b), pltpu.roll(here, cols - 1, 1)
                )
                south = jnp.where(
                    self.first_lane, self.uncolumn(south_row, b), pltpu.roll(here, 1, 1)
                )
                flux = self.east[layer, mid, :] * tees[j, layer, after, :]
                flux += self.east[layer, before, :] * tees[j, layer, before, :]
                flux += self.north[layer, at, :] * north + self.south[layer, at, :] * south
                flux += self.above[layer + 1, at, :] * tees[j, higher, mid, :]
                flux += self.above[layer, at, :] * tees[j, lower, mid, :]
                self.enns[j + 1, layer, at, :] = flux
                odd = odd + self.fold(here * flux)
                if j < 2:
                    tee = self.inverse[layer, at, :] * flux
                    tees[j + 1, layer, mid, :] = tee
                    even = even + self.fold(tee * flux)
            return odd, even

        last = self.moments[2 * j + 2] if j < 2 else self.zero
        odd, even = lax.fori_loop(low, high, body, (self.moments[2 * j + 1], last))
        self.moments[2 * j + 1] = odd
        if j < 2:
            self.moments[2 * j + 2] = even

    def total(self, extra):
        partial, gathered = self.partial, self.gathered
        partial[0] = jnp.zeros((8, 128), jnp.float32)
        for k, value in enumerate(self.moments):
            both = sum(value[:, i * 128 : (i + 1) * 128] for i in range(self.cols // 128))
            partial[0, k : k + 1, :] = jnp.sum(both, axis=0, keepdims=True)
        partial[0, 6:7, :] = extra
        base = 0
        for s, peers in enumerate(reversed(self.lay.stages())):
            copies = [
                remote(partial.at[s], gathered.at[base + i], self.sum_send.at[base + i],
                       self.sum_recv.at[base + i], self.lay.moved(**offset))
                for i, offset in enumerate(peers)
            ]
            for copy in copies:
                copy.start()
            for copy in copies:
                copy.wait()
            total = partial[s]
            for i in range(len(peers)):
                total = total + gathered[base + i]
            base += len(peers)
            partial[s + 1] = total
        return partial[len(self.lay.stages())]

    def finish(self, total, solution, residual, outs, sem):
        def leave(layer):
            return [
                pltpu.make_async_copy(source.at[layer], target.at[layer], sem.at[k, layer])
                for k, (source, target) in enumerate(zip((solution, residual), outs))
            ]

        sol_w, res_w = scalars(total)
        step = self.step

        def body(layer, carry):
            for b in range(self.blocks):
                at = pl.ds(b * step, step)
                mid = pl.ds(PAD + b * step, step)
                keep = (1 - self.fixed[layer, at, :]).astype(jnp.float32)
                out = sol_w[0] * self.tees[0, layer, mid, :]
                for j in range(1, 3):
                    out += sol_w[j] * self.tees[j, layer, mid, :]
                solution[layer, at, :] = out
                out = res_w[0] * self.enns[0, layer, at, :]
                for j in range(1, 4):
                    out += res_w[j] * self.enns[j, layer, at, :]
                residual[layer, at, :] = keep * out
            for copy in leave(layer):
                copy.start()
            return carry

        lax.fori_loop(0, self.layers, body, 0)
        for layer in range(self.layers):
            for copy in leave(layer):
                copy.wait()


def solve_scratch(lay, layers, rows, cols):
    peers = sum(len(s) for s in lay.stages())
    f32, dma = jnp.float32, pltpu.SemaphoreType.DMA

    def full(*lead, kind=f32):
        return pltpu.VMEM((*lead, layers, rows, cols), kind)

    def padded(*lead):
        return pltpu.VMEM((*lead, layers, rows + 2 * PAD, cols), f32)

    return [
        full(), full(), full(), full(), full(), full(kind=jnp.int32), full(kind=jnp.int32),
        padded(3), padded(), full(), full(),
        pltpu.VMEM((layers + 1, rows, cols), f32), full(), full(4),
        pltpu.VMEM((4, 2, layers, rows), f32), pltpu.VMEM((4, 2, layers, rows), f32),
        pltpu.VMEM((len(lay.stages()) + 1, 8, 128), f32), pltpu.VMEM((peers, 8, 128), f32),
        dma((7, 4)), dma((7, 4)), dma((peers,)), dma((peers,)),
    ]


def every_friend(lay, count_x):
    gx, gy = lax.axis_index("gx"), lax.axis_index("gy")
    friends = [((gx + 1) % count_x, gy), ((gx + count_x - 1) % count_x, gy), lay.moved(dc=1)]
    for axis in "xyz":
        friends += [
            lay.moved(**{"d" + axis: d, "dc": c}) for d in range(1, 4) for c in range(lay.cores)
        ]
    return friends + [lay.moved(dx=x, dz=z) for x in range(1, 4) for z in range(1, 4)]


def scalars(total):
    def reduce(row):
        return jnp.sum(row, axis=1, keepdims=True)

    rows = [total[k : k + 1, :] for k in range(6)]
    m0, m1 = reduce(rows[0]), reduce(rows[1])
    shift = jnp.where(m1 > 0.5 * m0, 1.0, 0.0)
    scale = 1.0 - shift
    c, current = [m0], rows
    for _ in range(5):
        current = [current[q + 1] - shift * current[q] for q in range(len(current) - 1)]
        c.append(reduce(current[0]))
    d = [scale * c[k] - c[k + 1] for k in range(5)]
    zero = jnp.zeros_like(m0)
    rho, pi, sol = [zero + 1.0], [zero + 1.0], [zero, zero, zero]
    inner = m0
    for i in range(3):
        curve = zero
        for a in range(len(pi)):
            for b in range(len(pi)):
                curve = curve + pi[a] * pi[b] * d[a + b]
        alpha = inner / curve
        for a in range(len(pi)):
            sol[a] = sol[a] + alpha * pi[a]
        rho = rho + [zero]
        for a in range(len(pi)):
            rho[a] = rho[a] - alpha * scale * pi[a]
            rho[a + 1] = rho[a + 1] + alpha * pi[a]
        if i < 2:
            inner_next = zero
            for a in range(len(rho)):
                for b in range(len(rho)):
                    inner_next = inner_next + rho[a] * rho[b] * c[a + b]
            beta = inner_next / inner
            pi = [rho[a] + beta * pi[a] if a < len(pi) else rho[a] for a in range(len(rho))]
            inner = inner_next

    def unshift(w):
        out = [zero] * len(w)
        for k in reversed(range(len(w))):
            moved = [zero] + out[:-1]
            out = [moved[i] - shift * out[i] for i in range(len(w))]
            out[0] = out[0] + w[k]
        return out

    return unshift(sol), unshift(rho)


ORDERS = (("x", "y", "z"), ("y", "z", "x"), ("z", "x", "y"))
DIMS = {"x": "zy", "y": "xz", "z": "xy"}


def portions(side):
    tiles = side // 8
    cut = [0, tiles // 3, tiles - tiles // 3, tiles]
    return [(8 * cut[i], 8 * (cut[i + 1] - cut[i])) for i in range(3)]


def exchange_body(
    lay, cap, solve, enter, load, owners, slots, surface, held, packed, arrived, summed, landed, second,
    third, index_v, weight_v, weight_in, index_s, weight_s, move_sem,
    send1, recv1, send1w, recv1w, send2, recv2, send3, recv3, *star,
):
    per_device, side, _ = held.shape
    me = dict(zip("xzcy", lay.me()))
    count = dict(x=lay.nx, y=lay.ny, z=lay.nz)
    parts = portions(side)

    shape = (per_device, 128)
    patch_ids = lax.broadcasted_iota(jnp.int32, shape, 0)
    row = (owners[...] * 2 + slots[...]).astype(jnp.float32)
    column = jnp.sum(
        jnp.where(solve.eye, jnp.broadcast_to(row, shape), 0.0), axis=1, keepdims=True
    )
    place = jnp.broadcast_to(column, shape) - (
        2 * lax.broadcasted_iota(jnp.int32, shape, 1)
    ).astype(jnp.float32)
    hit = jnp.logical_or(place == 0.0, place == 1.0)
    first = jnp.min(jnp.where(hit, patch_ids, per_device), axis=0, keepdims=True)
    last = jnp.max(jnp.where(hit, patch_ids, -1), axis=0, keepdims=True)
    index_v[0:1, :] = jnp.minimum(first, per_device - 1)
    index_v[1:2, :] = jnp.maximum(last, 0)
    again = last > first
    for j in range(2):
        chosen = patch_ids == (first if j == 0 else last)
        if j > 0:
            chosen = jnp.logical_and(chosen, again)
        chosen = jnp.logical_and(hit, chosen)
        for s in range(2):
            weight_v[2 * j + s : 2 * j + s + 1, :] = jnp.sum(
                jnp.where(jnp.logical_and(chosen, place == float(s)), 1.0, 0.0), axis=0, keepdims=True
            )
    doubled = jnp.where(again, 1.0, 0.0)
    for s in range(2):
        weight_v[4 + s : 5 + s, :] = jnp.broadcast_to(
            jnp.sum(weight_v[2 + s : 3 + s, :], axis=1, keepdims=True), (1, 128)
        )
    extra = jnp.maximum(jnp.sum(doubled, axis=1, keepdims=True) - 1.0, 0.0)
    weight_v[6:7, :] = jnp.broadcast_to(extra, (1, 128))
    weight_v[7:8, :] = doubled
    spare_index = jnp.max(jnp.where(again, last, 0), axis=1, keepdims=True)
    index_v[2:3, :] = jnp.broadcast_to(spare_index, (1, 128))
    to_scalar = pltpu.make_async_copy(index_v, index_s, move_sem.at[0])
    to_scalar.start()
    own_weight = pltpu.make_async_copy(weight_v, weight_s.at[0, 0], move_sem.at[1])
    own_weight.start()

    offsets = [(1, 0), (3, 1), (2, 0), (2, 1), (1, 1), (3, 0), (0, 1)]

    def moved(axis, d, c):
        return lay.moved(**{"d" + axis: d, "dc": c})

    weight_copies = [
        [
            remote(weight_v, weight_in.at[q, i], send1w.at[q, i], recv1w.at[q, i],
                   moved(order[0], d, c))
            for i, (d, c) in enumerate(offsets)
        ]
        for q, order in enumerate(ORDERS)
    ]
    for copy in load:
        copy.wait()
    solve.start_loads()
    to_scalar.wait()
    own_weight.wait()

    def pack(o, carry):
        for j in range(cap):
            packed[o // 32, o // 8 % 4, o // 4 % 2, o % 4, j] = held[index_s[j, o]]
        return carry

    lax.fori_loop(0, 128, pack, 0)
    common = Common(lay, me, held, weight_v, weight_in, *star) if cap == 1 else None
    if common:
        common.pack(index_s[2, 0])
    enter()
    for group in weight_copies:
        for copy in group:
            copy.start()
    if common:
        common.scatter()

    def first_stage(half):
        some = pl.ds(2 * half, 2)
        copies = [[], [], []]
        for i, (d, c) in enumerate(offsets):
            for q, order in enumerate(ORDERS):
                axis = order[0]
                at = pl.ds(*parts[q])
                a, core = (me[axis] + d) % 4, (me["c"] + c) % lay.cores
                if axis == "x":
                    source = packed.at[a, some, core, :, :, at, :]
                elif axis == "y":
                    source = packed.at[some, :, core, a, :, at, :]
                else:
                    source = packed.at[:, a, core, some, :, at, :]
                target = arrived[q].at[i, :, some] if axis == "z" else arrived[q].at[i, some]
                copy = remote(source, target, send1.at[half, q, i], recv1.at[half, q, i],
                              moved(axis, d, c))
                copy.start()
                copies[q].append(copy)
        return copies

    def second_stage(half, q, copies):
        order = ORDERS[q]
        for copy in copies[q]:
            copy.wait()
        at = pl.ds(*parts[q])
        rows = parts[q][1]
        dims = DIMS[order[0]]

        def reduce(k, carry):
            b, c = k // 2, 2 * half + k % 2
            spot = {order[0]: me[order[0]], order[1]: b, order[2]: c}
            owner = spot["x"] * 32 + spot["z"] * 8 + me["c"] * 4 + spot["y"]
            sums = [jnp.zeros((rows, side), jnp.float32) for _ in range(2)]
            for source in range(8):
                for j in range(cap):
                    if source == 0:
                        value = packed[spot["x"], spot["z"], me["c"], spot["y"], j, at, :]
                    else:
                        value = arrived[q][source - 1, spot[dims[0]], spot[dims[1]], j]
                    value = value.astype(jnp.float32)
                    table = (0, 0) if source == 0 else (q, source)
                    for s in range(2):
                        sums[s] = sums[s] + weight_s[(*table, 2 * j + s, owner)] * value
            for s in range(2):
                summed[q][b, c, s] = sums[s]
            return carry

        lax.fori_loop(0, 8, reduce, 0)
        some = pl.ds(2 * half, 2)
        mine = []
        for d in (1, 3, 2):
            copy = remote(summed[q].at[(me[order[1]] + d) % 4, some], landed[q].at[d - 1, some],
                          send2.at[half, q, d - 1], recv2.at[half, q, d - 1],
                          moved(order[1], d, 0))
            copy.start()
            mine.append(copy)
        return mine

    copies1 = [first_stage(0)]
    solve.load_faces()
    solve.faces()
    solve.send_rims()
    copies1.append(first_stage(1))
    gathers = []
    for q in range(3):
        for copy in weight_copies[q]:
            copy.wait()
        gathers.append(pltpu.make_async_copy(
            weight_in.at[q], weight_s.at[q, pl.ds(1, 7)], move_sem.at[2 + q]
        ))
        gathers[q].start()
    for gather in gathers:
        gather.wait()
    copies2 = [[second_stage(0, q, copies1[0]) for q in range(3)]]
    solve.load_rest()
    solve.prepare()
    solve.start(1, solve.layers)
    early = solve.send(0, 1, solve.layers, True)
    if common:
        common.reduce()
    copies2.append([second_stage(1, q, copies1[1]) for q in range(3)])
    for copy in early:
        copy.wait()
    solve.apply(0, 2, solve.layers)
    early = solve.send(1, 2, solve.layers, True)
    if common:
        common.gather()
    copies3 = []
    for q, order in enumerate(ORDERS):
        for half in range(2):
            for copy in copies2[half][q]:
                copy.wait()

        def reduce(k, carry, q=q, order=order):
            total = summed[q][me[order[1]], k]
            for d in range(3):
                total = total + landed[q][d, k]
            second[q][k] = total
            return carry

        lax.fori_loop(0, 4, reduce, 0)
        mine = []
        for d in (1, 3, 2):
            copy = remote(second[q].at[(me[order[2]] + d) % 4], third[q].at[d - 1],
                          send3.at[q, d - 1], recv3.at[q, d - 1], moved(order[2], d, 0))
            copy.start()
            mine.append(copy)
        copies3.append(mine)
    for copy in early:
        copy.wait()
    solve.apply(1, 3, solve.layers)
    early = solve.send(2, 3, solve.layers, True)
    if common:
        common.place(surface)
    for q, order in enumerate(ORDERS):
        for copy in copies3[q]:
            copy.wait()
        for s in range(2):
            total = second[q][me[order[2]], s]
            for d in range(3):
                total = total + third[q][d, s]
            spot = (pl.ds(*parts[q]), slice(s * side, (s + 1) * side))
            surface[spot] = surface[spot] + total if common else total
    return early


class Common:
    def __init__(self, lay, me, held, weight_v, weight_in, spare, pieces, sums, others, whole,
                 send_a, recv_a, send_b, recv_b, send_c, recv_c):
        self.__dict__.update(locals())
        self.offsets = [(1, 0), (3, 1), (2, 0), (2, 1), (1, 1), (3, 0), (0, 1)]
        self.wide = lay.stages()[1]

    def piece(self, d, c):
        return (self.me["y"] + d) % 4 * 2 + (self.me["c"] + c) % 2

    def pack(self, index):
        for k in range(8):
            self.spare[k] = self.held[index, 16 * k : 16 * (k + 1), :]

    def scatter(self):
        self.copies = [
            remote(self.spare.at[self.piece(d, c)], self.pieces.at[i], self.send_a.at[i],
                   self.recv_a.at[i], self.lay.moved(dy=d, dc=c))
            for i, (d, c) in enumerate(self.offsets)
        ]
        for copy in self.copies:
            copy.start()

    def reduce(self):
        for copy in self.copies:
            copy.wait()
        for s in range(2):
            mine = self.spare[self.piece(0, 0)].astype(jnp.float32)
            total = self.weight_v[4 + s : 5 + s, :] * mine
            for i in range(7):
                weight = self.weight_in[1, i, 4 + s : 5 + s, :]
                total = total + weight * self.pieces[i].astype(jnp.float32)
            self.sums[0, s] = total
        self.copies = [
            remote(self.sums.at[0], self.others.at[i], self.send_b.at[i], self.recv_b.at[i],
                   self.lay.moved(**offset))
            for i, offset in enumerate(self.wide)
        ]
        for copy in self.copies:
            copy.start()

    def gather(self):
        for copy in self.copies:
            copy.wait()
        for s in range(2):
            total = self.sums[0, s]
            for i in range(len(self.wide)):
                total = total + self.others[i, s]
            self.sums[1, s] = total
        k = self.piece(0, 0)
        self.whole[k] = self.sums[1]
        self.copies = [
            remote(self.sums.at[1], self.whole.at[k], self.send_c.at[i], self.recv_c.at[i],
                   self.lay.moved(dy=d, dc=c))
            for i, (d, c) in enumerate(self.offsets)
        ]
        for copy in self.copies:
            copy.start()

    def place(self, surface):
        for copy in self.copies:
            copy.wait()
        me = self.me
        owner = me["x"] * 32 + me["z"] * 8 + me["c"] * 4 + me["y"]
        here = lax.broadcasted_iota(jnp.int32, (1, 128), 1) == owner
        mine = jnp.sum(jnp.where(here, self.weight_v[7:8, :], 0.0), axis=1, keepdims=True)
        for k in range(8):
            for s in range(2):
                at = (slice(16 * k, 16 * (k + 1)), slice(128 * s, 128 * (s + 1)))
                surface[at] = mine * self.whole[k, s]


def exchange_scratch(cap, side):
    parts = portions(side)

    def each(*lead, kind=jnp.float32):
        return [pltpu.VMEM((*lead, rows, side), kind) for _, rows in parts]

    bf16 = jnp.bfloat16
    dma = pltpu.SemaphoreType.DMA
    return [
        pltpu.VMEM((128, side, side), bf16),
        pltpu.VMEM((4, 4, 2, 4, cap, side, side), bf16),
        each(7, 4, 4, cap, kind=bf16), each(4, 4, 2), each(3, 4, 2), each(4, 2), each(3, 2),
        pltpu.VMEM((8, 128), jnp.int32), pltpu.VMEM((8, 128), jnp.float32),
        pltpu.VMEM((3, 7, 8, 128), jnp.float32),
        pltpu.SMEM((8, 128), jnp.int32), pltpu.SMEM((3, 8, 8, 128), jnp.float32),
        dma((5,)),
        dma((2, 3, 7)), dma((2, 3, 7)), dma((3, 7)), dma((3, 7)),
        dma((2, 3, 3)), dma((2, 3, 3)), dma((3, 3)), dma((3, 3)),
    ] + ([
        pltpu.VMEM((8, 16, side), bf16), pltpu.VMEM((7, 16, side), bf16),
        pltpu.VMEM((2, 2, 16, side), jnp.float32), pltpu.VMEM((15, 2, 16, side), jnp.float32),
        pltpu.VMEM((8, 2, 16, side), jnp.float32),
        dma((7,)), dma((7,)), dma((15,)), dma((15,)), dma((7,)), dma((7,)),
    ] if cap == 1 else [])


def kernel(lay, count_x, count_y, cap, sizes, *refs):
    owners, slots, patches, *inputs = refs[:10]
    *outs, sums = refs[10:13]
    solve_refs = refs[13 : 13 + sizes[0]]
    exchange_refs = refs[13 + sizes[0] : 13 + sizes[0] + sizes[1]]
    surface, load_sem, solution, residual, leave_sem = refs[13 + sizes[0] + sizes[1] :]
    solve = Solve(lay, count_x, count_y, solve_refs)
    held = exchange_refs[0]
    some = held.shape[0] // 4
    load = [
        pltpu.make_async_copy(
            patches.at[pl.ds(i * some, some)], held.at[pl.ds(i * some, some)], load_sem.at[7 + i]
        )
        for i in range(4)
    ]
    for copy in load:
        copy.start()
    loads = [
        pltpu.make_async_copy(source, target, load_sem.at[i])
        for i, (source, target) in enumerate(zip(inputs, solve_refs[:7]))
    ]
    solve.loads = loads
    friends = every_friend(lay, count_x)
    barrier = pltpu.get_barrier_semaphore()
    for friend in friends:
        pl.semaphore_signal(barrier, inc=1, device_id=friend, device_id_type=MESH)
    early = exchange_body(
        lay, cap, solve, lambda: pl.semaphore_wait(barrier, len(friends)), load, owners, slots, surface,
        *exchange_refs,
    )
    solve.start(0, 1, surface)
    late = solve.send(0, 0, 1, False)
    for copy in early:
        copy.wait()
    solve.apply(2, 4, solve.layers)
    for j in range(3):
        solve.apply(j, j + 1, j + 2)
        for copy in late:
            copy.wait()
        solve.apply(j, 0, j + 1)
        if j < 2:
            late = solve.send(j + 1, 0, j + 2, False)
    weight_v = exchange_refs[8]
    total = solve.total(weight_v[6:7, :])
    sums[...] = jnp.where(total[6:7, 0:1] > 0.0, 1, 0)
    solve.finish(total, solution, residual, outs, leave_sem)


def move_kernel(a, b, c, d, held, sem):
    layers = a.shape[0]
    into = [pltpu.make_async_copy(x.at[i], held.at[k, i], sem.at[0, k, i])
            for i in range(layers) for k, x in enumerate((a, b))]
    away = [pltpu.make_async_copy(held.at[k, i], x.at[i], sem.at[1, k, i])
            for i in range(layers) for k, x in enumerate((c, d))]
    for copy in into:
        copy.start()
    for first, then in zip(into, away):
        first.wait()
        then.start()
    for copy in away:
        copy.wait()


def move(*arrays):
    shape = arrays[0].shape
    return tuple(pl.pallas_call(
        move_kernel,
        out_shape=[jax.ShapeDtypeStruct(x.shape, x.dtype) for x in arrays],
        in_specs=[pl.BlockSpec(memory_space=pl.ANY)] * 2,
        out_specs=[pl.BlockSpec(memory_space=pl.ANY)] * 2,
        scratch_shapes=[
            pltpu.VMEM((2, *shape), jnp.float32), pltpu.SemaphoreType.DMA((2, 2, shape[0]))
        ],
    )(*arrays))


def run(lay, count_x, count_y, cap, owners, slots, patches, *grids):
    layers, rows, cols = grids[0].shape
    solve = solve_scratch(lay, layers, rows, cols)
    moving = exchange_scratch(cap, patches.shape[1])
    return pl.pallas_call(
        functools.partial(kernel, lay, count_x, count_y, cap, (len(solve), len(moving))),
        out_shape=[jax.ShapeDtypeStruct((layers, rows, cols), jnp.float32)] * 2
        + [jax.ShapeDtypeStruct((1, 1), jnp.int32)],
        in_specs=[pl.BlockSpec(memory_space=pltpu.VMEM)] * 2
        + [pl.BlockSpec(memory_space=pl.ANY)] * (1 + len(grids)),
        out_specs=[pl.BlockSpec(memory_space=pl.ANY)] * 2
        + [pl.BlockSpec(memory_space=pltpu.VMEM)],
        scratch_shapes=solve + moving + [
            pltpu.VMEM((rows, cols), jnp.float32), pltpu.SemaphoreType.DMA((11,)),
            pltpu.VMEM((layers, rows, cols), jnp.float32),
            pltpu.VMEM((layers, rows, cols), jnp.float32),
            pltpu.SemaphoreType.DMA((2, layers)),
        ],
        compiler_params=pltpu.CompilerParams(
            collective_id=cap, has_side_effects=True,
            vmem_limit_bytes=(42 if cap == 1 else 60) * MIB,
        ),
    )(owners, slots, patches, *grids)


def on_device(forcing, patches, owners, slots, cond_x, cond_y, cond_z, storage, fixed, closed):
    count_x, count_y = lax.axis_size("gx"), lax.axis_size("gy")
    lay = Layout(count_x, count_y)
    args = (owners.T, slots.T, patches, forcing, cond_x, cond_y, cond_z, storage, fixed, closed)
    *quick, sums = run(lay, count_x, count_y, 1, *args)

    def general(args, quick):
        return tuple(run(lay, count_x, count_y, 2, *args)[:2])

    return move(*lax.cond(sums[0, 0] > 0, general, lambda args, quick: quick, args, tuple(quick)))


def solution(mesh):
    grid = P(None, "gx", "gy")
    return jax.shard_map(
        on_device,
        mesh=mesh,
        in_specs=(grid, P("gx", "gy", None), P("gx", "gy"), P("gx", "gy")) + (grid,) * 6,
        out_specs=(grid, grid),
        check_vma=False,
    )
```
